128 devices in a mesh: tile: 8 (over x, y_lo), chan: 16 (over y_hi, z, core).
Axes of the slice: x: 4, y: 4 (y_hi: 2, y_lo: 2; y = y_hi * 2 + y_lo), z: 4, core: 2. Of those that a mesh axis runs over, the one named last changes fastest.
Arguments:
- visibilities: float32 [8, 16, 2, 2048], P('tile', 'chan'), may hold values from -6 to 6
- cell_offsets: int32 [8, 16, 2, 2048], P('tile', 'chan'), may hold values from 0 to 1023
- support_index: int32 [8, 16, 2048], P('tile', 'chan'), may hold values from 0 to 3
- w_plane: int32 [8, 16, 2048], P('tile', 'chan'), may hold values from 0 to 15
- live_counts: int32 [8, 16], P('tile', 'chan'), may hold values from 256 to 2048, as said below
Outputs:
- grid: float32 [8192, 2, 1024], P(('tile', 'chan'))
The draws below stay inside these ranges and needn't reach their ends.
Inputs may be any that keep to these rules, and one draw needn't show every extreme that they name: Slots 0 to live_counts - 1 of a tile and group hold visibilities, the others are empty; some tile and group is full.
All inputs are finite; a program needn't handle non-finite values.
Results may differ from the reference program's by a relative error of at most 0.0037.
Values sent between devices are 32-bit elements; how exact they have to be, the bound alone decides.
A program may use at most 64 MiB of HBM per device.

```python
import math
import jax
import jax.numpy as jnp
from jax import lax

G = 1024
M = 32
PLANES = 16
VIS_DEV = 2048
TILES = 8
GROUPS = 16


def draw_live_counts(key, part):
    base_counts = jax.random.randint(key, (TILES, GROUPS), VIS_DEV // 8, VIS_DEV + 1, dtype=jnp.int32)
    chosen = jax.random.randint(jax.random.fold_in(key, 7), (), 0, TILES * GROUPS, dtype=jnp.int32)
    position = jnp.arange(TILES * GROUPS, dtype=jnp.int32).reshape(TILES, GROUPS)
    return jnp.where(position == chosen, jnp.int32(VIS_DEV), base_counts)


def set_ends(drawn, stream_key, low, high):
    place = [jax.random.randint(jax.random.fold_in(stream_key, axis), (), 0, length) for axis, length in enumerate(drawn.shape)]
    main_axis = drawn.shape.index(max(drawn.shape))
    beside = place[:main_axis] + [(place[main_axis] + 1) % drawn.shape[main_axis]] + place[main_axis + 1:]
    return drawn.at[tuple(place)].set(low).at[tuple(beside)].set(high)


def shard_levels(key, extent, pieces, low, largest):
    gain, own = 1.0, jax.random.fold_in(key, 6)
    for dim, shards_of in pieces:
        steps = jnp.exp(jax.random.uniform(jax.random.fold_in(own, dim), (shards_of,), jnp.float32, low / len(pieces), largest / len(pieces)))
        gain = gain * jnp.repeat(steps, extent[dim] // shards_of).reshape([-1 if axis == dim else 1 for axis in range(len(extent))])
    return gain


def gaussian(own_key, shape, scale, bound, shards=(), held_as=jnp.bfloat16):
    level = shard_levels(own_key, shape, shards, -0.22, 0.18) if shards else 1.0
    result = jax.random.normal(own_key, shape, jnp.float32) * scale * level
    return jnp.minimum(jnp.maximum(result, -bound), bound).astype(held_as)


def setup_inputs(seed: int = 0) -> dict:
    splits = jax.random.split(jax.random.key(seed), 6)
    return {
        "visibilities": gaussian(splits[0], (TILES, GROUPS, 2, VIS_DEV), 1.0, 6.0, ((0, 8), (1, 16)), jnp.float32),
        "cell_offsets": set_ends(jax.random.randint(splits[1], (TILES, GROUPS, 2, VIS_DEV), 0, G), jax.random.fold_in(splits[1], 1), 0, G - 1).astype(jnp.int32),
        "support_index": set_ends(jax.random.randint(splits[2], (TILES, GROUPS, VIS_DEV), 0, 4), jax.random.fold_in(splits[2], 1), 0, 3).astype(jnp.int32),
        "w_plane": set_ends(jax.random.randint(splits[3], (TILES, GROUPS, VIS_DEV), 0, PLANES), jax.random.fold_in(splits[3], 1), 0, PLANES - 1).astype(jnp.int32),
        "live_counts": draw_live_counts(jax.random.fold_in(splits[5], 71), 0),
    }


BETA = 7.0

def bessel_zero(value):
    quarter = value * value * 0.25
    term = jnp.ones_like(value)
    total = jnp.ones_like(value)
    for index in range(1, 30):
        term = term * quarter / float(index * index)
        total = total + term
    return total

def kernel_values(distance, half_width, w_coef):
    ratio = distance / half_width
    inside = jnp.abs(ratio) < 1.0
    radius = jnp.sqrt(jnp.maximum(1.0 - ratio * ratio, 0.0))
    bessel = bessel_zero(BETA * radius) / bessel_zero(jnp.float32(BETA))
    taper = jnp.cos(jnp.pi * w_coef * ratio * ratio)
    return jnp.where(inside, bessel * taper, jnp.float32(0.0))

def flatten_groups(vis_block, offset_block, support_block, plane_block, count_block):
    slot_total = vis_block.shape[-1]
    slot_ids = jnp.arange(slot_total, dtype=jnp.int32)
    live = (slot_ids[None, :] < count_block[:, None]).astype(jnp.float32).reshape(-1)
    real_part = vis_block[:, 0].reshape(-1) * live
    imag_part = vis_block[:, 1].reshape(-1) * live
    row_cell = offset_block[:, 0].reshape(-1).astype(jnp.float32)
    col_cell = offset_block[:, 1].reshape(-1).astype(jnp.float32)
    half_width = 8.0 * (support_block.reshape(-1) + 1).astype(jnp.float32)
    w_coef = 0.5 * (plane_block.reshape(-1) + 1).astype(jnp.float32) / PLANES
    return (real_part, imag_part, row_cell, col_cell, half_width, w_coef)

def grid_part(flat, row_start, row_count, width):
    total_vis = flat[0].shape[0]
    block_len = math.gcd(total_vis, 512)
    stacked = tuple((item.reshape(total_vis // block_len, block_len) for item in flat))
    row_pos = (row_start + jnp.arange(row_count, dtype=jnp.int32)).astype(jnp.float32)
    col_pos = jnp.arange(width, dtype=jnp.int32).astype(jnp.float32)

    def step_block(total, values):
        real_part, imag_part, row_cell, col_cell, half_width, w_coef = values
        row_weights = kernel_values(row_pos[None, :] - row_cell[:, None], half_width[:, None], w_coef[:, None]).astype(jnp.bfloat16)
        col_kern = kernel_values(col_pos[None, :] - col_cell[:, None], half_width[:, None], w_coef[:, None])
        col_weights = jnp.concatenate([real_part[:, None] * col_kern, imag_part[:, None] * col_kern], axis=1).astype(jnp.bfloat16)
        product = lax.dot_general(row_weights, col_weights, (((0,), (0,)), ((), ())), preferred_element_type=jnp.float32)
        return (total + product, None)
    start_total = jnp.zeros((row_count, 2 * width), jnp.float32)
    total, _ = lax.scan(step_block, start_total, stacked)
    return total.reshape(row_count, 2, width)

def reference(visibilities, cell_offsets, support_index, w_plane, live_counts):

    def one_tile(items):
        flat = flatten_groups(items[0], items[1], items[2], items[3], items[4])
        return grid_part(flat, -M, G + 2 * M, G)
    padded = lax.map(one_tile, (visibilities, cell_offsets, support_index, w_plane, live_counts))
    core = padded[:, M:M + G]
    zero_strip = jnp.zeros((1, M, 2, G), jnp.float32)
    left_in = jnp.concatenate([zero_strip, padded[:-1, G + M:]], axis=0)
    right_in = jnp.concatenate([padded[1:, :M], zero_strip], axis=0)
    core = core.at[:, :M].add(left_in)
    core = core.at[:, G - M:].add(right_in)
    return core.reshape(TILES * G, 2, G)
```

```python
import functools
import math

import jax
import jax.numpy as jnp
from jax import lax
from jax.experimental import pallas as pl
from jax.experimental.pallas import tpu as pltpu
from jax.sharding import PartitionSpec as P

G = 1024
M = 32
PLANES = 16
BETA = 7.0

BUCKET = 32
CAP = 128
LOW = 32
GROUPS_IN = CAP // LOW
FIELDS = 8
MESH = pl.DeviceIdType.MESH
F32 = jnp.float32
BF16 = jnp.bfloat16


def from_behind(x, axis, by):
    count = lax.axis_size(axis)
    pairs = [(i, i + by) for i in range(count) if 0 <= i + by < count]
    return lax.ppermute(x, axis, pairs)


def bessel_zero(value):
    quarter = value * value * 0.25
    term = jnp.ones_like(value)
    total = jnp.ones_like(value)
    for index in range(1, 30):
        term = term * quarter * (1.0 / float(index * index))
        total = total + term
    return total


def kernel_values(distance, half_width, w_coef):
    ratio = distance / half_width
    inside = jnp.abs(ratio) < 1.0
    radius = jnp.sqrt(jnp.maximum(1.0 - ratio * ratio, 0.0))
    bessel = bessel_zero(BETA * radius) / bessel_zero(jnp.float32(BETA))
    taper = jnp.cos(jnp.pi * w_coef * ratio * ratio)
    return jnp.where(inside, bessel * taper, jnp.float32(0.0))


def flatten_groups(vis_block, offset_block, support_block, plane_block, count_block):
    slot_total = vis_block.shape[-1]
    slot_ids = jnp.arange(slot_total, dtype=jnp.int32)
    live = (slot_ids[None, :] < count_block[:, None]).astype(jnp.float32).reshape(-1)
    real_part = vis_block[:, 0].reshape(-1) * live
    imag_part = vis_block[:, 1].reshape(-1) * live
    row_cell = offset_block[:, 0].reshape(-1).astype(jnp.float32)
    col_cell = offset_block[:, 1].reshape(-1).astype(jnp.float32)
    half_width = 8.0 * (support_block.reshape(-1) + 1).astype(jnp.float32)
    w_coef = 0.5 * (plane_block.reshape(-1) + 1).astype(jnp.float32) / PLANES
    return (real_part, imag_part, row_cell, col_cell, half_width, w_coef)


def grid_part(flat, row_start, row_count, width):
    total_vis = flat[0].shape[0]
    block_len = math.gcd(total_vis, 512)
    stacked = tuple((item.reshape(total_vis // block_len, block_len) for item in flat))
    row_pos = (row_start + jnp.arange(row_count, dtype=jnp.int32)).astype(jnp.float32)
    col_pos = jnp.arange(width, dtype=jnp.int32).astype(jnp.float32)

    def step_block(total, values):
        real_part, imag_part, row_cell, col_cell, half_width, w_coef = values
        row_weights = kernel_values(
            row_pos[None, :] - row_cell[:, None], half_width[:, None], w_coef[:, None]
        ).astype(jnp.bfloat16)
        col_kern = kernel_values(
            col_pos[None, :] - col_cell[:, None], half_width[:, None], w_coef[:, None]
        )
        col_weights = jnp.concatenate(
            [real_part[:, None] * col_kern, imag_part[:, None] * col_kern], axis=1
        ).astype(jnp.bfloat16)
        product = lax.dot_general(
            row_weights, col_weights, (((0,), (0,)), ((), ())), preferred_element_type=jnp.float32
        )
        return (total + product, None)

    start_total = jnp.zeros((row_count, 2 * width), jnp.float32)
    total, _ = lax.scan(step_block, start_total, stacked)
    return total.reshape(row_count, 2, width)


def any_cells(visibilities, cell_offsets, support_index, w_plane, live_counts):
    own_flat = flatten_groups(
        visibilities[0], cell_offsets[0], support_index[0], w_plane[0], live_counts[0]
    )
    share = G // lax.axis_size("chan")
    first_row = lax.axis_index("chan") * share
    owned = lax.psum_scatter(
        grid_part(own_flat, jnp.int32(0), share * lax.axis_size("chan"), G),
        "chan",
        scatter_dimension=0,
        tiled=True,
    )
    low_edge = grid_part(own_flat, -M, M, G)
    high_edge = grid_part(own_flat, G, M, G)
    high_sum, low_sum = lax.psum((high_edge, low_edge), "chan")
    left_in = from_behind(high_sum, "tile", 1)
    right_in = from_behind(low_sum, "tile", -1)
    zero_rows = jnp.zeros((share, 2, G), jnp.float32)
    upper = jnp.concatenate([left_in, zero_rows], axis=0)
    upper_part = lax.dynamic_slice_in_dim(upper, jnp.minimum(first_row, M), share, 0)
    lower = jnp.concatenate([zero_rows, right_in], axis=0)
    lower_start = jnp.clip(first_row - (G - M - share), 0, M)
    lower_part = lax.dynamic_slice_in_dim(lower, lower_start, share, 0)
    return owned + upper_part + lower_part


def class_table():
    klass = lax.broadcasted_iota(jnp.int32, (128, 128), 0)
    distance = lax.broadcasted_iota(jnp.int32, (128, 128), 1).astype(F32)
    half = (8 * (klass // PLANES + 1)).astype(F32)
    w_coef = 0.5 * (klass % PLANES + 1).astype(F32) / PLANES
    ratio = distance / half
    inside = (ratio < 1.0) & (klass < 4 * PLANES)
    bound = jnp.minimum(ratio, 1.0)
    square = bound * bound
    radius = jnp.sqrt(jnp.maximum(1.0 - square, 0.0))
    bessel = bessel_zero(BETA * radius) / bessel_zero(jnp.full((128, 128), BETA, F32))
    taper = jnp.cos(jnp.pi * w_coef * square)
    return jnp.where(inside, bessel * taper, 0.0)


def exchange(vis, cell, sup, wpl, cnt, got, edge, table, flag, vis_v, cell_v, sup_v, wpl_v, packed, tile_flags, chan_flags,
             load_sem, send_sem, recv_sem, edge_send, edge_recv, tf_send, tf_recv, cf_send, cf_recv):
    t, c = lax.axis_index("tile"), lax.axis_index("chan")
    nt, nc = lax.axis_size("tile"), lax.axis_size("chan")
    slots = vis_v.shape[-1]
    loads = [
        pltpu.make_async_copy(vis.at[0, 0], vis_v, load_sem.at[0]),
        pltpu.make_async_copy(cell.at[0, 0], cell_v, load_sem.at[1]),
        pltpu.make_async_copy(sup.at[0], sup_v, load_sem.at[2]),
        pltpu.make_async_copy(wpl.at[0], wpl_v, load_sem.at[3]),
    ]
    for load in loads:
        load.start()
    edge[...] = jnp.zeros_like(edge)

    bar = pltpu.get_barrier_semaphore()
    for i in range(1, nc):
        pl.semaphore_signal(bar, inc=1, device_id=(t, lax.rem(c + i, nc)), device_id_type=MESH)
    for i in range(1, nt):
        pl.semaphore_signal(bar, inc=1, device_id=(lax.rem(t + i, nt), c), device_id_type=MESH)
    from_low = (c == 0) & (t > 0)
    from_high = (c == nc - 1) & (t < nt - 1)

    @pl.when(from_low)
    def _():
        for g in range(nc):
            pl.semaphore_signal(bar, inc=1, device_id=(t - 1, g), device_id_type=MESH)

    @pl.when(from_high)
    def _():
        for g in range(nc):
            pl.semaphore_signal(bar, inc=1, device_id=(t + 1, g), device_id_type=MESH)

    for load in loads:
        load.wait()

    live = lax.broadcasted_iota(jnp.int32, (1, slots), 1) < cnt[0, 0]
    row = cell_v[0:1]
    bucket = jnp.where(live, row // BUCKET, -1)
    buckets = G // BUCKET
    hot = (lax.broadcasted_iota(jnp.int32, (buckets, slots), 0) == bucket).astype(F32)
    step = 256
    before = (
        lax.broadcasted_iota(jnp.int32, (step, step), 0) < lax.broadcasted_iota(jnp.int32, (step, step), 1)
    ).astype(F32).astype(BF16)
    parts = []
    carry = jnp.zeros((buckets, 1), F32)
    for s in range(0, slots, step):
        piece = hot[:, s : s + step]
        ahead = jnp.dot(piece.astype(BF16), before, preferred_element_type=F32) + carry
        parts.append(jnp.sum(piece * ahead, axis=0, keepdims=True))
        carry = carry + jnp.sum(piece, axis=1, keepdims=True)
    rank = jnp.concatenate(parts, axis=1).astype(jnp.int32)
    over = (jnp.max(carry, axis=0, keepdims=True) > CAP).astype(F32)
    tile_flags[t] = jnp.broadcast_to(over, (8, 128))

    group = jnp.where(live, (bucket + 1) * GROUPS_IN + rank // LOW, -1)
    place = rank % LOW
    groups = packed.shape[0]
    to_group = (lax.broadcasted_iota(jnp.int32, (groups, slots), 0) == group).astype(F32).astype(BF16)
    at_place = lax.broadcasted_iota(jnp.int32, (LOW, slots), 0) == place

    def halves(x):
        high = x.astype(BF16).astype(F32)
        return high, x - high

    re_hi, re_lo = halves(vis_v[0:1])
    im_hi, im_lo = halves(vis_v[1:2])
    col_hi, col_lo = halves(cell_v[1:2].astype(F32))
    pieces = [re_hi, im_hi, col_hi, (row % BUCKET).astype(F32), sup_v[...].astype(F32), wpl_v[...].astype(F32),
              jnp.ones((1, slots), F32), jnp.zeros((1, slots), F32), re_lo, im_lo, col_lo, jnp.zeros((1, slots), F32)]
    spread = jnp.concatenate([jnp.where(at_place, x, 0.0).astype(BF16) for x in pieces], axis=0)
    moved = lax.dot_general(to_group, spread, (((1,), (1,)), ((), ())), preferred_element_type=F32)
    packed[:, 0:128] = moved[:, 0:128] + moved[:, 256:384]
    packed[:, 128:256] = moved[:, 128:256]

    below, above = (t > 0).astype(jnp.int32), (t < nt - 1).astype(jnp.int32)
    pl.semaphore_wait(bar, nc - 1 + nt - 1 + below + above)

    def tile_flag(i, slot):
        return pltpu.make_async_remote_copy(
            src_ref=tile_flags.at[t], dst_ref=tile_flags.at[slot], send_sem=tf_send.at[i], recv_sem=tf_recv.at[slot],
            device_id=(lax.rem(t + i, nt), c), device_id_type=MESH)

    for i in range(1, nt):
        tile_flag(i, t).start()

    width = 4 * GROUPS_IN

    def payload(i, slot):
        peer = lax.rem(c + i, nc)
        return pltpu.make_async_remote_copy(
            src_ref=packed.at[pl.ds(pl.multiple_of(8 * peer, 8), width)], dst_ref=got.at[slot], send_sem=send_sem.at[i],
            recv_sem=recv_sem.at[slot], device_id=(t, peer), device_id_type=MESH)

    order = [8, 7, 9, 6, 10, 5, 11, 4, 12, 3, 13, 2, 14, 1, 15]
    for i in order:
        payload(i, c).start()

    def edge_up():
        return pltpu.make_async_remote_copy(
            src_ref=packed.at[pl.ds(buckets * GROUPS_IN, GROUPS_IN)], dst_ref=edge.at[c, 0:GROUPS_IN], send_sem=edge_send.at[0],
            recv_sem=edge_recv.at[c], device_id=(t + 1, 0), device_id_type=MESH)

    def edge_down():
        return pltpu.make_async_remote_copy(
            src_ref=packed.at[pl.ds(GROUPS_IN, GROUPS_IN)], dst_ref=edge.at[c, 0:GROUPS_IN], send_sem=edge_send.at[1],
            recv_sem=edge_recv.at[c], device_id=(t - 1, nc - 1), device_id_type=MESH)

    @pl.when(t < nt - 1)
    def _():
        edge_up().start()

    @pl.when(t > 0)
    def _():
        edge_down().start()

    got[c] = packed[pl.ds(pl.multiple_of(8 * c, 8), width), :]

    for i in range(1, nt):
        tile_flag(i, lax.rem(t + i, nt)).wait_recv()
    chan_flags[c] = jnp.max(tile_flags[...], axis=0)

    def chan_flag(i, slot):
        return pltpu.make_async_remote_copy(
            src_ref=chan_flags.at[c], dst_ref=chan_flags.at[slot], send_sem=cf_send.at[i], recv_sem=cf_recv.at[slot],
            device_id=(t, lax.rem(c + i, nc)), device_id_type=MESH)

    for i in range(1, nc):
        chan_flag(i, c).start()

    table[...] = class_table().astype(BF16)

    for i in range(1, nc):
        payload(i, lax.rem(c + i, nc)).wait_recv()

    @pl.when(from_low | from_high)
    def _():
        for g in range(nc):
            pltpu.make_async_remote_copy(
                src_ref=packed.at[pl.ds(0, GROUPS_IN)], dst_ref=edge.at[g, 0:GROUPS_IN], send_sem=edge_send.at[0],
                recv_sem=edge_recv.at[g], device_id=(t, g), device_id_type=MESH).wait_recv()

    for i in range(1, nc):
        chan_flag(i, lax.rem(c + i, nc)).wait_recv()
    flag[...] = jnp.max(chan_flags[...], axis=0)
    for i in range(1, nt):
        tile_flag(i, t).wait_send()
    for i in range(1, nc):
        payload(i, c).wait_send()
        chan_flag(i, c).wait_send()

    @pl.when(t < nt - 1)
    def _():
        edge_up().wait_send()

    @pl.when(t > 0)
    def _():
        edge_down().wait_send()


def owned_rows(got, edge, table, out, rows, total):
    c = lax.axis_index("chan")
    nc = got.shape[0]
    per = got.shape[1]
    main = nc * per
    count = main + nc * 8

    lanes = lax.broadcasted_iota(jnp.int32, (1, 256), 1) // LOW
    both = jnp.concatenate([got[...].reshape(main, 256), edge[...].reshape(nc * 8, 256)], axis=0)
    index = lax.broadcasted_iota(jnp.int32, (count, 256), 0)
    shift = jnp.where(index < main, BUCKET * ((index % per) // GROUPS_IN - 1), jnp.where(c == 0, -BUCKET, 2 * BUCKET))
    both = both + jnp.where(lanes == 3, shift, 0).astype(F32)
    used = jnp.where(lax.broadcasted_iota(jnp.int32, (128, count), 0) == 6 * LOW - 128, both[:, 128:256].T, 0.0)
    used = jnp.sum(used, axis=0, keepdims=True)
    before = (
        lax.broadcasted_iota(jnp.int32, (count, count), 0) < lax.broadcasted_iota(jnp.int32, (count, count), 1)
    ).astype(F32).astype(BF16)
    rank = jnp.dot(jnp.broadcast_to(used, (8, count)).astype(BF16), before, preferred_element_type=F32)[0:1]
    pick = jnp.where(
        (lax.broadcasted_iota(jnp.int32, (count, count), 0).astype(F32) == rank) & (used > 0.5), 1.0, 0.0
    ).astype(BF16)
    high = both.astype(BF16)
    low = (both - high.astype(F32)).astype(BF16)
    rows[...] = jnp.dot(pick, high, preferred_element_type=F32) + jnp.dot(pick, low, preferred_element_type=F32)
    trips = (jnp.sum(used).astype(jnp.int32) + 7) // 8

    total[...] = jnp.zeros_like(total)
    lane = lax.broadcasted_iota(jnp.int32, (256, 128), 1)

    def body(i, carry):
        block = rows[pl.ds(pl.multiple_of(8 * i, 8), 8), :]
        klass = block[:, 128 : 128 + LOW] * float(PLANES) + block[:, 128 + LOW : 128 + 2 * LOW]
        first = block[:, 0:128].T
        second = jnp.concatenate([klass, block[:, 128 + LOW : 256]], axis=1).T

        def field(x, f):
            return jnp.concatenate(
                [jnp.broadcast_to(x[f * LOW : (f + 1) * LOW, r : r + 1], (LOW, 128)) for r in range(8)], axis=0)

        re, im = field(first, 0), field(first, 1)
        col, row = field(first, 2).astype(jnp.int32), field(first, 3).astype(jnp.int32)
        hot = (field(second, 0).astype(jnp.int32) == lane).astype(F32).astype(BF16)
        values = jnp.dot(hot, table[...], preferred_element_type=F32)

        def look_up(distance):
            return jnp.take_along_axis(values, jnp.minimum(jnp.abs(distance), 127), axis=1, mode="promise_in_bounds")

        weights = (look_up(lane // 2 - row) * jnp.where(lane % 2 == 0, re, im)).astype(BF16)
        columns = jnp.concatenate([look_up(lane + 128 * b - col).astype(BF16) for b in range(G // 128)], axis=1)
        total[...] += lax.dot_general(weights, columns, (((0,), (0,)), ((), ())), preferred_element_type=F32)
        return carry

    lax.fori_loop(0, trips, body, 0)
    out[...] = total[...].reshape(out.shape)


def per_device(visibilities, cell_offsets, support_index, w_plane, live_counts):
    nt, nc = lax.axis_size("tile"), lax.axis_size("chan")
    slots = visibilities.shape[-1]
    groups = (G // BUCKET + 2) * GROUPS_IN
    vmem = pl.BlockSpec(memory_space=pltpu.VMEM)
    got, edge, table, flag = pl.pallas_call(
        exchange,
        out_shape=(
            jax.ShapeDtypeStruct((nc, 4 * GROUPS_IN, FIELDS * LOW), F32),
            jax.ShapeDtypeStruct((nc, 8, FIELDS * LOW), F32),
            jax.ShapeDtypeStruct((128, 128), BF16),
            jax.ShapeDtypeStruct((8, 128), F32),
        ),
        in_specs=[pl.BlockSpec(memory_space=pl.ANY)] * 4 + [pl.BlockSpec(memory_space=pltpu.SMEM)],
        out_specs=(vmem,) * 4,
        scratch_shapes=[
            pltpu.VMEM((2, slots), F32),
            pltpu.VMEM((2, slots), jnp.int32),
            pltpu.VMEM((1, slots), jnp.int32),
            pltpu.VMEM((1, slots), jnp.int32),
            pltpu.VMEM((groups, FIELDS * LOW), F32),
            pltpu.VMEM((nt, 8, 128), F32),
            pltpu.VMEM((nc, 8, 128), F32),
            pltpu.SemaphoreType.DMA((4,)),
            pltpu.SemaphoreType.DMA((nc,)),
            pltpu.SemaphoreType.DMA((nc,)),
            pltpu.SemaphoreType.DMA((2,)),
            pltpu.SemaphoreType.DMA((nc,)),
            pltpu.SemaphoreType.DMA((nt,)),
            pltpu.SemaphoreType.DMA((nt,)),
            pltpu.SemaphoreType.DMA((nc,)),
            pltpu.SemaphoreType.DMA((nc,)),
        ],
        compiler_params=pltpu.CompilerParams(collective_id=0, has_side_effects=True, vmem_limit_bytes=62 << 20),
    )(visibilities, cell_offsets, support_index, w_plane, live_counts)

    def usual(*_):
        return pl.pallas_call(
            owned_rows,
            out_shape=jax.ShapeDtypeStruct((G // nc, 2, G), F32),
            in_specs=[vmem] * 3,
            out_specs=vmem,
            scratch_shapes=[pltpu.VMEM((nc * (4 * GROUPS_IN + 8), FIELDS * LOW), F32), pltpu.VMEM((2 * G // nc, G), F32)],
            compiler_params=pltpu.CompilerParams(vmem_limit_bytes=40 << 20),
        )(got, edge, table)

    return lax.cond(
        flag[0, 0] > 0.5, any_cells, usual, visibilities, cell_offsets, support_index, w_plane, live_counts
    )


def solution(mesh):
    in_specs = (
        P("tile", "chan", None, None),
        P("tile", "chan", None, None),
        P("tile", "chan", None),
        P("tile", "chan", None),
        P("tile", "chan"),
    )
    out_specs = P(("tile", "chan"), None, None)
    return jax.shard_map(
        per_device, mesh=mesh, in_specs=in_specs, out_specs=out_specs, check_vma=False
    )
```

```python
import functools
import math

import jax
import jax.numpy as jnp
from jax import lax
from jax.experimental import pallas as pl
from jax.experimental.pallas import tpu as pltpu
from jax.sharding import PartitionSpec as P

G = 1024
M = 32
PLANES = 16
BETA = 7.0

BUCKET = 32
CAP = 128
LOW = 32
GROUPS_IN = CAP // LOW
FIELDS = 8
MESH = pl.DeviceIdType.MESH
F32 = jnp.float32
BF16 = jnp.bfloat16


def bessel_zero(value):
    quarter = value * value * 0.25
    term = jnp.ones_like(value)
    total = jnp.ones_like(value)
    for index in range(1, 30):
        term = term * quarter * (1.0 / float(index * index))
        total = total + term
    return total


def kernel_values(distance, half_width, w_coef):
    ratio = distance / half_width
    inside = jnp.abs(ratio) < 1.0
    radius = jnp.sqrt(jnp.maximum(1.0 - ratio * ratio, 0.0))
    bessel = bessel_zero(BETA * radius) / bessel_zero(jnp.float32(BETA))
    taper = jnp.cos(jnp.pi * w_coef * ratio * ratio)
    return jnp.where(inside, bessel * taper, jnp.float32(0.0))


def flatten_groups(vis_block, offset_block, support_block, plane_block, count_block):
    slot_total = vis_block.shape[-1]
    slot_ids = jnp.arange(slot_total, dtype=jnp.int32)
    live = (slot_ids[None, :] < count_block[:, None]).astype(jnp.float32).reshape(-1)
    real_part = vis_block[:, 0].reshape(-1) * live
    imag_part = vis_block[:, 1].reshape(-1) * live
    row_cell = offset_block[:, 0].reshape(-1).astype(jnp.float32)
    col_cell = offset_block[:, 1].reshape(-1).astype(jnp.float32)
    half_width = 8.0 * (support_block.reshape(-1) + 1).astype(jnp.float32)
    w_coef = 0.5 * (plane_block.reshape(-1) + 1).astype(jnp.float32) / PLANES
    return (real_part, imag_part, row_cell, col_cell, half_width, w_coef)


def grid_part(flat, row_start, row_count, width):
    total_vis = flat[0].shape[0]
    block_len = math.gcd(total_vis, 512)
    stacked = tuple((item.reshape(total_vis // block_len, block_len) for item in flat))
    row_pos = (row_start + jnp.arange(row_count, dtype=jnp.int32)).astype(jnp.float32)
    col_pos = jnp.arange(width, dtype=jnp.int32).astype(jnp.float32)

    def step_block(total, values):
        real_part, imag_part, row_cell, col_cell, half_width, w_coef = values
        row_weights = kernel_values(
            row_pos[None, :] - row_cell[:, None], half_width[:, None], w_coef[:, None]
        ).astype(jnp.bfloat16)
        col_kern = kernel_values(
            col_pos[None, :] - col_cell[:, None], half_width[:, None], w_coef[:, None]
        )
        col_weights = jnp.concatenate(
            [real_part[:, None] * col_kern, imag_part[:, None] * col_kern], axis=1
        ).astype(jnp.bfloat16)
        product = lax.dot_general(
            row_weights, col_weights, (((0,), (0,)), ((), ())), preferred_element_type=jnp.float32
        )
        return (total + product, None)

    start_total = jnp.zeros((row_count, 2 * width), jnp.float32)
    total, _ = lax.scan(step_block, start_total, stacked)
    return total.reshape(row_count, 2, width)


def any_cells(visibilities, cell_offsets, support_index, w_plane, live_counts):
    tiles, parts = lax.axis_size("tile"), lax.axis_size("chan")
    share = G // parts
    first_row = lax.axis_index("chan") * share - M
    held = jnp.stack(
        flatten_groups(visibilities[0], cell_offsets[0], support_index[0], w_plane[0], live_counts[0])
    )

    def step(_, carry):
        total, held = carry
        total = total + grid_part(held, first_row, share + 2 * M, G)
        return total, lax.ppermute(held, "chan", [(i, (i + 1) % parts) for i in range(parts)])

    total, _ = lax.fori_loop(0, parts, step, (jnp.zeros((share + 2 * M, 2, G), F32), held))
    last = parts - 1
    left_in = lax.ppermute(
        total[share + M :], ("tile", "chan"), [(t * parts + last, (t + 1) * parts) for t in range(tiles - 1)]
    )
    right_in = lax.ppermute(
        total[:M], ("tile", "chan"), [(t * parts, (t - 1) * parts + last) for t in range(1, tiles)]
    )
    owned = total[M : M + share]
    return owned.at[:M].add(left_in).at[share - M :].add(right_in)


def class_table():
    klass = lax.broadcasted_iota(jnp.int32, (128, 128), 0)
    distance = lax.broadcasted_iota(jnp.int32, (128, 128), 1).astype(F32)
    half = (8 * (klass // PLANES + 1)).astype(F32)
    w_coef = 0.5 * (klass % PLANES + 1).astype(F32) / PLANES
    ratio = distance / half
    inside = (ratio < 1.0) & (klass < 4 * PLANES)
    bound = jnp.minimum(ratio, 1.0)
    square = bound * bound
    radius = jnp.sqrt(jnp.maximum(1.0 - square, 0.0))
    bessel = bessel_zero(BETA * radius) / bessel_zero(jnp.full((128, 128), BETA, F32))
    taper = jnp.cos(jnp.pi * w_coef * square)
    return jnp.where(inside, bessel * taper, 0.0)


def exchange(vis, cell, sup, wpl, cnt, got, edge, table, flag, vis_v, cell_v, sup_v, wpl_v, packed, tile_flags, chan_flags,
             load_sem, send_sem, recv_sem, edge_send, edge_recv, tf_send, tf_recv, cf_send, cf_recv):
    t, c = lax.axis_index("tile"), lax.axis_index("chan")
    nt, nc = lax.axis_size("tile"), lax.axis_size("chan")
    slots = vis_v.shape[-1]
    loads = [
        pltpu.make_async_copy(vis.at[0, 0], vis_v, load_sem.at[0]),
        pltpu.make_async_copy(cell.at[0, 0], cell_v, load_sem.at[1]),
        pltpu.make_async_copy(sup.at[0], sup_v, load_sem.at[2]),
        pltpu.make_async_copy(wpl.at[0], wpl_v, load_sem.at[3]),
    ]
    for load in loads:
        load.start()
    edge[...] = jnp.zeros_like(edge)

    bar = pltpu.get_barrier_semaphore()
    for i in range(1, nc):
        pl.semaphore_signal(bar, inc=1, device_id=(t, lax.rem(c + i, nc)), device_id_type=MESH)
    for i in range(1, nt):
        pl.semaphore_signal(bar, inc=1, device_id=(lax.rem(t + i, nt), c), device_id_type=MESH)
    from_low = (c == 0) & (t > 0)
    from_high = (c == nc - 1) & (t < nt - 1)

    @pl.when(from_low)
    def _():
        for g in range(nc):
            pl.semaphore_signal(bar, inc=1, device_id=(t - 1, g), device_id_type=MESH)

    @pl.when(from_high)
    def _():
        for g in range(nc):
            pl.semaphore_signal(bar, inc=1, device_id=(t + 1, g), device_id_type=MESH)

    for load in loads:
        load.wait()

    live = lax.broadcasted_iota(jnp.int32, (1, slots), 1) < cnt[0, 0]
    row = cell_v[0:1]
    bucket = jnp.where(live, row // BUCKET, -1)
    buckets = G // BUCKET
    hot = (lax.broadcasted_iota(jnp.int32, (buckets, slots), 0) == bucket).astype(F32)
    step = 256
    before = (
        lax.broadcasted_iota(jnp.int32, (step, step), 0) < lax.broadcasted_iota(jnp.int32, (step, step), 1)
    ).astype(F32).astype(BF16)
    parts = []
    carry = jnp.zeros((buckets, 1), F32)
    for s in range(0, slots, step):
        piece = hot[:, s : s + step]
        ahead = jnp.dot(piece.astype(BF16), before, preferred_element_type=F32) + carry
        parts.append(jnp.sum(piece * ahead, axis=0, keepdims=True))
        carry = carry + jnp.sum(piece, axis=1, keepdims=True)
    rank = jnp.concatenate(parts, axis=1).astype(jnp.int32)
    over = (jnp.max(carry, axis=0, keepdims=True) > CAP).astype(F32)
    tile_flags[t] = jnp.broadcast_to(over, (8, 128))

    group = jnp.where(live, (bucket + 1) * GROUPS_IN + rank // LOW, -1)
    place = rank % LOW
    groups = packed.shape[0]
    to_group = (lax.broadcasted_iota(jnp.int32, (groups, slots), 0) == group).astype(F32).astype(BF16)
    at_place = lax.broadcasted_iota(jnp.int32, (LOW, slots), 0) == place

    def halves(x):
        high = x.astype(BF16).astype(F32)
        return high, x - high

    re_hi, re_lo = halves(vis_v[0:1])
    im_hi, im_lo = halves(vis_v[1:2])
    col_hi, col_lo = halves(cell_v[1:2].astype(F32))
    pieces = [re_hi, im_hi, col_hi, (row % BUCKET).astype(F32), sup_v[...].astype(F32), wpl_v[...].astype(F32),
              jnp.ones((1, slots), F32), jnp.zeros((1, slots), F32), re_lo, im_lo, col_lo, jnp.zeros((1, slots), F32)]
    spread = jnp.concatenate([jnp.where(at_place, x, 0.0).astype(BF16) for x in pieces], axis=0)
    moved = lax.dot_general(to_group, spread, (((1,), (1,)), ((), ())), preferred_element_type=F32)
    packed[:, 0:128] = moved[:, 0:128] + moved[:, 256:384]
    packed[:, 128:256] = moved[:, 128:256]

    below, above = (t > 0).astype(jnp.int32), (t < nt - 1).astype(jnp.int32)
    pl.semaphore_wait(bar, nc - 1 + nt - 1 + below + above)

    def tile_flag(i, slot):
        return pltpu.make_async_remote_copy(
            src_ref=tile_flags.at[t], dst_ref=tile_flags.at[slot], send_sem=tf_send.at[i], recv_sem=tf_recv.at[slot],
            device_id=(lax.rem(t + i, nt), c), device_id_type=MESH)

    for i in range(1, nt):
        tile_flag(i, t).start()

    width = 4 * GROUPS_IN

    def payload(i, slot):
        peer = lax.rem(c + i, nc)
        return pltpu.make_async_remote_copy(
            src_ref=packed.at[pl.ds(pl.multiple_of(8 * peer, 8), width)], dst_ref=got.at[slot], send_sem=send_sem.at[i],
            recv_sem=recv_sem.at[slot], device_id=(t, peer), device_id_type=MESH)

    order = [8, 7, 9, 6, 10, 5, 11, 4, 12, 3, 13, 2, 14, 1, 15]
    for i in order:
        payload(i, c).start()

    def edge_up():
        return pltpu.make_async_remote_copy(
            src_ref=packed.at[pl.ds(buckets * GROUPS_IN, GROUPS_IN)], dst_ref=edge.at[c, 0:GROUPS_IN], send_sem=edge_send.at[0],
            recv_sem=edge_recv.at[c], device_id=(t + 1, 0), device_id_type=MESH)

    def edge_down():
        return pltpu.make_async_remote_copy(
            src_ref=packed.at[pl.ds(GROUPS_IN, GROUPS_IN)], dst_ref=edge.at[c, 0:GROUPS_IN], send_sem=edge_send.at[1],
            recv_sem=edge_recv.at[c], device_id=(t - 1, nc - 1), device_id_type=MESH)

    @pl.when(t < nt - 1)
    def _():
        edge_up().start()

    @pl.when(t > 0)
    def _():
        edge_down().start()

    got[c] = packed[pl.ds(pl.multiple_of(8 * c, 8), width), :]

    for i in range(1, nt):
        tile_flag(i, lax.rem(t + i, nt)).wait_recv()
    chan_flags[c] = jnp.max(tile_flags[...], axis=0)

    def chan_flag(i, slot):
        return pltpu.make_async_remote_copy(
            src_ref=chan_flags.at[c], dst_ref=chan_flags.at[slot], send_sem=cf_send.at[i], recv_sem=cf_recv.at[slot],
            device_id=(t, lax.rem(c + i, nc)), device_id_type=MESH)

    for i in range(1, nc):
        chan_flag(i, c).start()

    table[...] = class_table().astype(BF16)

    for i in range(1, nc):
        payload(i, lax.rem(c + i, nc)).wait_recv()

    @pl.when(from_low | from_high)
    def _():
        for g in range(nc):
            pltpu.make_async_remote_copy(
                src_ref=packed.at[pl.ds(0, GROUPS_IN)], dst_ref=edge.at[g, 0:GROUPS_IN], send_sem=edge_send.at[0],
                recv_sem=edge_recv.at[g], device_id=(t, g), device_id_type=MESH).wait_recv()

    for i in range(1, nc):
        chan_flag(i, lax.rem(c + i, nc)).wait_recv()
    flag[0, 0] = (jnp.max(chan_flags[...]) > 0.5).astype(jnp.int32)
    for i in range(1, nt):
        tile_flag(i, t).wait_send()
    for i in range(1, nc):
        payload(i, c).wait_send()
        chan_flag(i, c).wait_send()

    @pl.when(t < nt - 1)
    def _():
        edge_up().wait_send()

    @pl.when(t > 0)
    def _():
        edge_down().wait_send()


def owned_rows(got, edge, table, out, rows, total):
    c = lax.axis_index("chan")
    nc = got.shape[0]
    per = got.shape[1]
    main = nc * per
    count = main + nc * 8

    lanes = lax.broadcasted_iota(jnp.int32, (1, 256), 1) // LOW
    both = jnp.concatenate([got[...].reshape(main, 256), edge[...].reshape(nc * 8, 256)], axis=0)
    index = lax.broadcasted_iota(jnp.int32, (count, 256), 0)
    shift = jnp.where(index < main, BUCKET * ((index % per) // GROUPS_IN - 1), jnp.where(c == 0, -BUCKET, 2 * BUCKET))
    both = both + jnp.where(lanes == 3, shift, 0).astype(F32)
    used = jnp.where(lax.broadcasted_iota(jnp.int32, (128, count), 0) == 6 * LOW - 128, both[:, 128:256].T, 0.0)
    used = jnp.sum(used, axis=0, keepdims=True)
    before = (
        lax.broadcasted_iota(jnp.int32, (count, count), 0) < lax.broadcasted_iota(jnp.int32, (count, count), 1)
    ).astype(F32).astype(BF16)
    rank = jnp.dot(jnp.broadcast_to(used, (8, count)).astype(BF16), before, preferred_element_type=F32)[0:1]
    pick = jnp.where(
        (lax.broadcasted_iota(jnp.int32, (count, count), 0).astype(F32) == rank) & (used > 0.5), 1.0, 0.0
    ).astype(BF16)
    high = both.astype(BF16)
    low = (both - high.astype(F32)).astype(BF16)
    rows[...] = jnp.dot(pick, high, preferred_element_type=F32) + jnp.dot(pick, low, preferred_element_type=F32)
    trips = (jnp.sum(used).astype(jnp.int32) + 7) // 8

    total[...] = jnp.zeros_like(total)
    lane = lax.broadcasted_iota(jnp.int32, (256, 128), 1)

    def body(i, carry):
        block = rows[pl.ds(pl.multiple_of(8 * i, 8), 8), :]
        klass = block[:, 128 : 128 + LOW] * float(PLANES) + block[:, 128 + LOW : 128 + 2 * LOW]
        first = block[:, 0:128].T
        second = jnp.concatenate([klass, block[:, 128 + LOW : 256]], axis=1).T

        def field(x, f):
            return jnp.concatenate(
                [jnp.broadcast_to(x[f * LOW : (f + 1) * LOW, r : r + 1], (LOW, 128)) for r in range(8)], axis=0)

        re, im = field(first, 0), field(first, 1)
        col, row = field(first, 2).astype(jnp.int32), field(first, 3).astype(jnp.int32)
        hot = (field(second, 0).astype(jnp.int32) == lane).astype(F32).astype(BF16)
        values = jnp.dot(hot, table[...], preferred_element_type=F32)

        def look_up(distance):
            return jnp.take_along_axis(values, jnp.minimum(jnp.abs(distance), 127), axis=1, mode="promise_in_bounds")

        weights = (look_up(lane // 2 - row) * jnp.where(lane % 2 == 0, re, im)).astype(BF16)
        columns = jnp.concatenate([look_up(lane + 128 * b - col).astype(BF16) for b in range(G // 128)], axis=1)
        total[...] += lax.dot_general(weights, columns, (((0,), (0,)), ((), ())), preferred_element_type=F32)
        return carry

    lax.fori_loop(0, trips, body, 0)
    out[...] = total[...].reshape(out.shape)


def per_device(visibilities, cell_offsets, support_index, w_plane, live_counts):
    nt, nc = lax.axis_size("tile"), lax.axis_size("chan")
    slots = visibilities.shape[-1]
    groups = (G // BUCKET + 2) * GROUPS_IN
    vmem = pl.BlockSpec(memory_space=pltpu.VMEM)
    got, edge, table, flag = pl.pallas_call(
        exchange,
        out_shape=(
            jax.ShapeDtypeStruct((nc, 4 * GROUPS_IN, FIELDS * LOW), F32),
            jax.ShapeDtypeStruct((nc, 8, FIELDS * LOW), F32),
            jax.ShapeDtypeStruct((128, 128), BF16),
            jax.ShapeDtypeStruct((1, 1), jnp.int32),
        ),
        in_specs=[pl.BlockSpec(memory_space=pl.ANY)] * 4 + [pl.BlockSpec(memory_space=pltpu.SMEM)],
        out_specs=(vmem, vmem, vmem, pl.BlockSpec(memory_space=pltpu.SMEM)),
        scratch_shapes=[
            pltpu.VMEM((2, slots), F32),
            pltpu.VMEM((2, slots), jnp.int32),
            pltpu.VMEM((1, slots), jnp.int32),
            pltpu.VMEM((1, slots), jnp.int32),
            pltpu.VMEM((groups, FIELDS * LOW), F32),
            pltpu.VMEM((nt, 8, 128), F32),
            pltpu.VMEM((nc, 8, 128), F32),
            pltpu.SemaphoreType.DMA((4,)),
            pltpu.SemaphoreType.DMA((nc,)),
            pltpu.SemaphoreType.DMA((nc,)),
            pltpu.SemaphoreType.DMA((2,)),
            pltpu.SemaphoreType.DMA((nc,)),
            pltpu.SemaphoreType.DMA((nt,)),
            pltpu.SemaphoreType.DMA((nt,)),
            pltpu.SemaphoreType.DMA((nc,)),
            pltpu.SemaphoreType.DMA((nc,)),
        ],
        compiler_params=pltpu.CompilerParams(collective_id=0, has_side_effects=True, vmem_limit_bytes=62 << 20),
    )(visibilities, cell_offsets, support_index, w_plane, live_counts)

    def usual(*_):
        return pl.pallas_call(
            owned_rows,
            out_shape=jax.ShapeDtypeStruct((G // nc, 2, G), F32),
            in_specs=[vmem] * 3,
            out_specs=vmem,
            scratch_shapes=[pltpu.VMEM((nc * (4 * GROUPS_IN + 8), FIELDS * LOW), F32), pltpu.VMEM((2 * G // nc, G), F32)],
            compiler_params=pltpu.CompilerParams(vmem_limit_bytes=40 << 20),
        )(got, edge, table)

    return lax.cond(
        flag[0, 0] > 0, any_cells, usual, visibilities, cell_offsets, support_index, w_plane, live_counts
    )


def solution(mesh):
    in_specs = (
        P("tile", "chan", None, None),
        P("tile", "chan", None, None),
        P("tile", "chan", None),
        P("tile", "chan", None),
        P("tile", "chan"),
    )
    out_specs = P(("tile", "chan"), None, None)
    return jax.shard_map(
        per_device, mesh=mesh, in_specs=in_specs, out_specs=out_specs, check_vma=False
    )
```

```python
import functools
import math

import jax
import jax.numpy as jnp
from jax import lax
from jax.experimental import pallas as pl
from jax.experimental.pallas import tpu as pltpu
from jax.sharding import PartitionSpec as P

G = 1024
M = 32
PLANES = 16
BETA = 7.0

BUCKET = 32
CAP = 128
LOW = 32
GROUPS_IN = CAP // LOW
FIELDS = 8
MESH = pl.DeviceIdType.MESH
F32 = jnp.float32
BF16 = jnp.bfloat16


def bessel_zero(value):
    quarter = value * value * 0.25
    term = jnp.ones_like(value)
    total = jnp.ones_like(value)
    for index in range(1, 30):
        term = term * quarter * (1.0 / float(index * index))
        total = total + term
    return total


def kernel_values(distance, half_width, w_coef):
    ratio = distance / half_width
    inside = jnp.abs(ratio) < 1.0
    radius = jnp.sqrt(jnp.maximum(1.0 - ratio * ratio, 0.0))
    bessel = bessel_zero(BETA * radius) / bessel_zero(jnp.float32(BETA))
    taper = jnp.cos(jnp.pi * w_coef * ratio * ratio)
    return jnp.where(inside, bessel * taper, jnp.float32(0.0))


def flatten_groups(vis_block, offset_block, support_block, plane_block, count_block):
    slot_total = vis_block.shape[-1]
    slot_ids = jnp.arange(slot_total, dtype=jnp.int32)
    live = (slot_ids[None, :] < count_block[:, None]).astype(jnp.float32).reshape(-1)
    real_part = vis_block[:, 0].reshape(-1) * live
    imag_part = vis_block[:, 1].reshape(-1) * live
    row_cell = offset_block[:, 0].reshape(-1).astype(jnp.float32)
    col_cell = offset_block[:, 1].reshape(-1).astype(jnp.float32)
    half_width = 8.0 * (support_block.reshape(-1) + 1).astype(jnp.float32)
    w_coef = 0.5 * (plane_block.reshape(-1) + 1).astype(jnp.float32) / PLANES
    return (real_part, imag_part, row_cell, col_cell, half_width, w_coef)


def grid_part(flat, row_start, row_count, width):
    total_vis = flat[0].shape[0]
    block_len = math.gcd(total_vis, 512)
    stacked = tuple((item.reshape(total_vis // block_len, block_len) for item in flat))
    row_pos = (row_start + jnp.arange(row_count, dtype=jnp.int32)).astype(jnp.float32)
    col_pos = jnp.arange(width, dtype=jnp.int32).astype(jnp.float32)

    def step_block(total, values):
        real_part, imag_part, row_cell, col_cell, half_width, w_coef = values
        row_weights = kernel_values(
            row_pos[None, :] - row_cell[:, None], half_width[:, None], w_coef[:, None]
        ).astype(jnp.bfloat16)
        col_kern = kernel_values(
            col_pos[None, :] - col_cell[:, None], half_width[:, None], w_coef[:, None]
        )
        col_weights = jnp.concatenate(
            [real_part[:, None] * col_kern, imag_part[:, None] * col_kern], axis=1
        ).astype(jnp.bfloat16)
        product = lax.dot_general(
            row_weights, col_weights, (((0,), (0,)), ((), ())), preferred_element_type=jnp.float32
        )
        return (total + product, None)

    start_total = jnp.zeros((row_count, 2 * width), jnp.float32)
    total, _ = lax.scan(step_block, start_total, stacked)
    return total.reshape(row_count, 2, width)


def any_cells(visibilities, cell_offsets, support_index, w_plane, live_counts):
    tiles, parts = lax.axis_size("tile"), lax.axis_size("chan")
    share = G // parts
    first_row = lax.axis_index("chan") * share - M
    held = jnp.stack(
        flatten_groups(visibilities[0], cell_offsets[0], support_index[0], w_plane[0], live_counts[0])
    )

    def step(_, carry):
        total, held = carry
        total = total + grid_part(held, first_row, share + 2 * M, G)
        return total, lax.ppermute(held, "chan", [(i, (i + 1) % parts) for i in range(parts)])

    total, _ = lax.fori_loop(0, parts, step, (jnp.zeros((share + 2 * M, 2, G), F32), held))
    last = parts - 1
    left_in = lax.ppermute(
        total[share + M :], ("tile", "chan"), [(t * parts + last, (t + 1) * parts) for t in range(tiles - 1)]
    )
    right_in = lax.ppermute(
        total[:M], ("tile", "chan"), [(t * parts, (t - 1) * parts + last) for t in range(1, tiles)]
    )
    owned = total[M : M + share]
    return owned.at[:M].add(left_in).at[share - M :].add(right_in)


def class_table():
    shape = (2 * M, 4 * PLANES)
    klass = lax.broadcasted_iota(jnp.int32, shape, 1)
    distance = jnp.abs(lax.broadcasted_iota(jnp.int32, shape, 0) - M).astype(F32)
    half = (8 * (klass // PLANES + 1)).astype(F32)
    w_coef = 0.5 * (klass % PLANES + 1).astype(F32) / PLANES
    ratio = jnp.minimum(distance / half, 1.0)
    square = ratio * ratio
    radius = jnp.sqrt(jnp.maximum(1.0 - square, 0.0))
    bessel = bessel_zero(BETA * radius) / bessel_zero(jnp.full(shape, BETA, F32))
    taper = jnp.cos(jnp.pi * w_coef * square)
    return jnp.where(ratio < 1.0, bessel * taper, 0.0).astype(BF16)


def exchange(vis, cell, sup, wpl, cnt, got, edge, table, flag, vis_v, cell_v, sup_v, wpl_v, packed, tile_flags,
             load_sem, send_sem, recv_sem, edge_send, edge_recv, tf_send, tf_recv):
    t, c = lax.axis_index("tile"), lax.axis_index("chan")
    nt, nc = lax.axis_size("tile"), lax.axis_size("chan")
    slots = vis_v.shape[-1]
    loads = [
        pltpu.make_async_copy(vis.at[0, 0], vis_v, load_sem.at[0]),
        pltpu.make_async_copy(cell.at[0, 0], cell_v, load_sem.at[1]),
        pltpu.make_async_copy(sup.at[0], sup_v, load_sem.at[2]),
        pltpu.make_async_copy(wpl.at[0], wpl_v, load_sem.at[3]),
    ]
    for load in loads:
        load.start()
    edge[...] = jnp.zeros_like(edge)

    bar = pltpu.get_barrier_semaphore()
    for i in range(1, nc):
        pl.semaphore_signal(bar, inc=1, device_id=(t, lax.rem(c + i, nc)), device_id_type=MESH)
    for i in range(1, nt):
        pl.semaphore_signal(bar, inc=1, device_id=(lax.rem(t + i, nt), c), device_id_type=MESH)
    from_low = (c == 0) & (t > 0)
    from_high = (c == nc - 1) & (t < nt - 1)

    @pl.when(from_low)
    def _():
        for g in range(nc):
            pl.semaphore_signal(bar, inc=1, device_id=(t - 1, g), device_id_type=MESH)

    @pl.when(from_high)
    def _():
        for g in range(nc):
            pl.semaphore_signal(bar, inc=1, device_id=(t + 1, g), device_id_type=MESH)

    for load in loads:
        load.wait()

    live = lax.broadcasted_iota(jnp.int32, (1, slots), 1) < cnt[0, 0]
    row = cell_v[0:1]
    bucket = jnp.where(live, row // BUCKET, -1)
    buckets = G // BUCKET
    hot = (lax.broadcasted_iota(jnp.int32, (buckets, slots), 0) == bucket).astype(F32)
    step = 256
    before = (
        lax.broadcasted_iota(jnp.int32, (step, step), 0) < lax.broadcasted_iota(jnp.int32, (step, step), 1)
    ).astype(F32).astype(BF16)
    parts = []
    carry = jnp.zeros((buckets, 1), F32)
    for s in range(0, slots, step):
        piece = hot[:, s : s + step]
        ahead = jnp.dot(piece.astype(BF16), before, preferred_element_type=F32) + carry
        parts.append(jnp.sum(piece * ahead, axis=0, keepdims=True))
        carry = carry + jnp.sum(piece, axis=1, keepdims=True)
    rank = jnp.concatenate(parts, axis=1).astype(jnp.int32)
    over = (jnp.max(carry, axis=0, keepdims=True) > CAP).astype(F32)
    tile_flags[t] = jnp.broadcast_to(over, (8, 128))

    below, above = (t > 0).astype(jnp.int32), (t < nt - 1).astype(jnp.int32)
    pl.semaphore_wait(bar, nc - 1 + nt - 1 + below + above)

    def tile_flag(i, slot):
        return pltpu.make_async_remote_copy(
            src_ref=tile_flags.at[t], dst_ref=tile_flags.at[slot], send_sem=tf_send.at[i], recv_sem=tf_recv.at[slot],
            device_id=(lax.rem(t + i, nt), c), device_id_type=MESH)

    for i in range(1, nt):
        tile_flag(i, t).start()

    group = jnp.where(live, (bucket + 1) * GROUPS_IN + rank // LOW, -1)
    place = rank % LOW
    groups = packed.shape[0]
    to_group = (lax.broadcasted_iota(jnp.int32, (groups, slots), 0) == group).astype(F32).astype(BF16)
    at_place = lax.broadcasted_iota(jnp.int32, (LOW, slots), 0) == place

    def halves(x):
        high = x.astype(BF16).astype(F32)
        return high, x - high

    re_hi, re_lo = halves(vis_v[0:1])
    im_hi, im_lo = halves(vis_v[1:2])
    col_hi, col_lo = halves(cell_v[1:2].astype(F32))
    pieces = [re_hi, im_hi, col_hi, (row % BUCKET).astype(F32), sup_v[...].astype(F32), wpl_v[...].astype(F32),
              jnp.ones((1, slots), F32), jnp.zeros((1, slots), F32), re_lo, im_lo, col_lo, jnp.zeros((1, slots), F32)]
    spread = jnp.concatenate([jnp.where(at_place, x, 0.0).astype(BF16) for x in pieces], axis=0)
    moved = lax.dot_general(to_group, spread, (((1,), (1,)), ((), ())), preferred_element_type=F32)
    packed[:, 0:128] = moved[:, 0:128] + moved[:, 256:384]
    for i in range(1, nt):
        tile_flag(i, lax.rem(t + i, nt)).wait_recv()
    over = jnp.max(tile_flags[...], axis=0)[0:1]
    spare = lax.broadcasted_iota(jnp.int32, (1, 128), 1) >= 3 * LOW
    packed[:, 128:256] = moved[:, 128:256] + jnp.where(spare, over, 0.0)

    width = 4 * GROUPS_IN

    def payload(i, slot):
        peer = lax.rem(c + i, nc)
        return pltpu.make_async_remote_copy(
            src_ref=packed.at[pl.ds(pl.multiple_of(8 * peer, 8), width)], dst_ref=got.at[slot], send_sem=send_sem.at[i],
            recv_sem=recv_sem.at[slot], device_id=(t, peer), device_id_type=MESH)

    order = [8, 7, 9, 6, 10, 5, 11, 4, 12, 3, 13, 2, 14, 1, 15]
    for i in order:
        payload(i, c).start()

    def edge_up():
        return pltpu.make_async_remote_copy(
            src_ref=packed.at[pl.ds(buckets * GROUPS_IN, GROUPS_IN)], dst_ref=edge.at[c, 0:GROUPS_IN], send_sem=edge_send.at[0],
            recv_sem=edge_recv.at[c], device_id=(t + 1, 0), device_id_type=MESH)

    def edge_down():
        return pltpu.make_async_remote_copy(
            src_ref=packed.at[pl.ds(GROUPS_IN, GROUPS_IN)], dst_ref=edge.at[c, 0:GROUPS_IN], send_sem=edge_send.at[1],
            recv_sem=edge_recv.at[c], device_id=(t - 1, nc - 1), device_id_type=MESH)

    @pl.when(t < nt - 1)
    def _():
        edge_up().start()

    @pl.when(t > 0)
    def _():
        edge_down().start()

    got[c] = packed[pl.ds(pl.multiple_of(8 * c, 8), width), :]

    table[...] = class_table()

    for i in range(1, nc):
        payload(i, lax.rem(c + i, nc)).wait_recv()

    @pl.when(from_low | from_high)
    def _():
        for g in range(nc):
            pltpu.make_async_remote_copy(
                src_ref=packed.at[pl.ds(0, GROUPS_IN)], dst_ref=edge.at[g, 0:GROUPS_IN], send_sem=edge_send.at[0],
                recv_sem=edge_recv.at[g], device_id=(t, g), device_id_type=MESH).wait_recv()

    top = jnp.max(jnp.max(got[:, :, 128:256], axis=0), axis=0, keepdims=True)
    flag[0, 0] = (jnp.max(jnp.where(spare, top, 0.0)) > 0.5).astype(jnp.int32)
    for i in range(1, nt):
        tile_flag(i, t).wait_send()
    for i in range(1, nc):
        payload(i, c).wait_send()

    @pl.when(t < nt - 1)
    def _():
        edge_up().wait_send()

    @pl.when(t > 0)
    def _():
        edge_down().wait_send()


def turned(values, by, sub):
    for bit in (32, 16, 8):
        chosen = (by & bit) != 0
        values = [jnp.where(chosen, values[(k - bit // 8) % 8], values[k]) for k in range(8)]
    for bit in (4, 2, 1):
        chosen = (by & bit) != 0
        rolled = [pltpu.roll(x, bit, 0) for x in values]
        values = [
            jnp.where(chosen, jnp.where(sub < bit, rolled[(k - 1) % 8], rolled[k]), values[k]) for k in range(8)
        ]
    return values


def owned_rows(got, edge, table, out, real, whole, total, weights, columns):
    c = lax.axis_index("chan")
    nc, per = got.shape[0], got.shape[1]
    main = nc * per
    count = main + nc * 8
    quarter = count // 4

    lanes = lax.broadcasted_iota(jnp.int32, (1, 256), 1) // LOW
    both = jnp.concatenate([got[...].reshape(main, 256), edge[...].reshape(nc * 8, 256)], axis=0)
    index = lax.broadcasted_iota(jnp.int32, (count, 256), 0)
    shift = jnp.where(index < main, BUCKET * ((index % per) // GROUPS_IN - 1), jnp.where(c == 0, -BUCKET, 2 * BUCKET))
    both = both + jnp.where(lanes == 3, shift, 0).astype(F32)
    used = jnp.where(lax.broadcasted_iota(jnp.int32, (128, count), 0) == 6 * LOW - 128, both[:, 128:256].T, 0.0)
    used = jnp.sum(used, axis=0, keepdims=True)
    before = (
        lax.broadcasted_iota(jnp.int32, (count, count), 0) < lax.broadcasted_iota(jnp.int32, (count, count), 1)
    ).astype(F32).astype(BF16)
    rank = jnp.dot(jnp.broadcast_to(used, (8, count)).astype(BF16), before, preferred_element_type=F32)[0:1]
    rank = jnp.where(used > 0.5, rank, -1.0)
    place = lax.broadcasted_iota(jnp.int32, (count, count), 0)
    place = (4 * (place % quarter) + place // quarter).astype(F32)
    pick = jnp.where(place == rank, 1.0, 0.0).astype(BF16)
    high = both.astype(BF16)
    low = (both - high.astype(F32)).astype(BF16)
    rows = jnp.dot(pick, high, preferred_element_type=F32) + jnp.dot(pick, low, preferred_element_type=F32)
    spot = lax.broadcasted_iota(jnp.int32, (quarter, 128), 1) // LOW

    def field(f):
        part, offset = divmod(f, 4)
        result = None
        for s in range(4):
            x = rows[s * quarter : (s + 1) * quarter, 128 * part : 128 * part + 128]
            if (s - offset) % 4:
                x = pltpu.roll(x, ((s - offset) % 4) * LOW, 1)
            result = x if result is None else jnp.where(spot == s, x, result)
        return result

    real[0], real[1] = field(0), field(1)
    whole[0], whole[1] = field(2).astype(jnp.int32) - M, field(3).astype(jnp.int32) - M
    whole[2] = (field(4) * float(PLANES) + field(5)).astype(jnp.int32)
    size = weights.shape[-1]
    lines = size // 128
    chunks = (jnp.sum(used).astype(jnp.int32) + 4 * lines - 1) // (4 * lines)

    total[...] = jnp.zeros_like(total)
    sub = lax.broadcasted_iota(jnp.int32, (8, size), 0)

    def fill(i, slot):
        def line(ref, f):
            return jnp.concatenate(
                [jnp.broadcast_to(ref[f, pl.ds(lines * i + h, 1), :], (8, 128)) for h in range(lines)], axis=1)

        klass = line(whole, 2)
        hot = jnp.concatenate([(klass == sub + 8 * k).astype(F32) for k in range(8)], axis=0).astype(BF16)
        values = jnp.dot(table[...], hot, preferred_element_type=F32)
        values = [values[8 * k : 8 * k + 8] for k in range(8)]
        row = line(whole, 1)
        by, first = row & 63, row >> 6
        mine = [
            jnp.where(jnp.where(sub + 8 * k < by, first + 1, first) == 0, x, 0.0)
            for k, x in enumerate(turned(values, by, sub))
        ]
        re, im = line(real, 0), line(real, 1)
        weights[slot, 0:64] = jnp.concatenate([x * re for x in mine], axis=0).astype(BF16)
        weights[slot, 64:128] = jnp.concatenate([x * im for x in mine], axis=0).astype(BF16)
        col = line(whole, 0)
        by, first = col & 63, col >> 6
        window = jnp.concatenate(turned(values, by, sub), axis=0).astype(BF16)
        block = jnp.concatenate(
            [jnp.where(sub + 8 * k < by, first + 1, first).astype(F32) for k in range(8)], axis=0).astype(BF16)
        for b in range(G // 64):
            columns[slot, 64 * b : 64 * b + 64] = jnp.where(
                block == jnp.asarray(b, BF16), window, jnp.asarray(0, BF16))

    def add(slot):
        total[...] += lax.dot_general(
            weights[slot], columns[slot], (((1,), (1,)), ((), ())), preferred_element_type=F32)

    fill(0, 0)

    def body(j, carry):
        fill(2 * j + 1, 1)
        add(0)
        fill(2 * j + 2, 0)
        add(1)
        return carry

    lax.fori_loop(0, (chunks + 1) // 2, body, 0)
    out[:, 0, :] = total[0:64]
    out[:, 1, :] = total[64:128]


def per_device(visibilities, cell_offsets, support_index, w_plane, live_counts):
    nt, nc = lax.axis_size("tile"), lax.axis_size("chan")
    slots = visibilities.shape[-1]
    groups = (G // BUCKET + 2) * GROUPS_IN
    vmem = pl.BlockSpec(memory_space=pltpu.VMEM)
    got, edge, table, flag = pl.pallas_call(
        exchange,
        out_shape=(
            jax.ShapeDtypeStruct((nc, 4 * GROUPS_IN, FIELDS * LOW), F32),
            jax.ShapeDtypeStruct((nc, 8, FIELDS * LOW), F32),
            jax.ShapeDtypeStruct((2 * M, 4 * PLANES), BF16),
            jax.ShapeDtypeStruct((1, 1), jnp.int32),
        ),
        in_specs=[pl.BlockSpec(memory_space=pl.ANY)] * 4 + [pl.BlockSpec(memory_space=pltpu.SMEM)],
        out_specs=(vmem, vmem, vmem, pl.BlockSpec(memory_space=pltpu.SMEM)),
        scratch_shapes=[
            pltpu.VMEM((2, slots), F32),
            pltpu.VMEM((2, slots), jnp.int32),
            pltpu.VMEM((1, slots), jnp.int32),
            pltpu.VMEM((1, slots), jnp.int32),
            pltpu.VMEM((groups, FIELDS * LOW), F32),
            pltpu.VMEM((nt, 8, 128), F32),
            pltpu.SemaphoreType.DMA((4,)),
            pltpu.SemaphoreType.DMA((nc,)),
            pltpu.SemaphoreType.DMA((nc,)),
            pltpu.SemaphoreType.DMA((2,)),
            pltpu.SemaphoreType.DMA((nc,)),
            pltpu.SemaphoreType.DMA((nt,)),
            pltpu.SemaphoreType.DMA((nt,)),
        ],
        compiler_params=pltpu.CompilerParams(collective_id=0, has_side_effects=True, vmem_limit_bytes=62 << 20),
    )(visibilities, cell_offsets, support_index, w_plane, live_counts)

    groups_got = nc * (4 * GROUPS_IN + 8)

    def usual(*_):
        return pl.pallas_call(
            owned_rows,
            out_shape=jax.ShapeDtypeStruct((G // nc, 2, G), F32),
            in_specs=[vmem] * 3,
            out_specs=vmem,
            scratch_shapes=[
                pltpu.VMEM((2, groups_got // 4, 128), F32),
                pltpu.VMEM((3, groups_got // 4, 128), jnp.int32),
                pltpu.VMEM((2 * G // nc, G), F32),
                pltpu.VMEM((2, 2 * G // nc, 512), BF16),
                pltpu.VMEM((2, G, 512), BF16),
            ],
            compiler_params=pltpu.CompilerParams(vmem_limit_bytes=40 << 20),
        )(got, edge, table)

    return lax.cond(
        flag[0, 0] > 0, any_cells, usual, visibilities, cell_offsets, support_index, w_plane, live_counts
    )


def solution(mesh):
    in_specs = (
        P("tile", "chan", None, None),
        P("tile", "chan", None, None),
        P("tile", "chan", None),
        P("tile", "chan", None),
        P("tile", "chan"),
    )
    out_specs = P(("tile", "chan"), None, None)
    return jax.shard_map(
        per_device, mesh=mesh, in_specs=in_specs, out_specs=out_specs, check_vma=False
    )
```

```python
import functools
import math

import jax
import jax.numpy as jnp
from jax import lax
from jax.experimental import pallas as pl
from jax.experimental.pallas import tpu as pltpu
from jax.sharding import PartitionSpec as P

G = 1024
M = 32
PLANES = 16
BETA = 7.0

BUCKET = 32
CAP = 128
LOW = 32
GROUPS_IN = CAP // LOW
EARLY = 2
FIELDS = 8
MESH = pl.DeviceIdType.MESH
F32 = jnp.float32
BF16 = jnp.bfloat16


def bessel_zero(value):
    quarter = value * value * 0.25
    term = jnp.ones_like(value)
    total = jnp.ones_like(value)
    for index in range(1, 30):
        term = term * quarter * (1.0 / float(index * index))
        total = total + term
    return total


def kernel_values(distance, half_width, w_coef):
    ratio = distance / half_width
    inside = jnp.abs(ratio) < 1.0
    radius = jnp.sqrt(jnp.maximum(1.0 - ratio * ratio, 0.0))
    bessel = bessel_zero(BETA * radius) / bessel_zero(jnp.float32(BETA))
    taper = jnp.cos(jnp.pi * w_coef * ratio * ratio)
    return jnp.where(inside, bessel * taper, jnp.float32(0.0))


def flatten_groups(vis_block, offset_block, support_block, plane_block, count_block):
    slot_total = vis_block.shape[-1]
    slot_ids = jnp.arange(slot_total, dtype=jnp.int32)
    live = (slot_ids[None, :] < count_block[:, None]).astype(jnp.float32).reshape(-1)
    real_part = vis_block[:, 0].reshape(-1) * live
    imag_part = vis_block[:, 1].reshape(-1) * live
    row_cell = offset_block[:, 0].reshape(-1).astype(jnp.float32)
    col_cell = offset_block[:, 1].reshape(-1).astype(jnp.float32)
    half_width = 8.0 * (support_block.reshape(-1) + 1).astype(jnp.float32)
    w_coef = 0.5 * (plane_block.reshape(-1) + 1).astype(jnp.float32) / PLANES
    return (real_part, imag_part, row_cell, col_cell, half_width, w_coef)


def grid_part(flat, row_start, row_count, width):
    total_vis = flat[0].shape[0]
    block_len = math.gcd(total_vis, 512)
    stacked = tuple((item.reshape(total_vis // block_len, block_len) for item in flat))
    row_pos = (row_start + jnp.arange(row_count, dtype=jnp.int32)).astype(jnp.float32)
    col_pos = jnp.arange(width, dtype=jnp.int32).astype(jnp.float32)

    def step_block(total, values):
        real_part, imag_part, row_cell, col_cell, half_width, w_coef = values
        row_weights = kernel_values(
            row_pos[None, :] - row_cell[:, None], half_width[:, None], w_coef[:, None]
        ).astype(jnp.bfloat16)
        col_kern = kernel_values(
            col_pos[None, :] - col_cell[:, None], half_width[:, None], w_coef[:, None]
        )
        col_weights = jnp.concatenate(
            [real_part[:, None] * col_kern, imag_part[:, None] * col_kern], axis=1
        ).astype(jnp.bfloat16)
        product = lax.dot_general(
            row_weights, col_weights, (((0,), (0,)), ((), ())), preferred_element_type=jnp.float32
        )
        return (total + product, None)

    start_total = jnp.zeros((row_count, 2 * width), jnp.float32)
    total, _ = lax.scan(step_block, start_total, stacked)
    return total.reshape(row_count, 2, width)


def any_cells(visibilities, cell_offsets, support_index, w_plane, live_counts):
    tiles, parts = lax.axis_size("tile"), lax.axis_size("chan")
    share = G // parts
    first_row = lax.axis_index("chan") * share - M
    held = jnp.stack(
        flatten_groups(visibilities[0], cell_offsets[0], support_index[0], w_plane[0], live_counts[0])
    )

    def step(_, carry):
        total, held = carry
        total = total + grid_part(held, first_row, share + 2 * M, G)
        return total, lax.ppermute(held, "chan", [(i, (i + 1) % parts) for i in range(parts)])

    total, _ = lax.fori_loop(0, parts, step, (jnp.zeros((share + 2 * M, 2, G), F32), held))
    last = parts - 1
    left_in = lax.ppermute(
        total[share + M :], ("tile", "chan"), [(t * parts + last, (t + 1) * parts) for t in range(tiles - 1)]
    )
    right_in = lax.ppermute(
        total[:M], ("tile", "chan"), [(t * parts, (t - 1) * parts + last) for t in range(1, tiles)]
    )
    owned = total[M : M + share]
    return owned.at[:M].add(left_in).at[share - M :].add(right_in)


def class_table():
    shape = (2 * M, 4 * PLANES)
    klass = lax.broadcasted_iota(jnp.int32, shape, 1)
    distance = jnp.abs(lax.broadcasted_iota(jnp.int32, shape, 0) - M).astype(F32)
    half = (8 * (klass // PLANES + 1)).astype(F32)
    w_coef = 0.5 * (klass % PLANES + 1).astype(F32) / PLANES
    ratio = jnp.minimum(distance / half, 1.0)
    square = ratio * ratio
    radius = jnp.sqrt(jnp.maximum(1.0 - square, 0.0))
    bessel = bessel_zero(BETA * radius) / bessel_zero(jnp.full(shape, BETA, F32))
    taper = jnp.cos(jnp.pi * w_coef * square)
    return jnp.where(ratio < 1.0, bessel * taper, 0.0).astype(BF16)


def turned(values, by, sub):
    for bit in (32, 16, 8):
        chosen = (by & bit) != 0
        values = [jnp.where(chosen, values[(k - bit // 8) % 8], values[k]) for k in range(8)]
    for bit in (4, 2, 1):
        chosen = (by & bit) != 0
        rolled = [pltpu.roll(x, bit, 0) for x in values]
        values = [
            jnp.where(chosen, jnp.where(sub < bit, rolled[(k - 1) % 8], rolled[k]), values[k]) for k in range(8)
        ]
    return values


def lay(klass, row, col, re, im, table, weights, columns):
    sub = lax.broadcasted_iota(jnp.int32, klass.shape, 0)
    hot = jnp.concatenate([(klass == sub + 8 * k).astype(F32) for k in range(8)], axis=0).astype(BF16)
    values = jnp.dot(table[...], hot, preferred_element_type=F32)
    values = [values[8 * k : 8 * k + 8] for k in range(8)]
    by, first = row & 63, row >> 6
    mine = [
        jnp.where(jnp.where(sub + 8 * k < by, first + 1, first) == 0, x, 0.0)
        for k, x in enumerate(turned(values, by, sub))
    ]
    weights[0:64] = jnp.concatenate([x * re for x in mine], axis=0).astype(BF16)
    weights[64:128] = jnp.concatenate([x * im for x in mine], axis=0).astype(BF16)
    by, first = col & 63, col >> 6
    window = jnp.concatenate(turned(values, by, sub), axis=0).astype(BF16)
    block = jnp.concatenate(
        [jnp.where(sub + 8 * k < by, first + 1, first).astype(F32) for k in range(8)], axis=0).astype(BF16)
    for b in range(G // 64):
        columns[64 * b : 64 * b + 64] = jnp.where(block == jnp.asarray(b, BF16), window, jnp.asarray(0, BF16))


def add(total, weights, columns):
    total[...] += lax.dot_general(
        weights[...], columns[...], (((1,), (1,)), ((), ())), preferred_element_type=F32)


def exchange(vis, cell, sup, wpl, cnt, got, edge, table, total, flag, vis_v, cell_v, sup_v, wpl_v, packed, tile_flags, chan_flags,
             weights, columns,
             load_sem, send_sem, recv_sem, edge_send, edge_recv, tf_send, tf_recv, cf_send, cf_recv):
    t, c = lax.axis_index("tile"), lax.axis_index("chan")
    nt, nc = lax.axis_size("tile"), lax.axis_size("chan")
    slots = vis_v.shape[-1]
    loads = [
        pltpu.make_async_copy(vis.at[0, 0], vis_v, load_sem.at[0]),
        pltpu.make_async_copy(cell.at[0, 0], cell_v, load_sem.at[1]),
        pltpu.make_async_copy(sup.at[0], sup_v, load_sem.at[2]),
        pltpu.make_async_copy(wpl.at[0], wpl_v, load_sem.at[3]),
    ]
    for load in loads:
        load.start()
    edge[...] = jnp.zeros_like(edge)

    bar = pltpu.get_barrier_semaphore()
    for i in range(1, nc):
        pl.semaphore_signal(bar, inc=1, device_id=(t, lax.rem(c + i, nc)), device_id_type=MESH)
    for i in range(1, nt):
        pl.semaphore_signal(bar, inc=1, device_id=(lax.rem(t + i, nt), c), device_id_type=MESH)
    from_low = (c == 0) & (t > 0)
    from_high = (c == nc - 1) & (t < nt - 1)

    @pl.when(from_low)
    def _():
        for g in range(nc):
            pl.semaphore_signal(bar, inc=1, device_id=(t - 1, g), device_id_type=MESH)

    @pl.when(from_high)
    def _():
        for g in range(nc):
            pl.semaphore_signal(bar, inc=1, device_id=(t + 1, g), device_id_type=MESH)

    for load in loads:
        load.wait()

    live = lax.broadcasted_iota(jnp.int32, (1, slots), 1) < cnt[0, 0]
    row = cell_v[0:1]
    bucket = jnp.where(live, row // BUCKET, -1)
    buckets = G // BUCKET
    hot = (lax.broadcasted_iota(jnp.int32, (buckets, slots), 0) == bucket).astype(F32)
    step = 256
    before = (
        lax.broadcasted_iota(jnp.int32, (step, step), 0) < lax.broadcasted_iota(jnp.int32, (step, step), 1)
    ).astype(F32).astype(BF16)
    parts = []
    carry = jnp.zeros((buckets, 1), F32)
    for s in range(0, slots, step):
        piece = hot[:, s : s + step]
        ahead = jnp.dot(piece.astype(BF16), before, preferred_element_type=F32) + carry
        parts.append(jnp.sum(piece * ahead, axis=0, keepdims=True))
        carry = carry + jnp.sum(piece, axis=1, keepdims=True)
    rank = jnp.concatenate(parts, axis=1).astype(jnp.int32)
    over = (jnp.max(carry, axis=0, keepdims=True) > CAP).astype(F32)
    tile_flags[t] = jnp.broadcast_to(over, (1, 128))

    below, above = (t > 0).astype(jnp.int32), (t < nt - 1).astype(jnp.int32)
    pl.semaphore_wait(bar, nc - 1 + nt - 1 + below + above)

    def tile_flag(i, slot):
        return pltpu.make_async_remote_copy(
            src_ref=tile_flags.at[t], dst_ref=tile_flags.at[slot], send_sem=tf_send.at[i], recv_sem=tf_recv.at[slot],
            device_id=(lax.rem(t + i, nt), c), device_id_type=MESH)

    for i in range(1, nt):
        tile_flag(i, t).start()

    group = jnp.where(live, (bucket + 1) * GROUPS_IN + rank // LOW, -1)
    place = rank % LOW
    groups = packed.shape[0]
    to_group = (lax.broadcasted_iota(jnp.int32, (groups, slots), 0) == group).astype(F32).astype(BF16)
    at_place = lax.broadcasted_iota(jnp.int32, (LOW, slots), 0) == place

    def halves(x):
        high = x.astype(BF16).astype(F32)
        return high, x - high

    re_hi, re_lo = halves(vis_v[0:1])
    im_hi, im_lo = halves(vis_v[1:2])
    col_hi, col_lo = halves(cell_v[1:2].astype(F32))
    pieces = [re_hi, im_hi, col_hi, (row % BUCKET).astype(F32), sup_v[...].astype(F32), wpl_v[...].astype(F32),
              jnp.ones((1, slots), F32), jnp.zeros((1, slots), F32), re_lo, im_lo, col_lo, jnp.zeros((1, slots), F32)]
    spread = jnp.concatenate([jnp.where(at_place, x, 0.0).astype(BF16) for x in pieces], axis=0)
    moved = lax.dot_general(to_group, spread, (((1,), (1,)), ((), ())), preferred_element_type=F32)
    packed[:, 0:128] = moved[:, 0:128] + moved[:, 256:384]
    packed[:, 128:256] = moved[:, 128:256]

    width = 4 * GROUPS_IN

    def payload(i, slot):
        peer = lax.rem(c + i, nc)
        return pltpu.make_async_remote_copy(
            src_ref=packed.at[pl.ds(pl.multiple_of(8 * peer, 8), width)], dst_ref=got.at[slot], send_sem=send_sem.at[i],
            recv_sem=recv_sem.at[slot], device_id=(t, peer), device_id_type=MESH)

    order = [8, 7, 9, 6, 10, 5, 11, 4, 12, 3, 13, 2, 14, 1, 15]
    for i in order:
        payload(i, c).start()

    def edge_up():
        return pltpu.make_async_remote_copy(
            src_ref=packed.at[pl.ds(buckets * GROUPS_IN, GROUPS_IN)], dst_ref=edge.at[c, 0:GROUPS_IN], send_sem=edge_send.at[0],
            recv_sem=edge_recv.at[c], device_id=(t + 1, 0), device_id_type=MESH)

    def edge_down():
        return pltpu.make_async_remote_copy(
            src_ref=packed.at[pl.ds(GROUPS_IN, GROUPS_IN)], dst_ref=edge.at[c, 0:GROUPS_IN], send_sem=edge_send.at[1],
            recv_sem=edge_recv.at[c], device_id=(t - 1, nc - 1), device_id_type=MESH)

    @pl.when(t < nt - 1)
    def _():
        edge_up().start()

    @pl.when(t > 0)
    def _():
        edge_down().start()

    got[c] = packed[pl.ds(pl.multiple_of(8 * c, 8), width), :]

    for i in range(1, nt):
        tile_flag(i, lax.rem(t + i, nt)).wait_recv()
    chan_flags[c] = jnp.max(tile_flags[...], axis=0)

    def chan_flag(i, slot):
        return pltpu.make_async_remote_copy(
            src_ref=chan_flags.at[c], dst_ref=chan_flags.at[slot], send_sem=cf_send.at[i], recv_sem=cf_recv.at[slot],
            device_id=(t, lax.rem(c + i, nc)), device_id_type=MESH)

    for i in order:
        chan_flag(i, c).start()

    table[...] = class_table()
    total[...] = jnp.zeros_like(total)

    spot = lax.broadcasted_iota(jnp.int32, (8, 128), 1) // LOW
    lift = BUCKET * (lax.broadcasted_iota(jnp.int32, (width, 128), 0) // GROUPS_IN - 1) - M
    row_lanes = lax.broadcasted_iota(jnp.int32, (width, 128), 1) // LOW == 3

    def fields(source):
        first, second = got[source, :, 0:128], got[source, :, 128:256]
        cells = first.astype(jnp.int32)
        cells = jnp.where(row_lanes, cells + lift, cells - M)
        klass = (second * float(PLANES) + pltpu.roll(second, 3 * LOW, 1)).astype(jnp.int32)

        def lines(x, offset):
            shifted = [pltpu.roll(x, ((b - offset) % 4) * LOW, 1) if (b - offset) % 4 else x for b in range(4)]
            made = []
            for g in range(EARLY):
                parts = [jnp.broadcast_to(shifted[b][GROUPS_IN * b + g : GROUPS_IN * b + g + 1], (8, 128)) for b in range(4)]
                line = parts[0]
                for b in range(1, 4):
                    line = jnp.where(spot == b, parts[b], line)
                made.append(line)
            return made

        return lines(klass, 0), lines(cells, 3), lines(cells, 2), lines(first, 0), lines(first, 1)

    here = 2 * (c // 2)

    def chip(k):
        q = k % 4
        dz = q + jnp.where(q == 2, 1, 0) - jnp.where(q == 3, 1, 0)
        z, y = (here // 2) % 4, here // 8
        return (((y + k // 4) % 2) * 4 + (z + dz) % 4) * 2

    def prepare(source, slot):
        both = [a + b for a, b in zip(fields(source), fields(source + 1))]
        lay(*[jnp.concatenate(x, axis=1) for x in both], table, weights.at[slot], columns.at[slot])

    def arrive(source):
        pltpu.make_async_remote_copy(
            src_ref=packed.at[pl.ds(0, width)], dst_ref=got.at[source], send_sem=send_sem.at[1],
            recv_sem=recv_sem.at[source], device_id=(t, source), device_id_type=MESH).wait_recv()

    arrive(here + (c + 1) % 2)
    prepare(here, 0)

    def two_chips(j, carry):
        for odd in (1, 0):
            source = chip(2 * j + 2 - odd)
            arrive(source)
            arrive(source + 1)
            prepare(source, odd)
            add(total, weights.at[1 - odd], columns.at[1 - odd])
        return carry

    chips = nc // 2
    lax.fori_loop(0, chips // 2 - 1, two_chips, 0)
    source = chip(chips - 1)
    arrive(source)
    arrive(source + 1)
    prepare(source, 1)
    add(total, weights.at[0], columns.at[0])
    add(total, weights.at[1], columns.at[1])

    @pl.when(from_low | from_high)
    def _():
        for g in range(nc):
            pltpu.make_async_remote_copy(
                src_ref=packed.at[pl.ds(0, GROUPS_IN)], dst_ref=edge.at[g, 0:GROUPS_IN], send_sem=edge_send.at[0],
                recv_sem=edge_recv.at[g], device_id=(t, g), device_id_type=MESH).wait_recv()

    for i in range(1, nc):
        chan_flag(i, lax.rem(c + i, nc)).wait_recv()
    flag[0, 0] = (jnp.max(jnp.max(chan_flags[...], axis=0)) > 0.5).astype(jnp.int32)
    for i in range(1, nt):
        tile_flag(i, t).wait_send()
    for i in range(1, nc):
        payload(i, c).wait_send()
        chan_flag(i, c).wait_send()

    @pl.when(t < nt - 1)
    def _():
        edge_up().wait_send()

    @pl.when(t > 0)
    def _():
        edge_down().wait_send()


def owned_rows(got, edge, table, begun, out, real, whole, total, weights, columns):
    c = lax.axis_index("chan")
    nc, per = got.shape[0], got.shape[1]
    main = nc * per
    count = main + nc * 8
    quarter = count // 4

    lanes = lax.broadcasted_iota(jnp.int32, (1, 256), 1) // LOW
    both = jnp.concatenate([got[...].reshape(main, 256), edge[...].reshape(nc * 8, 256)], axis=0)
    index = lax.broadcasted_iota(jnp.int32, (count, 256), 0)
    shift = jnp.where(index < main, BUCKET * ((index % per) // GROUPS_IN - 1), jnp.where(c == 0, -BUCKET, 2 * BUCKET))
    both = both + jnp.where(lanes == 3, shift, 0).astype(F32)
    used = jnp.where(lax.broadcasted_iota(jnp.int32, (128, count), 0) == 6 * LOW - 128, both[:, 128:256].T, 0.0)
    used = jnp.sum(used, axis=0, keepdims=True)
    at = lax.broadcasted_iota(jnp.int32, (1, count), 1)
    used = jnp.where((at < main) & (at % GROUPS_IN < EARLY), 0.0, used)
    before = (
        lax.broadcasted_iota(jnp.int32, (count, count), 0) < lax.broadcasted_iota(jnp.int32, (count, count), 1)
    ).astype(F32).astype(BF16)
    rank = jnp.dot(jnp.broadcast_to(used, (8, count)).astype(BF16), before, preferred_element_type=F32)[0:1]
    rank = jnp.where(used > 0.5, rank, -1.0)
    place = lax.broadcasted_iota(jnp.int32, (count, count), 0)
    place = (4 * (place % quarter) + place // quarter).astype(F32)
    pick = jnp.where(place == rank, 1.0, 0.0).astype(BF16)
    high = both.astype(BF16)
    low = (both - high.astype(F32)).astype(BF16)
    rows = jnp.dot(pick, high, preferred_element_type=F32) + jnp.dot(pick, low, preferred_element_type=F32)
    spot = lax.broadcasted_iota(jnp.int32, (quarter, 128), 1) // LOW

    def field(f):
        part, offset = divmod(f, 4)
        result = None
        for s in range(4):
            x = rows[s * quarter : (s + 1) * quarter, 128 * part : 128 * part + 128]
            if (s - offset) % 4:
                x = pltpu.roll(x, ((s - offset) % 4) * LOW, 1)
            result = x if result is None else jnp.where(spot == s, x, result)
        return result

    real[0], real[1] = field(0), field(1)
    whole[0], whole[1] = field(2).astype(jnp.int32) - M, field(3).astype(jnp.int32) - M
    whole[2] = (field(4) * float(PLANES) + field(5)).astype(jnp.int32)
    size = weights.shape[-1]
    lines = size // 128
    chunks = (jnp.sum(used).astype(jnp.int32) + 4 * lines - 1) // (4 * lines)

    total[...] = begun[...]

    def fill(i, slot):
        def line(ref, f):
            return jnp.concatenate(
                [jnp.broadcast_to(ref[f, pl.ds(lines * i + h, 1), :], (8, 128)) for h in range(lines)], axis=1)

        lay(line(whole, 2), line(whole, 1), line(whole, 0), line(real, 0), line(real, 1), table,
            weights.at[slot], columns.at[slot])

    fill(0, 0)

    def body(j, carry):
        fill(2 * j + 1, 1)
        add(total, weights.at[0], columns.at[0])
        fill(2 * j + 2, 0)
        add(total, weights.at[1], columns.at[1])
        return carry

    lax.fori_loop(0, (chunks + 1) // 2, body, 0)
    out[:, 0, :] = total[0:64]
    out[:, 1, :] = total[64:128]


def per_device(visibilities, cell_offsets, support_index, w_plane, live_counts):
    nt, nc = lax.axis_size("tile"), lax.axis_size("chan")
    slots = visibilities.shape[-1]
    groups = (G // BUCKET + 2) * GROUPS_IN
    vmem = pl.BlockSpec(memory_space=pltpu.VMEM)
    got, edge, table, begun, flag = pl.pallas_call(
        exchange,
        out_shape=(
            jax.ShapeDtypeStruct((nc, 4 * GROUPS_IN, FIELDS * LOW), F32),
            jax.ShapeDtypeStruct((nc, 8, FIELDS * LOW), F32),
            jax.ShapeDtypeStruct((2 * M, 4 * PLANES), BF16),
            jax.ShapeDtypeStruct((2 * G // nc, G), F32),
            jax.ShapeDtypeStruct((1, 1), jnp.int32),
        ),
        in_specs=[pl.BlockSpec(memory_space=pl.ANY)] * 4 + [pl.BlockSpec(memory_space=pltpu.SMEM)],
        out_specs=(vmem, vmem, vmem, vmem, pl.BlockSpec(memory_space=pltpu.SMEM)),
        scratch_shapes=[
            pltpu.VMEM((2, slots), F32),
            pltpu.VMEM((2, slots), jnp.int32),
            pltpu.VMEM((1, slots), jnp.int32),
            pltpu.VMEM((1, slots), jnp.int32),
            pltpu.VMEM((groups, FIELDS * LOW), F32),
            pltpu.VMEM((nt, 1, 128), F32),
            pltpu.VMEM((nc, 1, 128), F32),
            pltpu.VMEM((2, 2 * G // nc, 512), BF16),
            pltpu.VMEM((2, G, 512), BF16),
            pltpu.SemaphoreType.DMA((4,)),
            pltpu.SemaphoreType.DMA((nc,)),
            pltpu.SemaphoreType.DMA((nc,)),
            pltpu.SemaphoreType.DMA((2,)),
            pltpu.SemaphoreType.DMA((nc,)),
            pltpu.SemaphoreType.DMA((nt,)),
            pltpu.SemaphoreType.DMA((nt,)),
            pltpu.SemaphoreType.DMA((nc,)),
            pltpu.SemaphoreType.DMA((nc,)),
        ],
        compiler_params=pltpu.CompilerParams(collective_id=0, has_side_effects=True, vmem_limit_bytes=62 << 20),
    )(visibilities, cell_offsets, support_index, w_plane, live_counts)

    groups_got = nc * (4 * GROUPS_IN + 8)

    def usual(*_):
        return pl.pallas_call(
            owned_rows,
            out_shape=jax.ShapeDtypeStruct((G // nc, 2, G), F32),
            in_specs=[vmem] * 4,
            out_specs=vmem,
            scratch_shapes=[
                pltpu.VMEM((2, groups_got // 4, 128), F32),
                pltpu.VMEM((3, groups_got // 4, 128), jnp.int32),
                pltpu.VMEM((2 * G // nc, G), F32),
                pltpu.VMEM((2, 2 * G // nc, 512), BF16),
                pltpu.VMEM((2, G, 512), BF16),
            ],
            compiler_params=pltpu.CompilerParams(vmem_limit_bytes=40 << 20),
        )(got, edge, table, begun)

    return lax.cond(
        flag[0, 0] > 0, any_cells, usual, visibilities, cell_offsets, support_index, w_plane, live_counts
    )


def solution(mesh):
    in_specs = (
        P("tile", "chan", None, None),
        P("tile", "chan", None, None),
        P("tile", "chan", None),
        P("tile", "chan", None),
        P("tile", "chan"),
    )
    out_specs = P(("tile", "chan"), None, None)
    return jax.shard_map(
        per_device, mesh=mesh, in_specs=in_specs, out_specs=out_specs, check_vma=False
    )
```

```python
import functools
import math

import jax
import jax.numpy as jnp
from jax import lax
from jax.experimental import pallas as pl
from jax.experimental.pallas import tpu as pltpu
from jax.sharding import PartitionSpec as P

G = 1024
M = 32
PLANES = 16
BETA = 7.0

BUCKET = 32
CAP = 128
LOW = 32
GROUPS_IN = CAP // LOW
EARLY = (0, GROUPS_IN - 1)
SPAN = 9
FIELDS = 8
MESH = pl.DeviceIdType.MESH
F32 = jnp.float32
BF16 = jnp.bfloat16


def bessel_zero(value):
    quarter = value * value * 0.25
    term = jnp.ones_like(value)
    total = jnp.ones_like(value)
    for index in range(1, 30):
        term = term * quarter * (1.0 / float(index * index))
        total = total + term
    return total


def kernel_values(distance, half_width, w_coef):
    ratio = distance / half_width
    inside = jnp.abs(ratio) < 1.0
    radius = jnp.sqrt(jnp.maximum(1.0 - ratio * ratio, 0.0))
    bessel = bessel_zero(BETA * radius) / bessel_zero(jnp.float32(BETA))
    taper = jnp.cos(jnp.pi * w_coef * ratio * ratio)
    return jnp.where(inside, bessel * taper, jnp.float32(0.0))


def flatten_groups(vis_block, offset_block, support_block, plane_block, count_block):
    slot_total = vis_block.shape[-1]
    slot_ids = jnp.arange(slot_total, dtype=jnp.int32)
    live = (slot_ids[None, :] < count_block[:, None]).astype(jnp.float32).reshape(-1)
    real_part = vis_block[:, 0].reshape(-1) * live
    imag_part = vis_block[:, 1].reshape(-1) * live
    row_cell = offset_block[:, 0].reshape(-1).astype(jnp.float32)
    col_cell = offset_block[:, 1].reshape(-1).astype(jnp.float32)
    half_width = 8.0 * (support_block.reshape(-1) + 1).astype(jnp.float32)
    w_coef = 0.5 * (plane_block.reshape(-1) + 1).astype(jnp.float32) / PLANES
    return (real_part, imag_part, row_cell, col_cell, half_width, w_coef)


def grid_part(flat, row_start, row_count, width):
    total_vis = flat[0].shape[0]
    block_len = math.gcd(total_vis, 512)
    stacked = tuple((item.reshape(total_vis // block_len, block_len) for item in flat))
    row_pos = (row_start + jnp.arange(row_count, dtype=jnp.int32)).astype(jnp.float32)
    col_pos = jnp.arange(width, dtype=jnp.int32).astype(jnp.float32)

    def step_block(total, values):
        real_part, imag_part, row_cell, col_cell, half_width, w_coef = values
        row_weights = kernel_values(
            row_pos[None, :] - row_cell[:, None], half_width[:, None], w_coef[:, None]
        ).astype(jnp.bfloat16)
        col_kern = kernel_values(
            col_pos[None, :] - col_cell[:, None], half_width[:, None], w_coef[:, None]
        )
        col_weights = jnp.concatenate(
            [real_part[:, None] * col_kern, imag_part[:, None] * col_kern], axis=1
        ).astype(jnp.bfloat16)
        product = lax.dot_general(
            row_weights, col_weights, (((0,), (0,)), ((), ())), preferred_element_type=jnp.float32
        )
        return (total + product, None)

    start_total = jnp.zeros((row_count, 2 * width), jnp.float32)
    total, _ = lax.scan(step_block, start_total, stacked)
    return total.reshape(row_count, 2, width)


def any_cells(visibilities, cell_offsets, support_index, w_plane, live_counts):
    tiles, parts = lax.axis_size("tile"), lax.axis_size("chan")
    share = G // parts
    first_row = lax.axis_index("chan") * share - M
    held = jnp.stack(
        flatten_groups(visibilities[0], cell_offsets[0], support_index[0], w_plane[0], live_counts[0])
    )

    def step(_, carry):
        total, held = carry
        total = total + grid_part(held, first_row, share + 2 * M, G)
        return total, lax.ppermute(held, "chan", [(i, (i + 1) % parts) for i in range(parts)])

    total, _ = lax.fori_loop(0, parts, step, (jnp.zeros((share + 2 * M, 2, G), F32), held))
    last = parts - 1
    left_in = lax.ppermute(
        total[share + M :], ("tile", "chan"), [(t * parts + last, (t + 1) * parts) for t in range(tiles - 1)]
    )
    right_in = lax.ppermute(
        total[:M], ("tile", "chan"), [(t * parts, (t - 1) * parts + last) for t in range(1, tiles)]
    )
    owned = total[M : M + share]
    return owned.at[:M].add(left_in).at[share - M :].add(right_in)


def class_table():
    shape = (2 * M, 4 * PLANES)
    klass = lax.broadcasted_iota(jnp.int32, shape, 1)
    distance = jnp.abs(lax.broadcasted_iota(jnp.int32, shape, 0) - M).astype(F32)
    half = (8 * (klass // PLANES + 1)).astype(F32)
    w_coef = 0.5 * (klass % PLANES + 1).astype(F32) / PLANES
    ratio = jnp.minimum(distance / half, 1.0)
    square = ratio * ratio
    radius = jnp.sqrt(jnp.maximum(1.0 - square, 0.0))
    bessel = bessel_zero(BETA * radius) / bessel_zero(jnp.full(shape, BETA, F32))
    taper = jnp.cos(jnp.pi * w_coef * square)
    return jnp.where(ratio < 1.0, bessel * taper, 0.0).astype(BF16)


def turned(values, by, sub):
    for bit in (32, 16, 8):
        chosen = (by & bit) != 0
        values = [jnp.where(chosen, values[(k - bit // 8) % 8], values[k]) for k in range(8)]
    for bit in (4, 2, 1):
        chosen = (by & bit) != 0
        rolled = [pltpu.roll(x, bit, 0) for x in values]
        values = [
            jnp.where(chosen, jnp.where(sub < bit, rolled[(k - 1) % 8], rolled[k]), values[k]) for k in range(8)
        ]
    return values


def lay(klass, row, col, re, im, table, weights, columns, start=0):
    sub = lax.broadcasted_iota(jnp.int32, klass.shape, 0)
    hot = jnp.concatenate([(klass == sub + 8 * k).astype(F32) for k in range(8)], axis=0).astype(BF16)
    values = jnp.dot(table[...], hot, preferred_element_type=F32)
    values = [values[8 * k : 8 * k + 8] for k in range(8)]
    by, first = row & 63, row >> 6
    mine = [
        jnp.where(jnp.where(sub + 8 * k < by, first + 1, first) == 0, x, 0.0)
        for k, x in enumerate(turned(values, by, sub))
    ]
    weights[0:64] = jnp.concatenate([x * re for x in mine], axis=0).astype(BF16)
    weights[64:128] = jnp.concatenate([x * im for x in mine], axis=0).astype(BF16)
    by, first = col & 63, col >> 6
    window = jnp.concatenate(turned(values, by, sub), axis=0).astype(BF16)
    block = jnp.concatenate(
        [jnp.where(sub + 8 * k < by, first + 1, first).astype(F32) for k in range(8)], axis=0).astype(BF16)
    for b in range(columns.shape[0] // 64):
        columns[64 * b : 64 * b + 64] = jnp.where(block == jnp.asarray(start + b, BF16), window, jnp.asarray(0, BF16))


def add(total, weights, columns, start=0):
    stop = 64 * start + columns.shape[0]
    total[64 * start : stop] += lax.dot_general(
        columns[...], weights[...], (((1,), (1,)), ((), ())), preferred_element_type=F32)


def exchange(vis, cell, sup, wpl, cnt, got, edge, table, total, flag, vis_v, cell_v, sup_v, wpl_v, packed, tile_flags, chan_flags,
             weights, columns,
             load_sem, send_sem, recv_sem, edge_send, edge_recv, tf_send, tf_recv, cf_send, cf_recv):
    t, c = lax.axis_index("tile"), lax.axis_index("chan")
    nt, nc = lax.axis_size("tile"), lax.axis_size("chan")
    slots = vis_v.shape[-1]
    loads = [
        pltpu.make_async_copy(vis.at[0, 0], vis_v, load_sem.at[0]),
        pltpu.make_async_copy(cell.at[0, 0], cell_v, load_sem.at[1]),
        pltpu.make_async_copy(sup.at[0], sup_v, load_sem.at[2]),
        pltpu.make_async_copy(wpl.at[0], wpl_v, load_sem.at[3]),
    ]
    for load in loads:
        load.start()
    edge[...] = jnp.zeros_like(edge)

    bar = pltpu.get_barrier_semaphore()
    for i in range(1, nc):
        pl.semaphore_signal(bar, inc=1, device_id=(t, lax.rem(c + i, nc)), device_id_type=MESH)
    for i in range(1, nt):
        pl.semaphore_signal(bar, inc=1, device_id=(lax.rem(t + i, nt), c), device_id_type=MESH)
    from_low = (c == 0) & (t > 0)
    from_high = (c == nc - 1) & (t < nt - 1)

    @pl.when(from_low)
    def _():
        for g in range(nc):
            pl.semaphore_signal(bar, inc=1, device_id=(t - 1, g), device_id_type=MESH)

    @pl.when(from_high)
    def _():
        for g in range(nc):
            pl.semaphore_signal(bar, inc=1, device_id=(t + 1, g), device_id_type=MESH)

    for load in loads:
        load.wait()

    live = lax.broadcasted_iota(jnp.int32, (1, slots), 1) < cnt[0, 0]
    row = cell_v[0:1]
    buckets = G // BUCKET
    bucket = row // BUCKET
    right = cell_v[1:2] >= G // 2
    side = jnp.where(live, bucket + jnp.where(right, buckets, 0), -1)
    hot = (lax.broadcasted_iota(jnp.int32, (2 * buckets, slots), 0) == side).astype(F32)
    step = 256
    before = (
        lax.broadcasted_iota(jnp.int32, (step, step), 0) < lax.broadcasted_iota(jnp.int32, (step, step), 1)
    ).astype(F32).astype(BF16)
    parts = []
    carry = jnp.zeros((2 * buckets, 1), F32)
    for s in range(0, slots, step):
        piece = hot[:, s : s + step]
        ahead = jnp.dot(piece.astype(BF16), before, preferred_element_type=F32) + carry
        parts.append(jnp.sum(piece * ahead, axis=0, keepdims=True))
        carry = carry + jnp.sum(piece, axis=1, keepdims=True)
    rank = jnp.concatenate(parts, axis=1).astype(jnp.int32)
    full = jnp.max(carry[:buckets] + carry[buckets:], axis=0, keepdims=True) > CAP
    full = full | (jnp.max(carry, axis=0, keepdims=True) > CAP - LOW)
    over = full.astype(F32)
    tile_flags[t] = jnp.broadcast_to(over, (1, 128))

    below, above = (t > 0).astype(jnp.int32), (t < nt - 1).astype(jnp.int32)
    pl.semaphore_wait(bar, nc - 1 + nt - 1 + below + above)

    def tile_flag(i, slot):
        return pltpu.make_async_remote_copy(
            src_ref=tile_flags.at[t], dst_ref=tile_flags.at[slot], send_sem=tf_send.at[i], recv_sem=tf_recv.at[slot],
            device_id=(lax.rem(t + i, nt), c), device_id_type=MESH)

    for i in range(1, nt):
        tile_flag(i, t).start()

    spot = jnp.where(right, CAP - 1 - rank, rank)
    group = jnp.where(live, (bucket + 1) * GROUPS_IN + (spot >> (LOW.bit_length() - 1)), -1)
    place = spot & (LOW - 1)
    groups = packed.shape[0]
    to_group = (lax.broadcasted_iota(jnp.int32, (groups, slots), 0) == group).astype(F32).astype(BF16)
    at_place = lax.broadcasted_iota(jnp.int32, (LOW, slots), 0) == place

    def halves(x):
        high = x.astype(BF16).astype(F32)
        return high, x - high

    re_hi, re_lo = halves(vis_v[0:1])
    im_hi, im_lo = halves(vis_v[1:2])
    col_hi, col_lo = halves(cell_v[1:2].astype(F32))
    pieces = [re_hi, im_hi, col_hi, (row % BUCKET).astype(F32), sup_v[...].astype(F32), wpl_v[...].astype(F32),
              jnp.ones((1, slots), F32), jnp.zeros((1, slots), F32), re_lo, im_lo, col_lo, jnp.zeros((1, slots), F32)]
    spread = jnp.concatenate([jnp.where(at_place, x, 0.0).astype(BF16) for x in pieces], axis=0)
    moved = lax.dot_general(to_group, spread, (((1,), (1,)), ((), ())), preferred_element_type=F32)
    packed[:, 0:128] = moved[:, 0:128] + moved[:, 256:384]
    packed[:, 128:256] = moved[:, 128:256]

    width = 4 * GROUPS_IN

    def payload(i, slot):
        peer = lax.rem(c + i, nc)
        return pltpu.make_async_remote_copy(
            src_ref=packed.at[pl.ds(pl.multiple_of(8 * peer, 8), width)], dst_ref=got.at[slot], send_sem=send_sem.at[i],
            recv_sem=recv_sem.at[slot], device_id=(t, peer), device_id_type=MESH)

    order = [8, 7, 9, 6, 10, 5, 11, 4, 12, 3, 13, 2, 14, 1, 15]
    for i in order:
        payload(i, c).start()

    def edge_up():
        return pltpu.make_async_remote_copy(
            src_ref=packed.at[pl.ds(buckets * GROUPS_IN, GROUPS_IN)], dst_ref=edge.at[c, 0:GROUPS_IN], send_sem=edge_send.at[0],
            recv_sem=edge_recv.at[c], device_id=(t + 1, 0), device_id_type=MESH)

    def edge_down():
        return pltpu.make_async_remote_copy(
            src_ref=packed.at[pl.ds(GROUPS_IN, GROUPS_IN)], dst_ref=edge.at[c, 0:GROUPS_IN], send_sem=edge_send.at[1],
            recv_sem=edge_recv.at[c], device_id=(t - 1, nc - 1), device_id_type=MESH)

    @pl.when(t < nt - 1)
    def _():
        edge_up().start()

    @pl.when(t > 0)
    def _():
        edge_down().start()

    got[c] = packed[pl.ds(pl.multiple_of(8 * c, 8), width), :]

    for i in range(1, nt):
        tile_flag(i, lax.rem(t + i, nt)).wait_recv()
    chan_flags[c] = jnp.max(tile_flags[...], axis=0)

    def chan_flag(i, slot):
        return pltpu.make_async_remote_copy(
            src_ref=chan_flags.at[c], dst_ref=chan_flags.at[slot], send_sem=cf_send.at[i], recv_sem=cf_recv.at[slot],
            device_id=(t, lax.rem(c + i, nc)), device_id_type=MESH)

    for i in order:
        chan_flag(i, c).start()

    table[...] = class_table()
    total[...] = jnp.zeros_like(total)

    spot = lax.broadcasted_iota(jnp.int32, (8, 128), 1) // LOW

    def fields(first, second, lift, picks):
        row_lanes = lax.broadcasted_iota(jnp.int32, first.shape, 1) // LOW == 3
        cells = first.astype(jnp.int32) - M
        cells = jnp.where(row_lanes, cells + lift, cells)
        klass = (second * float(PLANES) + pltpu.roll(second, 3 * LOW, 1)).astype(jnp.int32)

        def lines(x, offset):
            shifted = [pltpu.roll(x, ((b - offset) % 4) * LOW, 1) if (b - offset) % 4 else x for b in range(4)]
            made = []
            for pick in picks:
                parts = [jnp.broadcast_to(shifted[b][r : r + 1], (8, 128)) for b, r in enumerate(pick)]
                line = parts[0]
                for b in range(1, 4):
                    line = jnp.where(spot == b, parts[b], line)
                made.append(line)
            return made

        return lines(klass, 0), lines(cells, 3), lines(cells, 2), lines(first, 0), lines(first, 1)

    halves_at = (0, G // 64 - SPAN)
    lift = BUCKET * (lax.broadcasted_iota(jnp.int32, (width, 128), 0) // GROUPS_IN - 1)

    here = 2 * (c // 2)

    def chip(k):
        q = k % 4
        dz = q + jnp.where(q == 2, 1, 0) - jnp.where(q == 3, 1, 0)
        z, y = (here // 2) % 4, here // 8
        return (((y + k // 4) % 2) * 4 + (z + dz) % 4) * 2

    def prepare(source, slot):
        made = [
            fields(got[x, :, 0:128], got[x, :, 128:256], lift, [[GROUPS_IN * b + g for b in range(4)] for g in EARLY])
            for x in (source, source + 1)
        ]
        for h in range(2):
            lay(*[jnp.concatenate([x[h], y[h]], axis=1) for x, y in zip(*made)], table, weights.at[slot, h],
                columns.at[slot, h], halves_at[h])

    def add_both(slot):
        for h in range(2):
            add(total, weights.at[slot, h], columns.at[slot, h], halves_at[h])

    def arrive(source):
        pltpu.make_async_remote_copy(
            src_ref=packed.at[pl.ds(0, width)], dst_ref=got.at[source], send_sem=send_sem.at[1],
            recv_sem=recv_sem.at[source], device_id=(t, source), device_id_type=MESH).wait_recv()

    arrive(here + (c + 1) % 2)
    prepare(here, 0)

    def two_chips(j, carry):
        for odd in (1, 0):
            source = chip(2 * j + 2 - odd)
            arrive(source)
            arrive(source + 1)
            prepare(source, odd)
            add_both(1 - odd)
        return carry

    chips = nc // 2
    lax.fori_loop(0, chips // 2 - 1, two_chips, 0)
    source = chip(chips - 1)
    arrive(source)
    arrive(source + 1)
    prepare(source, 1)
    add_both(0)
    add_both(1)

    @pl.when(from_low | from_high)
    def _():
        for g in range(nc):
            pltpu.make_async_remote_copy(
                src_ref=packed.at[pl.ds(0, GROUPS_IN)], dst_ref=edge.at[g, 0:GROUPS_IN], send_sem=edge_send.at[0],
                recv_sem=edge_recv.at[g], device_id=(t, g), device_id_type=MESH).wait_recv()
        rows = edge[...].reshape(nc * 8, 256)
        lines = nc // 4
        picks = [[8 * (4 * n + b) + g for b in range(4)] for g in EARLY for n in range(lines)]
        made = fields(rows[:, 0:128], rows[:, 128:256], jnp.where(from_low, -BUCKET, 2 * BUCKET), picks)
        for h in range(2):
            for n in range(0, lines, 2):
                lay(*[jnp.concatenate(x[h * lines + n : h * lines + n + 2], axis=1) for x in made], table,
                    weights.at[n // 2, h], columns.at[n // 2, h], halves_at[h])
        for n in range(lines // 2):
            add_both(n)

    for i in range(1, nc):
        chan_flag(i, lax.rem(c + i, nc)).wait_recv()
    flag[0, 0] = (jnp.max(jnp.max(chan_flags[...], axis=0)) > 0.5).astype(jnp.int32)
    for i in range(1, nt):
        tile_flag(i, t).wait_send()
    for i in range(1, nc):
        payload(i, c).wait_send()
        chan_flag(i, c).wait_send()

    @pl.when(t < nt - 1)
    def _():
        edge_up().wait_send()

    @pl.when(t > 0)
    def _():
        edge_down().wait_send()


def owned_rows(got, edge, table, begun, out, real, whole, total, weights, columns):
    c = lax.axis_index("chan")
    nc, per = got.shape[0], got.shape[1]
    main = nc * per
    count = main + nc * 8
    left = nc * (per // GROUPS_IN + 1) * (GROUPS_IN - len(EARLY))
    quarter = left // 4

    lanes = lax.broadcasted_iota(jnp.int32, (1, 256), 1) // LOW
    both = jnp.concatenate([got[...].reshape(main, 256), edge[...].reshape(nc * 8, 256)], axis=0)
    index = lax.broadcasted_iota(jnp.int32, (count, 256), 0)
    shift = jnp.where(index < main, BUCKET * ((index % per) // GROUPS_IN - 1), jnp.where(c == 0, -BUCKET, 2 * BUCKET))
    both = both + jnp.where(lanes == 3, shift, 0).astype(F32)
    used = jnp.max(both[:, 128:256].T[2 * LOW : 3 * LOW], axis=0, keepdims=True)
    at = lax.broadcasted_iota(jnp.int32, (1, count), 1) % GROUPS_IN
    used = jnp.where((at == EARLY[0]) | (at == EARLY[1]), 0.0, used)
    before = (
        lax.broadcasted_iota(jnp.int32, (count, count), 0) < lax.broadcasted_iota(jnp.int32, (count, count), 1)
    ).astype(F32).astype(BF16)
    rank = jnp.dot(jnp.broadcast_to(used, (8, count)).astype(BF16), before, preferred_element_type=F32)[0:1]
    rank = jnp.where(used > 0.5, rank, -1.0)
    place = lax.broadcasted_iota(jnp.int32, (left, count), 0)
    place = (4 * (place % quarter) + place // quarter).astype(F32)
    pick = jnp.where(place == rank, 1.0, 0.0).astype(BF16)
    high = both.astype(BF16)
    low = (both - high.astype(F32)).astype(BF16)
    rows = jnp.dot(pick, high, preferred_element_type=F32) + jnp.dot(pick, low, preferred_element_type=F32)
    spot = lax.broadcasted_iota(jnp.int32, (quarter, 128), 1) // LOW

    def field(f):
        part, offset = divmod(f, 4)
        result = None
        for s in range(4):
            x = rows[s * quarter : (s + 1) * quarter, 128 * part : 128 * part + 128]
            if (s - offset) % 4:
                x = pltpu.roll(x, ((s - offset) % 4) * LOW, 1)
            result = x if result is None else jnp.where(spot == s, x, result)
        return result

    real[0], real[1] = field(0), field(1)
    whole[0], whole[1] = field(2).astype(jnp.int32) - M, field(3).astype(jnp.int32) - M
    whole[2] = (field(4) * float(PLANES) + field(5)).astype(jnp.int32)
    size = weights.shape[-1]
    lines = size // 128
    chunks = (jnp.sum(used).astype(jnp.int32) + 4 * lines - 1) // (4 * lines)

    total[...] = begun[...]

    def body(i, carry):
        def line(ref, f):
            return jnp.concatenate(
                [jnp.broadcast_to(ref[f, pl.ds(lines * i + h, 1), :], (8, 128)) for h in range(lines)], axis=1)

        lay(line(whole, 2), line(whole, 1), line(whole, 0), line(real, 0), line(real, 1), table, weights, columns)
        add(total, weights, columns)
        return carry

    lax.fori_loop(0, chunks, body, 0)
    rows = total[...].T
    out[:, 0, :] = rows[0:64]
    out[:, 1, :] = rows[64:128]


def per_device(visibilities, cell_offsets, support_index, w_plane, live_counts):
    nt, nc = lax.axis_size("tile"), lax.axis_size("chan")
    slots = visibilities.shape[-1]
    groups = (G // BUCKET + 2) * GROUPS_IN
    vmem = pl.BlockSpec(memory_space=pltpu.VMEM)
    got, edge, table, begun, flag = pl.pallas_call(
        exchange,
        out_shape=(
            jax.ShapeDtypeStruct((nc, 4 * GROUPS_IN, FIELDS * LOW), F32),
            jax.ShapeDtypeStruct((nc, 8, FIELDS * LOW), F32),
            jax.ShapeDtypeStruct((2 * M, 4 * PLANES), BF16),
            jax.ShapeDtypeStruct((G, 2 * G // nc), F32),
            jax.ShapeDtypeStruct((1, 1), jnp.int32),
        ),
        in_specs=[pl.BlockSpec(memory_space=pl.ANY)] * 4 + [pl.BlockSpec(memory_space=pltpu.SMEM)],
        out_specs=(vmem, vmem, vmem, vmem, pl.BlockSpec(memory_space=pltpu.SMEM)),
        scratch_shapes=[
            pltpu.VMEM((2, slots), F32),
            pltpu.VMEM((2, slots), jnp.int32),
            pltpu.VMEM((1, slots), jnp.int32),
            pltpu.VMEM((1, slots), jnp.int32),
            pltpu.VMEM((groups, FIELDS * LOW), F32),
            pltpu.VMEM((nt, 1, 128), F32),
            pltpu.VMEM((nc, 1, 128), F32),
            pltpu.VMEM((2, 2, 2 * G // nc, 256), BF16),
            pltpu.VMEM((2, 2, 64 * SPAN, 256), BF16),
            pltpu.SemaphoreType.DMA((4,)),
            pltpu.SemaphoreType.DMA((nc,)),
            pltpu.SemaphoreType.DMA((nc,)),
            pltpu.SemaphoreType.DMA((2,)),
            pltpu.SemaphoreType.DMA((nc,)),
            pltpu.SemaphoreType.DMA((nt,)),
            pltpu.SemaphoreType.DMA((nt,)),
            pltpu.SemaphoreType.DMA((nc,)),
            pltpu.SemaphoreType.DMA((nc,)),
        ],
        compiler_params=pltpu.CompilerParams(collective_id=0, has_side_effects=True, vmem_limit_bytes=62 << 20),
    )(visibilities, cell_offsets, support_index, w_plane, live_counts)

    groups_left = nc * 5 * (GROUPS_IN - len(EARLY))

    def usual(*_):
        return pl.pallas_call(
            owned_rows,
            out_shape=jax.ShapeDtypeStruct((G // nc, 2, G), F32),
            in_specs=[vmem] * 4,
            out_specs=vmem,
            scratch_shapes=[
                pltpu.VMEM((2, groups_left // 4, 128), F32),
                pltpu.VMEM((3, groups_left // 4, 128), jnp.int32),
                pltpu.VMEM((G, 2 * G // nc), F32),
                pltpu.VMEM((2 * G // nc, 512), BF16),
                pltpu.VMEM((G, 512), BF16),
            ],
            compiler_params=pltpu.CompilerParams(vmem_limit_bytes=40 << 20),
        )(got, edge, table, begun)

    return lax.cond(
        flag[0, 0] > 0, any_cells, usual, visibilities, cell_offsets, support_index, w_plane, live_counts
    )


def solution(mesh):
    in_specs = (
        P("tile", "chan", None, None),
        P("tile", "chan", None, None),
        P("tile", "chan", None),
        P("tile", "chan", None),
        P("tile", "chan"),
    )
    out_specs = P(("tile", "chan"), None, None)
    return jax.shard_map(
        per_device, mesh=mesh, in_specs=in_specs, out_specs=out_specs, check_vma=False
    )
```

```python
import functools
import math

import jax
import jax.numpy as jnp
from jax import lax
from jax.experimental import pallas as pl
from jax.experimental.pallas import tpu as pltpu
from jax.sharding import PartitionSpec as P

G = 1024
M = 32
PLANES = 16
BETA = 7.0

BUCKET = 32
CAP = 128
LOW = 32
GROUPS_IN = CAP // LOW
EARLY = (0, GROUPS_IN - 1)
SPAN = 9
FIELDS = 8
MESH = pl.DeviceIdType.MESH
F32 = jnp.float32
BF16 = jnp.bfloat16


def bessel_zero(value):
    quarter = value * value * 0.25
    term = jnp.ones_like(value)
    total = jnp.ones_like(value)
    for index in range(1, 30):
        term = term * quarter * (1.0 / float(index * index))
        total = total + term
    return total


def kernel_values(distance, half_width, w_coef):
    ratio = distance / half_width
    inside = jnp.abs(ratio) < 1.0
    radius = jnp.sqrt(jnp.maximum(1.0 - ratio * ratio, 0.0))
    bessel = bessel_zero(BETA * radius) / bessel_zero(jnp.float32(BETA))
    taper = jnp.cos(jnp.pi * w_coef * ratio * ratio)
    return jnp.where(inside, bessel * taper, jnp.float32(0.0))


def flatten_groups(vis_block, offset_block, support_block, plane_block, count_block):
    slot_total = vis_block.shape[-1]
    slot_ids = jnp.arange(slot_total, dtype=jnp.int32)
    live = (slot_ids[None, :] < count_block[:, None]).astype(jnp.float32).reshape(-1)
    real_part = vis_block[:, 0].reshape(-1) * live
    imag_part = vis_block[:, 1].reshape(-1) * live
    row_cell = offset_block[:, 0].reshape(-1).astype(jnp.float32)
    col_cell = offset_block[:, 1].reshape(-1).astype(jnp.float32)
    half_width = 8.0 * (support_block.reshape(-1) + 1).astype(jnp.float32)
    w_coef = 0.5 * (plane_block.reshape(-1) + 1).astype(jnp.float32) / PLANES
    return (real_part, imag_part, row_cell, col_cell, half_width, w_coef)


def grid_part(flat, row_start, row_count, width):
    total_vis = flat[0].shape[0]
    block_len = math.gcd(total_vis, 512)
    stacked = tuple((item.reshape(total_vis // block_len, block_len) for item in flat))
    row_pos = (row_start + jnp.arange(row_count, dtype=jnp.int32)).astype(jnp.float32)
    col_pos = jnp.arange(width, dtype=jnp.int32).astype(jnp.float32)

    def step_block(total, values):
        real_part, imag_part, row_cell, col_cell, half_width, w_coef = values
        row_weights = kernel_values(
            row_pos[None, :] - row_cell[:, None], half_width[:, None], w_coef[:, None]
        ).astype(jnp.bfloat16)
        col_kern = kernel_values(
            col_pos[None, :] - col_cell[:, None], half_width[:, None], w_coef[:, None]
        )
        col_weights = jnp.concatenate(
            [real_part[:, None] * col_kern, imag_part[:, None] * col_kern], axis=1
        ).astype(jnp.bfloat16)
        product = lax.dot_general(
            row_weights, col_weights, (((0,), (0,)), ((), ())), preferred_element_type=jnp.float32
        )
        return (total + product, None)

    start_total = jnp.zeros((row_count, 2 * width), jnp.float32)
    total, _ = lax.scan(step_block, start_total, stacked)
    return total.reshape(row_count, 2, width)


def any_cells(visibilities, cell_offsets, support_index, w_plane, live_counts):
    tiles, parts = lax.axis_size("tile"), lax.axis_size("chan")
    share = G // parts
    first_row = lax.axis_index("chan") * share - M
    held = jnp.stack(
        flatten_groups(visibilities[0], cell_offsets[0], support_index[0], w_plane[0], live_counts[0])
    )

    def step(_, carry):
        total, held = carry
        total = total + grid_part(held, first_row, share + 2 * M, G)
        return total, lax.ppermute(held, "chan", [(i, (i + 1) % parts) for i in range(parts)])

    total, _ = lax.fori_loop(0, parts, step, (jnp.zeros((share + 2 * M, 2, G), F32), held))
    last = parts - 1
    left_in = lax.ppermute(
        total[share + M :], ("tile", "chan"), [(t * parts + last, (t + 1) * parts) for t in range(tiles - 1)]
    )
    right_in = lax.ppermute(
        total[:M], ("tile", "chan"), [(t * parts, (t - 1) * parts + last) for t in range(1, tiles)]
    )
    owned = total[M : M + share]
    return owned.at[:M].add(left_in).at[share - M :].add(right_in)


def class_table():
    shape = (2 * M, 4 * PLANES)
    klass = lax.broadcasted_iota(jnp.int32, shape, 1)
    distance = jnp.abs(lax.broadcasted_iota(jnp.int32, shape, 0) - M).astype(F32)
    half = (8 * (klass // PLANES + 1)).astype(F32)
    w_coef = 0.5 * (klass % PLANES + 1).astype(F32) / PLANES
    ratio = jnp.minimum(distance / half, 1.0)
    square = ratio * ratio
    radius = jnp.sqrt(jnp.maximum(1.0 - square, 0.0))
    bessel = bessel_zero(BETA * radius) / bessel_zero(jnp.full(shape, BETA, F32))
    taper = jnp.cos(jnp.pi * w_coef * square)
    return jnp.where(ratio < 1.0, bessel * taper, 0.0).astype(BF16)


def turned(values, by, sub):
    for bit in (32, 16, 8):
        chosen = (by & bit) != 0
        values = [jnp.where(chosen, values[(k - bit // 8) % 8], values[k]) for k in range(8)]
    for bit in (4, 2, 1):
        chosen = (by & bit) != 0
        rolled = [pltpu.roll(x, bit, 0) for x in values]
        values = [
            jnp.where(chosen, jnp.where(sub < bit, rolled[(k - 1) % 8], rolled[k]), values[k]) for k in range(8)
        ]
    return values


def lay(klass, row, col, re, im, table, weights, columns, start=0):
    sub = lax.broadcasted_iota(jnp.int32, klass.shape, 0)
    hot = jnp.concatenate([(klass == sub + 8 * k).astype(F32) for k in range(8)], axis=0).astype(BF16)
    values = jnp.dot(table[...], hot, preferred_element_type=F32)
    values = [values[8 * k : 8 * k + 8] for k in range(8)]
    by, first = row & 63, row >> 6
    mine = [
        jnp.where(jnp.where(sub + 8 * k < by, first + 1, first) == 0, x, 0.0)
        for k, x in enumerate(turned(values, by, sub))
    ]
    weights[0:64] = jnp.concatenate([x * re for x in mine], axis=0).astype(BF16)
    weights[64:128] = jnp.concatenate([x * im for x in mine], axis=0).astype(BF16)
    by, first = col & 63, col >> 6
    window = jnp.concatenate(turned(values, by, sub), axis=0).astype(BF16)
    block = jnp.concatenate(
        [jnp.where(sub + 8 * k < by, first + 1, first).astype(F32) for k in range(8)], axis=0).astype(BF16)
    for b in range(columns.shape[0] // 64):
        columns[64 * b : 64 * b + 64] = jnp.where(block == jnp.asarray(start + b, BF16), window, jnp.asarray(0, BF16))


def add(total, weights, columns, start=0):
    stop = 64 * start + columns.shape[0]
    total[64 * start : stop] += lax.dot_general(
        columns[...], weights[...], (((1,), (1,)), ((), ())), preferred_element_type=F32)


def exchange(vis, cell, sup, wpl, cnt, got, edge, table, total, flag, vis_v, cell_v, sup_v, wpl_v, cnt_v, packed, tile_flags, chan_flags,
             weights, columns,
             load_sem, send_sem, recv_sem, edge_send, edge_recv, tf_send, tf_recv, cf_send, cf_recv):
    t, c = lax.axis_index("tile"), lax.axis_index("chan")
    nt, nc = lax.axis_size("tile"), lax.axis_size("chan")
    slots = vis_v.shape[-1]
    loads = [
        pltpu.make_async_copy(vis.at[0, 0], vis_v, load_sem.at[0]),
        pltpu.make_async_copy(cell.at[0, 0], cell_v, load_sem.at[1]),
        pltpu.make_async_copy(sup.at[0], sup_v, load_sem.at[2]),
        pltpu.make_async_copy(wpl.at[0], wpl_v, load_sem.at[3]),
        pltpu.make_async_copy(cnt, cnt_v, load_sem.at[4]),
    ]
    for load in loads:
        load.start()
    edge[...] = jnp.zeros_like(edge)

    bar = pltpu.get_barrier_semaphore()
    for i in range(1, nc):
        pl.semaphore_signal(bar, inc=1, device_id=(t, lax.rem(c + i, nc)), device_id_type=MESH)
    for i in range(1, nt):
        pl.semaphore_signal(bar, inc=1, device_id=(lax.rem(t + i, nt), c), device_id_type=MESH)
    from_low = (c == 0) & (t > 0)
    from_high = (c == nc - 1) & (t < nt - 1)

    @pl.when(from_low)
    def _():
        for g in range(nc):
            pl.semaphore_signal(bar, inc=1, device_id=(t - 1, g), device_id_type=MESH)

    @pl.when(from_high)
    def _():
        for g in range(nc):
            pl.semaphore_signal(bar, inc=1, device_id=(t + 1, g), device_id_type=MESH)

    for load in loads:
        load.wait()

    live = lax.broadcasted_iota(jnp.int32, (1, slots), 1) < cnt_v[...]
    row = cell_v[0:1]
    buckets = G // BUCKET
    bucket = row // BUCKET
    right = cell_v[1:2] >= G // 2
    side = jnp.where(live, bucket + jnp.where(right, buckets, 0), -1)
    hot = (lax.broadcasted_iota(jnp.int32, (2 * buckets, slots), 0) == side).astype(F32)
    step = 256
    before = (
        lax.broadcasted_iota(jnp.int32, (step, step), 0) < lax.broadcasted_iota(jnp.int32, (step, step), 1)
    ).astype(F32).astype(BF16)
    parts = []
    carry = jnp.zeros((2 * buckets, 1), F32)
    for s in range(0, slots, step):
        piece = hot[:, s : s + step]
        ahead = jnp.dot(piece.astype(BF16), before, preferred_element_type=F32) + carry
        parts.append(jnp.sum(piece * ahead, axis=0, keepdims=True))
        carry = carry + jnp.sum(piece, axis=1, keepdims=True)
    rank = jnp.concatenate(parts, axis=1).astype(jnp.int32)
    full = jnp.max(carry[:buckets] + carry[buckets:], axis=0, keepdims=True) > CAP
    full = full | (jnp.max(carry, axis=0, keepdims=True) > CAP - LOW)
    over = full.astype(F32)
    tile_flags[t] = jnp.broadcast_to(over, (1, 128))

    below, above = (t > 0).astype(jnp.int32), (t < nt - 1).astype(jnp.int32)
    pl.semaphore_wait(bar, nc - 1 + nt - 1 + below + above)

    def tile_flag(i, slot):
        return pltpu.make_async_remote_copy(
            src_ref=tile_flags.at[t], dst_ref=tile_flags.at[slot], send_sem=tf_send.at[i], recv_sem=tf_recv.at[slot],
            device_id=(lax.rem(t + i, nt), c), device_id_type=MESH)

    for i in range(1, nt):
        tile_flag(i, t).start()

    spot = jnp.where(right, CAP - 1 - rank, rank)
    group = jnp.where(live, (bucket + 1) * GROUPS_IN + (spot >> (LOW.bit_length() - 1)), -1)
    place = spot & (LOW - 1)
    groups = packed.shape[0]
    to_group = (lax.broadcasted_iota(jnp.int32, (groups, slots), 0) == group).astype(F32).astype(BF16)
    at_place = lax.broadcasted_iota(jnp.int32, (LOW, slots), 0) == place

    def halves(x):
        high = x.astype(BF16).astype(F32)
        return high, x - high

    re_hi, re_lo = halves(vis_v[0:1])
    im_hi, im_lo = halves(vis_v[1:2])
    col = cell_v[1:2]
    pieces = [re_hi, im_hi, col >> 2, sup_v[...] * PLANES + wpl_v[...], re_lo, im_lo,
              (col & 3) * 64 + (row & (BUCKET - 1)) + 1, jnp.zeros((1, slots), F32)]
    spread = jnp.concatenate([jnp.where(at_place, x.astype(F32), 0.0).astype(BF16) for x in pieces], axis=0)
    moved = lax.dot_general(to_group, spread, (((1,), (1,)), ((), ())), preferred_element_type=F32)
    first, second = moved[:, 0:128], moved[:, 128:256]
    whole_1, whole_2 = first.astype(jnp.int32), second.astype(jnp.int32)
    lane = lax.broadcasted_iota(jnp.int32, first.shape, 1) // LOW
    packed[:, 0:128] = jnp.where(
        lane < 2, first + second,
        jnp.where(lane == 2, whole_1 * 4 + (whole_2 >> 6), pltpu.roll(whole_2, LOW, 1) & 63).astype(F32))
    klass = pltpu.roll(whole_1, LOW, 1)
    packed[:, 128:256] = jnp.where(
        lane == 0, klass >> 4,
        jnp.where(lane == 1, pltpu.roll(klass, LOW, 1) & (PLANES - 1),
                  jnp.where((lane == 2) & ((whole_2 & 63) > 0), 1, 0))).astype(F32)

    width = 4 * GROUPS_IN

    def payload(peer, slot):
        return pltpu.make_async_remote_copy(
            src_ref=packed.at[pl.ds(8 * peer, width)], dst_ref=got.at[slot], send_sem=send_sem.at[peer],
            recv_sem=recv_sem.at[slot], device_id=(t, peer), device_id_type=MESH)

    order = [0, 1, 2, 3, 4, 5, 8, 9, 6, 7, 10, 11, 12, 13, 14, 15]
    for peer in order:
        @pl.when(c != peer)
        def _(peer=peer):
            payload(peer, c).start()

    def edge_up():
        return pltpu.make_async_remote_copy(
            src_ref=packed.at[pl.ds(buckets * GROUPS_IN, GROUPS_IN)], dst_ref=edge.at[c, 0:GROUPS_IN], send_sem=edge_send.at[0],
            recv_sem=edge_recv.at[c], device_id=(t + 1, 0), device_id_type=MESH)

    def edge_down():
        return pltpu.make_async_remote_copy(
            src_ref=packed.at[pl.ds(GROUPS_IN, GROUPS_IN)], dst_ref=edge.at[c, 0:GROUPS_IN], send_sem=edge_send.at[1],
            recv_sem=edge_recv.at[c], device_id=(t - 1, nc - 1), device_id_type=MESH)

    @pl.when(t < nt - 1)
    def _():
        edge_up().start()

    @pl.when(t > 0)
    def _():
        edge_down().start()

    got[c] = packed[pl.ds(pl.multiple_of(8 * c, 8), width), :]

    for i in range(1, nt):
        tile_flag(i, lax.rem(t + i, nt)).wait_recv()
    chan_flags[c] = jnp.max(tile_flags[...], axis=0)

    def chan_flag(peer, slot):
        return pltpu.make_async_remote_copy(
            src_ref=chan_flags.at[c], dst_ref=chan_flags.at[slot], send_sem=cf_send.at[peer], recv_sem=cf_recv.at[slot],
            device_id=(t, peer), device_id_type=MESH)

    for peer in order:
        @pl.when(c != peer)
        def _(peer=peer):
            chan_flag(peer, c).start()

    table[...] = class_table()
    total[...] = jnp.zeros_like(total)

    spot = lax.broadcasted_iota(jnp.int32, (8, 128), 1) // LOW

    def fields(first, second, lift, picks):
        row_lanes = lax.broadcasted_iota(jnp.int32, first.shape, 1) // LOW == 3
        cells = first.astype(jnp.int32) - M
        cells = jnp.where(row_lanes, cells + lift, cells)
        klass = (second * float(PLANES) + pltpu.roll(second, 3 * LOW, 1)).astype(jnp.int32)

        def lines(x, offset):
            shifted = [pltpu.roll(x, ((b - offset) % 4) * LOW, 1) if (b - offset) % 4 else x for b in range(4)]
            made = []
            for pick in picks:
                parts = [jnp.broadcast_to(shifted[b][r : r + 1], (8, 128)) for b, r in enumerate(pick)]
                line = parts[0]
                for b in range(1, 4):
                    line = jnp.where(spot == b, parts[b], line)
                made.append(line)
            return made

        return lines(klass, 0), lines(cells, 3), lines(cells, 2), lines(first, 0), lines(first, 1)

    halves_at = (0, G // 64 - SPAN)
    lift = BUCKET * (lax.broadcasted_iota(jnp.int32, (width, 128), 0) // GROUPS_IN - 1) - 1

    here = 2 * (c // 2)

    def chip(k):
        q = k % 4
        dz = q + jnp.where(q == 2, 1, 0) - jnp.where(q == 3, 1, 0)
        z, y = (here // 2) % 4, here // 8
        return (((y + k // 4) % 2) * 4 + (z + dz) % 4) * 2

    def prepare(source, slot):
        made = [
            fields(got[x, :, 0:128], got[x, :, 128:256], lift, [[GROUPS_IN * b + g for b in range(4)] for g in EARLY])
            for x in (source, source + 1)
        ]
        for h in range(2):
            lay(*[jnp.concatenate([x[h], y[h]], axis=1) for x, y in zip(*made)], table, weights.at[slot, h],
                columns.at[slot, h], halves_at[h])

    def add_both(slot):
        for h in range(2):
            add(total, weights.at[slot, h], columns.at[slot, h], halves_at[h])

    def arrive(source):
        pltpu.make_async_remote_copy(
            src_ref=packed.at[pl.ds(0, width)], dst_ref=got.at[source], send_sem=send_sem.at[1],
            recv_sem=recv_sem.at[source], device_id=(t, source), device_id_type=MESH).wait_recv()

    arrive(here + (c + 1) % 2)
    prepare(here, 0)

    def two_chips(j, carry):
        for odd in (1, 0):
            source = chip(2 * j + 2 - odd)
            arrive(source)
            arrive(source + 1)
            prepare(source, odd)
            add_both(1 - odd)
        return carry

    chips = nc // 2
    lax.fori_loop(0, chips // 2 - 1, two_chips, 0)
    source = chip(chips - 1)
    arrive(source)
    arrive(source + 1)
    prepare(source, 1)
    add_both(0)
    add_both(1)

    @pl.when(from_low | from_high)
    def _():
        for g in range(nc):
            pltpu.make_async_remote_copy(
                src_ref=packed.at[pl.ds(0, GROUPS_IN)], dst_ref=edge.at[g, 0:GROUPS_IN], send_sem=edge_send.at[0],
                recv_sem=edge_recv.at[g], device_id=(t, g), device_id_type=MESH).wait_recv()
        rows = edge[...].reshape(nc * 8, 256)
        lines = nc // 4
        picks = [[8 * (4 * n + b) + g for b in range(4)] for g in EARLY for n in range(lines)]
        made = fields(rows[:, 0:128], rows[:, 128:256], jnp.where(from_low, -BUCKET, 2 * BUCKET) - 1, picks)
        for h in range(2):
            for n in range(0, lines, 2):
                lay(*[jnp.concatenate(x[h * lines + n : h * lines + n + 2], axis=1) for x in made], table,
                    weights.at[n // 2, h], columns.at[n // 2, h], halves_at[h])
        for n in range(lines // 2):
            add_both(n)

    for peer in range(nc):
        @pl.when(c != peer)
        def _(peer=peer):
            chan_flag(peer, peer).wait_recv()
            chan_flag(peer, c).wait_send()
            payload(peer, c).wait_send()

    flag[0, 0] = (jnp.max(jnp.max(chan_flags[...], axis=0)) > 0.5).astype(jnp.int32)
    for i in range(1, nt):
        tile_flag(i, t).wait_send()

    @pl.when(t < nt - 1)
    def _():
        edge_up().wait_send()

    @pl.when(t > 0)
    def _():
        edge_down().wait_send()


def owned_rows(got, edge, table, begun, out, real, whole, total, weights, columns):
    c = lax.axis_index("chan")
    nc, per = got.shape[0], got.shape[1]
    main = nc * per
    count = main + nc * 8
    left = nc * (per // GROUPS_IN + 1) * (GROUPS_IN - len(EARLY))
    quarter = left // 4

    lanes = lax.broadcasted_iota(jnp.int32, (1, 256), 1) // LOW
    both = jnp.concatenate([got[...].reshape(main, 256), edge[...].reshape(nc * 8, 256)], axis=0)
    index = lax.broadcasted_iota(jnp.int32, (count, 256), 0)
    shift = jnp.where(index < main, BUCKET * ((index % per) // GROUPS_IN - 1), jnp.where(c == 0, -BUCKET, 2 * BUCKET))
    both = both + jnp.where(lanes == 3, shift - 1, 0).astype(F32)
    used = jnp.max(both[:, 128:256].T[2 * LOW : 3 * LOW], axis=0, keepdims=True)
    at = lax.broadcasted_iota(jnp.int32, (1, count), 1) % GROUPS_IN
    used = jnp.where((at == EARLY[0]) | (at == EARLY[1]), 0.0, used)
    before = (
        lax.broadcasted_iota(jnp.int32, (count, count), 0) < lax.broadcasted_iota(jnp.int32, (count, count), 1)
    ).astype(F32).astype(BF16)
    rank = jnp.dot(jnp.broadcast_to(used, (8, count)).astype(BF16), before, preferred_element_type=F32)[0:1]
    rank = jnp.where(used > 0.5, rank, -1.0)
    place = lax.broadcasted_iota(jnp.int32, (left, count), 0)
    place = (4 * (place % quarter) + place // quarter).astype(F32)
    pick = jnp.where(place == rank, 1.0, 0.0).astype(BF16)
    high = both.astype(BF16)
    low = (both - high.astype(F32)).astype(BF16)
    rows = jnp.dot(pick, high, preferred_element_type=F32) + jnp.dot(pick, low, preferred_element_type=F32)
    spot = lax.broadcasted_iota(jnp.int32, (quarter, 128), 1) // LOW

    def field(f):
        part, offset = divmod(f, 4)
        result = None
        for s in range(4):
            x = rows[s * quarter : (s + 1) * quarter, 128 * part : 128 * part + 128]
            if (s - offset) % 4:
                x = pltpu.roll(x, ((s - offset) % 4) * LOW, 1)
            result = x if result is None else jnp.where(spot == s, x, result)
        return result

    real[0], real[1] = field(0), field(1)
    whole[0], whole[1] = field(2).astype(jnp.int32) - M, field(3).astype(jnp.int32) - M
    whole[2] = (field(4) * float(PLANES) + field(5)).astype(jnp.int32)
    size = weights.shape[-1]
    lines = size // 128
    chunks = (jnp.sum(used).astype(jnp.int32) + 4 * lines - 1) // (4 * lines)

    total[...] = begun[...]

    def body(i, carry):
        def line(ref, f):
            return jnp.concatenate(
                [jnp.broadcast_to(ref[f, pl.ds(lines * i + h, 1), :], (8, 128)) for h in range(lines)], axis=1)

        lay(line(whole, 2), line(whole, 1), line(whole, 0), line(real, 0), line(real, 1), table, weights, columns)
        add(total, weights, columns)
        return carry

    lax.fori_loop(0, chunks, body, 0)
    rows = total[...].T
    out[:, 0, :] = rows[0:64]
    out[:, 1, :] = rows[64:128]


def per_device(visibilities, cell_offsets, support_index, w_plane, live_counts):
    nt, nc = lax.axis_size("tile"), lax.axis_size("chan")
    slots = visibilities.shape[-1]
    groups = (G // BUCKET + 2) * GROUPS_IN
    vmem = pl.BlockSpec(memory_space=pltpu.VMEM)
    got, edge, table, begun, flag = pl.pallas_call(
        exchange,
        out_shape=(
            jax.ShapeDtypeStruct((nc, 4 * GROUPS_IN, FIELDS * LOW), F32),
            jax.ShapeDtypeStruct((nc, 8, FIELDS * LOW), F32),
            jax.ShapeDtypeStruct((2 * M, 4 * PLANES), BF16),
            jax.ShapeDtypeStruct((G, 2 * G // nc), F32),
            jax.ShapeDtypeStruct((1, 1), jnp.int32),
        ),
        in_specs=[pl.BlockSpec(memory_space=pltpu.MemorySpace.HBM)] * 5,
        out_specs=(vmem, vmem, vmem, vmem, pl.BlockSpec(memory_space=pltpu.SMEM)),
        scratch_shapes=[
            pltpu.VMEM((2, slots), F32),
            pltpu.VMEM((2, slots), jnp.int32),
            pltpu.VMEM((1, slots), jnp.int32),
            pltpu.VMEM((1, slots), jnp.int32),
            pltpu.VMEM((1, 1), jnp.int32),
            pltpu.VMEM((groups, FIELDS * LOW), F32),
            pltpu.VMEM((nt, 1, 128), F32),
            pltpu.VMEM((nc, 1, 128), F32),
            pltpu.VMEM((2, 2, 2 * G // nc, 256), BF16),
            pltpu.VMEM((2, 2, 64 * SPAN, 256), BF16),
            pltpu.SemaphoreType.DMA((5,)),
            pltpu.SemaphoreType.DMA((nc,)),
            pltpu.SemaphoreType.DMA((nc,)),
            pltpu.SemaphoreType.DMA((2,)),
            pltpu.SemaphoreType.DMA((nc,)),
            pltpu.SemaphoreType.DMA((nt,)),
            pltpu.SemaphoreType.DMA((nt,)),
            pltpu.SemaphoreType.DMA((nc,)),
            pltpu.SemaphoreType.DMA((nc,)),
        ],
        compiler_params=pltpu.CompilerParams(collective_id=0, has_side_effects=True, vmem_limit_bytes=62 << 20),
    )(visibilities, cell_offsets, support_index, w_plane, live_counts)

    groups_left = nc * 5 * (GROUPS_IN - len(EARLY))

    def usual(*_):
        return pl.pallas_call(
            owned_rows,
            out_shape=jax.ShapeDtypeStruct((G // nc, 2, G), F32),
            in_specs=[vmem] * 4,
            out_specs=vmem,
            scratch_shapes=[
                pltpu.VMEM((2, groups_left // 4, 128), F32),
                pltpu.VMEM((3, groups_left // 4, 128), jnp.int32),
                pltpu.VMEM((G, 2 * G // nc), F32),
                pltpu.VMEM((2 * G // nc, 512), BF16),
                pltpu.VMEM((G, 512), BF16),
            ],
            compiler_params=pltpu.CompilerParams(vmem_limit_bytes=40 << 20),
        )(got, edge, table, begun)

    return lax.cond(
        flag[0, 0] > 0, any_cells, usual, visibilities, cell_offsets, support_index, w_plane, live_counts
    )


def solution(mesh):
    in_specs = (
        P("tile", "chan", None, None),
        P("tile", "chan", None, None),
        P("tile", "chan", None),
        P("tile", "chan", None),
        P("tile", "chan"),
    )
    out_specs = P(("tile", "chan"), None, None)
    return jax.shard_map(
        per_device, mesh=mesh, in_specs=in_specs, out_specs=out_specs, check_vma=False
    )
```

```python
import functools
import math

import jax
import jax.numpy as jnp
from jax import lax
from jax.experimental import pallas as pl
from jax.experimental.pallas import tpu as pltpu
from jax.sharding import PartitionSpec as P

G = 1024
M = 32
PLANES = 16
BETA = 7.0

BUCKET = 32
CAP = 128
LOW = 32
GROUPS_IN = CAP // LOW
EARLY = (0, GROUPS_IN - 1)
SPAN = 10
FIELDS = 8
MESH = pl.DeviceIdType.MESH
F32 = jnp.float32
BF16 = jnp.bfloat16


def bessel_zero(value):
    quarter = value * value * 0.25
    term = jnp.ones_like(value)
    total = jnp.ones_like(value)
    for index in range(1, 30):
        term = term * quarter * (1.0 / float(index * index))
        total = total + term
    return total


def kernel_values(distance, half_width, w_coef):
    ratio = distance / half_width
    inside = jnp.abs(ratio) < 1.0
    radius = jnp.sqrt(jnp.maximum(1.0 - ratio * ratio, 0.0))
    bessel = bessel_zero(BETA * radius) / bessel_zero(jnp.float32(BETA))
    taper = jnp.cos(jnp.pi * w_coef * ratio * ratio)
    return jnp.where(inside, bessel * taper, jnp.float32(0.0))


def flatten_groups(vis_block, offset_block, support_block, plane_block, count_block):
    slot_total = vis_block.shape[-1]
    slot_ids = jnp.arange(slot_total, dtype=jnp.int32)
    live = (slot_ids[None, :] < count_block[:, None]).astype(jnp.float32).reshape(-1)
    real_part = vis_block[:, 0].reshape(-1) * live
    imag_part = vis_block[:, 1].reshape(-1) * live
    row_cell = offset_block[:, 0].reshape(-1).astype(jnp.float32)
    col_cell = offset_block[:, 1].reshape(-1).astype(jnp.float32)
    half_width = 8.0 * (support_block.reshape(-1) + 1).astype(jnp.float32)
    w_coef = 0.5 * (plane_block.reshape(-1) + 1).astype(jnp.float32) / PLANES
    return (real_part, imag_part, row_cell, col_cell, half_width, w_coef)


def grid_part(flat, row_start, row_count, width):
    total_vis = flat[0].shape[0]
    block_len = math.gcd(total_vis, 512)
    stacked = tuple((item.reshape(total_vis // block_len, block_len) for item in flat))
    row_pos = (row_start + jnp.arange(row_count, dtype=jnp.int32)).astype(jnp.float32)
    col_pos = jnp.arange(width, dtype=jnp.int32).astype(jnp.float32)

    def step_block(total, values):
        real_part, imag_part, row_cell, col_cell, half_width, w_coef = values
        row_weights = kernel_values(
            row_pos[None, :] - row_cell[:, None], half_width[:, None], w_coef[:, None]
        ).astype(jnp.bfloat16)
        col_kern = kernel_values(
            col_pos[None, :] - col_cell[:, None], half_width[:, None], w_coef[:, None]
        )
        col_weights = jnp.concatenate(
            [real_part[:, None] * col_kern, imag_part[:, None] * col_kern], axis=1
        ).astype(jnp.bfloat16)
        product = lax.dot_general(
            row_weights, col_weights, (((0,), (0,)), ((), ())), preferred_element_type=jnp.float32
        )
        return (total + product, None)

    start_total = jnp.zeros((row_count, 2 * width), jnp.float32)
    total, _ = lax.scan(step_block, start_total, stacked)
    return total.reshape(row_count, 2, width)


def any_cells(visibilities, cell_offsets, support_index, w_plane, live_counts):
    tiles, parts = lax.axis_size("tile"), lax.axis_size("chan")
    share = G // parts
    first_row = lax.axis_index("chan") * share - M
    held = jnp.stack(
        flatten_groups(visibilities[0], cell_offsets[0], support_index[0], w_plane[0], live_counts[0])
    )

    def step(_, carry):
        total, held = carry
        total = total + grid_part(held, first_row, share + 2 * M, G)
        return total, lax.ppermute(held, "chan", [(i, (i + 1) % parts) for i in range(parts)])

    total, _ = lax.fori_loop(0, parts, step, (jnp.zeros((share + 2 * M, 2, G), F32), held))
    last = parts - 1
    left_in = lax.ppermute(
        total[share + M :], ("tile", "chan"), [(t * parts + last, (t + 1) * parts) for t in range(tiles - 1)]
    )
    right_in = lax.ppermute(
        total[:M], ("tile", "chan"), [(t * parts, (t - 1) * parts + last) for t in range(1, tiles)]
    )
    owned = total[M : M + share]
    return owned.at[:M].add(left_in).at[share - M :].add(right_in)


def class_table():
    shape = (2 * M, 4 * PLANES)
    klass = lax.broadcasted_iota(jnp.int32, shape, 1)
    distance = jnp.abs(lax.broadcasted_iota(jnp.int32, shape, 0) - M).astype(F32)
    half = (8 * (klass // PLANES + 1)).astype(F32)
    w_coef = 0.5 * (klass % PLANES + 1).astype(F32) / PLANES
    ratio = jnp.minimum(distance / half, 1.0)
    square = ratio * ratio
    radius = jnp.sqrt(jnp.maximum(1.0 - square, 0.0))
    bessel = bessel_zero(BETA * radius) / bessel_zero(jnp.full(shape, BETA, F32))
    taper = jnp.cos(jnp.pi * w_coef * square)
    return jnp.where(ratio < 1.0, bessel * taper, 0.0).astype(BF16)


def turned(values, by, sub):
    for bit in (32, 16, 8):
        chosen = (by & bit) != 0
        values = [jnp.where(chosen, values[(k - bit // 8) % 8], values[k]) for k in range(8)]
    for bit in (4, 2, 1):
        chosen = (by & bit) != 0
        rolled = [pltpu.roll(x, bit, 0) for x in values]
        values = [
            jnp.where(chosen, jnp.where(sub < bit, rolled[(k - 1) % 8], rolled[k]), values[k]) for k in range(8)
        ]
    return values


def lay(klass, row, col, re, im, table, weights, columns, start=0):
    sub = lax.broadcasted_iota(jnp.int32, klass.shape, 0)
    hot = jnp.concatenate([(klass == sub + 8 * k).astype(F32) for k in range(8)], axis=0).astype(BF16)
    values = jnp.dot(table[...], hot, preferred_element_type=F32)
    values = [values[8 * k : 8 * k + 8] for k in range(8)]
    by, first = row & 63, row >> 6
    mine = [
        jnp.where(jnp.where(sub + 8 * k < by, first + 1, first) == 0, x, 0.0)
        for k, x in enumerate(turned(values, by, sub))
    ]
    weights[0:64] = jnp.concatenate([x * re for x in mine], axis=0).astype(BF16)
    weights[64:128] = jnp.concatenate([x * im for x in mine], axis=0).astype(BF16)
    by, first = col & 63, col >> 6
    window = jnp.concatenate(turned(values, by, sub), axis=0).astype(BF16)
    block = jnp.concatenate(
        [jnp.where(sub + 8 * k < by, first + 1, first).astype(F32) for k in range(8)], axis=0).astype(BF16)
    for b in range(columns.shape[0] // 64):
        columns[64 * b : 64 * b + 64] = jnp.where(block == jnp.asarray(start + b, BF16), window, jnp.asarray(0, BF16))


def add(total, weights, columns, start=0):
    stop = 64 * start + columns.shape[0]
    total[:, 64 * start : stop] += lax.dot_general(
        weights[...], columns[...], (((1,), (1,)), ((), ())), preferred_element_type=F32)


def list_left(got, edge, real, whole, number):
    c = lax.axis_index("chan")
    nc, per = got.shape[0], got.shape[1]
    main = nc * per
    count = main + nc * 8
    left = 4 * real.shape[1]
    quarter = left // 4

    lanes = lax.broadcasted_iota(jnp.int32, (1, 256), 1) // LOW
    both = jnp.concatenate([got[...].reshape(main, 256), edge[...].reshape(nc * 8, 256)], axis=0)
    index = lax.broadcasted_iota(jnp.int32, (count, 256), 0)
    shift = jnp.where(index < main, BUCKET * ((index % per) // GROUPS_IN - 1), jnp.where(c == 0, -BUCKET, 2 * BUCKET))
    both = both + jnp.where(lanes == 3, shift - 1, 0).astype(F32)
    used = jnp.max(both[:, 128:256].T[2 * LOW : 3 * LOW], axis=0, keepdims=True)
    at = lax.broadcasted_iota(jnp.int32, (1, count), 1) % GROUPS_IN
    used = jnp.where((at == EARLY[0]) | (at == EARLY[1]), 0.0, used)
    before = (
        lax.broadcasted_iota(jnp.int32, (count, count), 0) < lax.broadcasted_iota(jnp.int32, (count, count), 1)
    ).astype(F32).astype(BF16)
    rank = jnp.dot(jnp.broadcast_to(used, (8, count)).astype(BF16), before, preferred_element_type=F32)[0:1]
    rank = jnp.where(used > 0.5, rank, -1.0)
    place = lax.broadcasted_iota(jnp.int32, (left, count), 0)
    place = (4 * (place % quarter) + place // quarter).astype(F32)
    pick = jnp.where(place == rank, 1.0, 0.0).astype(BF16)
    high = both.astype(BF16)
    low = (both - high.astype(F32)).astype(BF16)
    rows = jnp.dot(pick, high, preferred_element_type=F32) + jnp.dot(pick, low, preferred_element_type=F32)
    spot = lax.broadcasted_iota(jnp.int32, (quarter, 128), 1) // LOW

    def field(f):
        part, offset = divmod(f, 4)
        result = None
        for s in range(4):
            x = rows[s * quarter : (s + 1) * quarter, 128 * part : 128 * part + 128]
            if (s - offset) % 4:
                x = pltpu.roll(x, ((s - offset) % 4) * LOW, 1)
            result = x if result is None else jnp.where(spot == s, x, result)
        return result

    real[0], real[1] = field(0), field(1)
    whole[0], whole[1] = field(2).astype(jnp.int32) - M, field(3).astype(jnp.int32) - M
    whole[2] = (field(4) * float(PLANES) + field(5)).astype(jnp.int32)
    number[...] = jnp.broadcast_to(jnp.sum(used, axis=1, keepdims=True), number.shape)


def exchange(vis, cell, sup, wpl, cnt, table, total, real, whole, number, flag, got, edge, vis_v, cell_v, sup_v, wpl_v, cnt_v, packed, tile_flags, chan_flags,
             weights, columns,
             load_sem, send_sem, recv_sem, edge_send, edge_recv, tf_send, tf_recv, cf_send, cf_recv):
    t, c = lax.axis_index("tile"), lax.axis_index("chan")
    nt, nc = lax.axis_size("tile"), lax.axis_size("chan")
    slots = vis_v.shape[-1]
    loads = [
        pltpu.make_async_copy(vis.at[0, 0], vis_v, load_sem.at[0]),
        pltpu.make_async_copy(cell.at[0, 0], cell_v, load_sem.at[1]),
        pltpu.make_async_copy(sup.at[0], sup_v, load_sem.at[2]),
        pltpu.make_async_copy(wpl.at[0], wpl_v, load_sem.at[3]),
        pltpu.make_async_copy(cnt, cnt_v, load_sem.at[4]),
    ]
    for load in loads:
        load.start()
    edge[...] = jnp.zeros_like(edge)

    bar = pltpu.get_barrier_semaphore()
    for i in range(1, nc):
        pl.semaphore_signal(bar, inc=1, device_id=(t, lax.rem(c + i, nc)), device_id_type=MESH)
    for i in range(1, nt):
        pl.semaphore_signal(bar, inc=1, device_id=(lax.rem(t + i, nt), c), device_id_type=MESH)
    from_low = (c == 0) & (t > 0)
    from_high = (c == nc - 1) & (t < nt - 1)

    @pl.when(from_low)
    def _():
        for g in range(nc):
            pl.semaphore_signal(bar, inc=1, device_id=(t - 1, g), device_id_type=MESH)

    @pl.when(from_high)
    def _():
        for g in range(nc):
            pl.semaphore_signal(bar, inc=1, device_id=(t + 1, g), device_id_type=MESH)

    for load in loads:
        load.wait()

    live = lax.broadcasted_iota(jnp.int32, (1, slots), 1) < cnt_v[...]
    row = cell_v[0:1]
    buckets = G // BUCKET
    bucket = row // BUCKET
    right = cell_v[1:2] >= G // 2
    side = jnp.where(live, bucket + jnp.where(right, buckets, 0), -1)
    hot = (lax.broadcasted_iota(jnp.int32, (2 * buckets, slots), 0) == side).astype(F32)
    step = 256
    before = (
        lax.broadcasted_iota(jnp.int32, (step, step), 0) < lax.broadcasted_iota(jnp.int32, (step, step), 1)
    ).astype(F32).astype(BF16)
    parts = []
    carry = jnp.zeros((2 * buckets, 1), F32)
    for s in range(0, slots, step):
        piece = hot[:, s : s + step]
        ahead = jnp.dot(piece.astype(BF16), before, preferred_element_type=F32) + carry
        parts.append(jnp.sum(piece * ahead, axis=0, keepdims=True))
        carry = carry + jnp.sum(piece, axis=1, keepdims=True)
    rank = jnp.concatenate(parts, axis=1).astype(jnp.int32)
    full = jnp.max(carry[:buckets] + carry[buckets:], axis=0, keepdims=True) > CAP
    full = full | (jnp.max(carry, axis=0, keepdims=True) > CAP - LOW)
    over = full.astype(F32)
    tile_flags[t] = jnp.broadcast_to(over, (1, 128))

    below, above = (t > 0).astype(jnp.int32), (t < nt - 1).astype(jnp.int32)
    pl.semaphore_wait(bar, nc - 1 + nt - 1 + below + above)

    def tile_flag(i, slot):
        return pltpu.make_async_remote_copy(
            src_ref=tile_flags.at[t], dst_ref=tile_flags.at[slot], send_sem=tf_send.at[i], recv_sem=tf_recv.at[slot],
            device_id=(lax.rem(t + i, nt), c), device_id_type=MESH)

    for i in range(1, nt):
        tile_flag(i, t).start()

    spot = jnp.where(right, CAP - 1 - rank, rank)
    group = jnp.where(live, (bucket + 1) * GROUPS_IN + (spot >> (LOW.bit_length() - 1)), -1)
    place = spot & (LOW - 1)
    groups = packed.shape[0]
    to_group = (lax.broadcasted_iota(jnp.int32, (groups, slots), 0) == group).astype(F32).astype(BF16)
    at_place = lax.broadcasted_iota(jnp.int32, (LOW, slots), 0) == place

    def halves(x):
        high = x.astype(BF16).astype(F32)
        return high, x - high

    re_hi, re_lo = halves(vis_v[0:1])
    im_hi, im_lo = halves(vis_v[1:2])
    col = cell_v[1:2]
    pieces = [re_hi, im_hi, col >> 2, sup_v[...] * PLANES + wpl_v[...], re_lo, im_lo,
              (col & 3) * 64 + (row & (BUCKET - 1)) + 1, jnp.zeros((1, slots), F32)]
    spread = jnp.concatenate([jnp.where(at_place, x.astype(F32), 0.0).astype(BF16) for x in pieces], axis=0)
    moved = lax.dot_general(to_group, spread, (((1,), (1,)), ((), ())), preferred_element_type=F32)
    first, second = moved[:, 0:128], moved[:, 128:256]
    whole_1, whole_2 = first.astype(jnp.int32), second.astype(jnp.int32)
    lane = lax.broadcasted_iota(jnp.int32, first.shape, 1) // LOW
    packed[:, 0:128] = jnp.where(
        lane < 2, first + second,
        jnp.where(lane == 2, whole_1 * 4 + (whole_2 >> 6), pltpu.roll(whole_2, LOW, 1) & 63).astype(F32))
    klass = pltpu.roll(whole_1, LOW, 1)
    packed[:, 128:256] = jnp.where(
        lane == 0, klass >> 4,
        jnp.where(lane == 1, pltpu.roll(klass, LOW, 1) & (PLANES - 1),
                  jnp.where((lane == 2) & ((whole_2 & 63) > 0), 1, 0))).astype(F32)

    width = 4 * GROUPS_IN

    def payload(peer, slot):
        return pltpu.make_async_remote_copy(
            src_ref=packed.at[pl.ds(8 * peer, width)], dst_ref=got.at[slot], send_sem=send_sem.at[peer],
            recv_sem=recv_sem.at[slot], device_id=(t, peer), device_id_type=MESH)

    order = [0, 1, 2, 3, 4, 5, 8, 9, 6, 7, 10, 11, 12, 13, 14, 15]
    for peer in order:
        @pl.when(c != peer)
        def _(peer=peer):
            payload(peer, c).start()

    def edge_up():
        return pltpu.make_async_remote_copy(
            src_ref=packed.at[pl.ds(buckets * GROUPS_IN, GROUPS_IN)], dst_ref=edge.at[c, 0:GROUPS_IN], send_sem=edge_send.at[0],
            recv_sem=edge_recv.at[c], device_id=(t + 1, 0), device_id_type=MESH)

    def edge_down():
        return pltpu.make_async_remote_copy(
            src_ref=packed.at[pl.ds(GROUPS_IN, GROUPS_IN)], dst_ref=edge.at[c, 0:GROUPS_IN], send_sem=edge_send.at[1],
            recv_sem=edge_recv.at[c], device_id=(t - 1, nc - 1), device_id_type=MESH)

    @pl.when(t < nt - 1)
    def _():
        edge_up().start()

    @pl.when(t > 0)
    def _():
        edge_down().start()

    got[c] = packed[pl.ds(pl.multiple_of(8 * c, 8), width), :]

    for i in range(1, nt):
        tile_flag(i, lax.rem(t + i, nt)).wait_recv()
    chan_flags[c] = jnp.max(tile_flags[...], axis=0)

    def chan_flag(peer, slot):
        return pltpu.make_async_remote_copy(
            src_ref=chan_flags.at[c], dst_ref=chan_flags.at[slot], send_sem=cf_send.at[peer], recv_sem=cf_recv.at[slot],
            device_id=(t, peer), device_id_type=MESH)

    for peer in order:
        @pl.when(c != peer)
        def _(peer=peer):
            chan_flag(peer, c).start()

    table[...] = class_table()
    total[...] = jnp.zeros_like(total)

    spot = lax.broadcasted_iota(jnp.int32, (8, 128), 1) // LOW

    def fields(first, second, lift, picks):
        row_lanes = lax.broadcasted_iota(jnp.int32, first.shape, 1) // LOW == 3
        cells = first.astype(jnp.int32) - M
        cells = jnp.where(row_lanes, cells + lift, cells)
        klass = (second * float(PLANES) + pltpu.roll(second, 3 * LOW, 1)).astype(jnp.int32)

        def lines(x, offset):
            shifted = [pltpu.roll(x, ((b - offset) % 4) * LOW, 1) if (b - offset) % 4 else x for b in range(4)]
            made = []
            for pick in picks:
                parts = [jnp.broadcast_to(shifted[b][r : r + 1], (8, 128)) for b, r in enumerate(pick)]
                line = parts[0]
                for b in range(1, 4):
                    line = jnp.where(spot == b, parts[b], line)
                made.append(line)
            return made

        return lines(klass, 0), lines(cells, 3), lines(cells, 2), lines(first, 0), lines(first, 1)

    halves_at = (0, G // 64 - SPAN)
    lift = BUCKET * (lax.broadcasted_iota(jnp.int32, (width, 128), 0) // GROUPS_IN - 1) - 1

    here = 2 * (c // 2)

    def chip(k):
        q = k % 4
        dz = q + jnp.where(q == 2, 1, 0) - jnp.where(q == 3, 1, 0)
        z, y = (here // 2) % 4, here // 8
        return (((y + k // 4) % 2) * 4 + (z + dz) % 4) * 2

    def prepare(source, slot):
        made = [
            fields(got[x, :, 0:128], got[x, :, 128:256], lift, [[GROUPS_IN * b + g for b in range(4)] for g in EARLY])
            for x in (source, source + 1)
        ]
        for h in range(2):
            lay(*[jnp.concatenate([x[h], y[h]], axis=1) for x, y in zip(*made)], table, weights.at[slot, h],
                columns.at[slot, h], halves_at[h])

    def add_both(slot):
        for h in range(2):
            add(total, weights.at[slot, h], columns.at[slot, h], halves_at[h])

    def arrive(source):
        pltpu.make_async_remote_copy(
            src_ref=packed.at[pl.ds(0, width)], dst_ref=got.at[source], send_sem=send_sem.at[1],
            recv_sem=recv_sem.at[source], device_id=(t, source), device_id_type=MESH).wait_recv()

    arrive(here + (c + 1) % 2)
    prepare(here, 0)

    def two_chips(j, carry):
        for odd in (1, 0):
            source = chip(2 * j + 2 - odd)
            arrive(source)
            arrive(source + 1)
            prepare(source, odd)
            add_both(1 - odd)
        return carry

    chips = nc // 2
    lax.fori_loop(0, chips // 2 - 1, two_chips, 0)
    add_both(0)

    @pl.when(from_low | from_high)
    def _():
        for g in range(nc):
            pltpu.make_async_remote_copy(
                src_ref=packed.at[pl.ds(0, GROUPS_IN)], dst_ref=edge.at[g, 0:GROUPS_IN], send_sem=edge_send.at[0],
                recv_sem=edge_recv.at[g], device_id=(t, g), device_id_type=MESH).wait_recv()
        rows = edge[...].reshape(nc * 8, 256)
        lines = nc // 4
        picks = [[8 * (4 * n + b) + g for b in range(4)] for g in EARLY for n in range(lines)]
        made = fields(rows[:, 0:128], rows[:, 128:256], jnp.where(from_low, -BUCKET, 2 * BUCKET) - 1, picks)
        for h in range(2):
            for n in range(0, lines, 2):
                lay(*[jnp.concatenate(x[h * lines + n : h * lines + n + 2], axis=1) for x in made], table,
                    weights.at[n // 2, h], columns.at[n // 2, h], halves_at[h])
        for n in range(lines // 2):
            add_both(n)

    source = chip(chips - 1)
    arrive(source)
    arrive(source + 1)
    prepare(source, 1)
    list_left(got, edge, real, whole, number)
    add_both(1)

    for peer in range(nc):
        @pl.when(c != peer)
        def _(peer=peer):
            chan_flag(peer, peer).wait_recv()
            chan_flag(peer, c).wait_send()
            payload(peer, c).wait_send()

    flag[0, 0] = (jnp.max(jnp.max(chan_flags[...], axis=0)) > 0.5).astype(jnp.int32)
    for i in range(1, nt):
        tile_flag(i, t).wait_send()

    @pl.when(t < nt - 1)
    def _():
        edge_up().wait_send()

    @pl.when(t > 0)
    def _():
        edge_down().wait_send()


def owned_rows(real, whole, number, table, begun, out, total, weights, columns):
    size = weights.shape[-1]
    lines = size // 128
    chunks = (jnp.max(number[...]).astype(jnp.int32) + 4 * lines - 1) // (4 * lines)
    total[...] = begun[...]

    def body(i, carry):
        def line(ref, f):
            return jnp.concatenate(
                [jnp.broadcast_to(ref[f, pl.ds(lines * i + h, 1), :], (8, 128)) for h in range(lines)], axis=1)

        lay(line(whole, 2), line(whole, 1), line(whole, 0), line(real, 0), line(real, 1), table, weights, columns)
        add(total, weights, columns)
        return carry

    lax.fori_loop(0, chunks, body, 0)
    out[:, 0, :] = total[0:64]
    out[:, 1, :] = total[64:128]


def per_device(visibilities, cell_offsets, support_index, w_plane, live_counts):
    nt, nc = lax.axis_size("tile"), lax.axis_size("chan")
    slots = visibilities.shape[-1]
    groups = (G // BUCKET + 2) * GROUPS_IN
    vmem = pl.BlockSpec(memory_space=pltpu.VMEM)
    left_lines = nc * 5 * (GROUPS_IN - len(EARLY)) // 4
    table, begun, real, whole, number, flag = pl.pallas_call(
        exchange,
        out_shape=(
            jax.ShapeDtypeStruct((2 * M, 4 * PLANES), BF16),
            jax.ShapeDtypeStruct((2 * G // nc, G), F32),
            jax.ShapeDtypeStruct((2, left_lines, 128), F32),
            jax.ShapeDtypeStruct((3, left_lines, 128), jnp.int32),
            jax.ShapeDtypeStruct((8, 128), F32),
            jax.ShapeDtypeStruct((1, 1), jnp.int32),
        ),
        in_specs=[pl.BlockSpec(memory_space=pltpu.MemorySpace.HBM)] * 5,
        out_specs=(vmem, vmem, vmem, vmem, vmem, pl.BlockSpec(memory_space=pltpu.SMEM)),
        scratch_shapes=[
            pltpu.VMEM((nc, 4 * GROUPS_IN, FIELDS * LOW), F32),
            pltpu.VMEM((nc, 8, FIELDS * LOW), F32),
            pltpu.VMEM((2, slots), F32),
            pltpu.VMEM((2, slots), jnp.int32),
            pltpu.VMEM((1, slots), jnp.int32),
            pltpu.VMEM((1, slots), jnp.int32),
            pltpu.VMEM((1, 1), jnp.int32),
            pltpu.VMEM((groups, FIELDS * LOW), F32),
            pltpu.VMEM((nt, 1, 128), F32),
            pltpu.VMEM((nc, 1, 128), F32),
            pltpu.VMEM((2, 2, 2 * G // nc, 256), BF16),
            pltpu.VMEM((2, 2, 64 * SPAN, 256), BF16),
            pltpu.SemaphoreType.DMA((5,)),
            pltpu.SemaphoreType.DMA((nc,)),
            pltpu.SemaphoreType.DMA((nc,)),
            pltpu.SemaphoreType.DMA((2,)),
            pltpu.SemaphoreType.DMA((nc,)),
            pltpu.SemaphoreType.DMA((nt,)),
            pltpu.SemaphoreType.DMA((nt,)),
            pltpu.SemaphoreType.DMA((nc,)),
            pltpu.SemaphoreType.DMA((nc,)),
        ],
        compiler_params=pltpu.CompilerParams(collective_id=0, has_side_effects=True, vmem_limit_bytes=62 << 20),
    )(visibilities, cell_offsets, support_index, w_plane, live_counts)


    def usual(*_):
        return pl.pallas_call(
            owned_rows,
            out_shape=jax.ShapeDtypeStruct((G // nc, 2, G), F32),
            in_specs=[vmem] * 5,
            out_specs=vmem,
            scratch_shapes=[
                pltpu.VMEM((2 * G // nc, G), F32),
                pltpu.VMEM((2 * G // nc, 512), BF16),
                pltpu.VMEM((G, 512), BF16),
            ],
            compiler_params=pltpu.CompilerParams(vmem_limit_bytes=40 << 20),
        )(real, whole, number, table, begun)

    return lax.cond(
        flag[0, 0] > 0, any_cells, usual, visibilities, cell_offsets, support_index, w_plane, live_counts
    )


def solution(mesh):
    in_specs = (
        P("tile", "chan", None, None),
        P("tile", "chan", None, None),
        P("tile", "chan", None),
        P("tile", "chan", None),
        P("tile", "chan"),
    )
    out_specs = P(("tile", "chan"), None, None)
    return jax.shard_map(
        per_device, mesh=mesh, in_specs=in_specs, out_specs=out_specs, check_vma=False
    )
```

```python
import functools
import math

import jax
import jax.numpy as jnp
from jax import lax
from jax.experimental import pallas as pl
from jax.experimental.pallas import tpu as pltpu
from jax.sharding import PartitionSpec as P

G = 1024
M = 32
PLANES = 16
BETA = 7.0

BUCKET = 32
CAP = 128
LOW = 32
GROUPS_IN = CAP // LOW
EARLY = (0, GROUPS_IN - 1)
SPAN = 10
FIELDS = 8
MESH = pl.DeviceIdType.MESH
F32 = jnp.float32
BF16 = jnp.bfloat16


def bessel_zero(value):
    quarter = value * value * 0.25
    term = jnp.ones_like(value)
    total = jnp.ones_like(value)
    for index in range(1, 30):
        term = term * quarter * (1.0 / float(index * index))
        total = total + term
    return total


def kernel_values(distance, half_width, w_coef):
    ratio = distance / half_width
    inside = jnp.abs(ratio) < 1.0
    radius = jnp.sqrt(jnp.maximum(1.0 - ratio * ratio, 0.0))
    bessel = bessel_zero(BETA * radius) / bessel_zero(jnp.float32(BETA))
    taper = jnp.cos(jnp.pi * w_coef * ratio * ratio)
    return jnp.where(inside, bessel * taper, jnp.float32(0.0))


def flatten_groups(vis_block, offset_block, support_block, plane_block, count_block):
    slot_total = vis_block.shape[-1]
    slot_ids = jnp.arange(slot_total, dtype=jnp.int32)
    live = (slot_ids[None, :] < count_block[:, None]).astype(jnp.float32).reshape(-1)
    real_part = vis_block[:, 0].reshape(-1) * live
    imag_part = vis_block[:, 1].reshape(-1) * live
    row_cell = offset_block[:, 0].reshape(-1).astype(jnp.float32)
    col_cell = offset_block[:, 1].reshape(-1).astype(jnp.float32)
    half_width = 8.0 * (support_block.reshape(-1) + 1).astype(jnp.float32)
    w_coef = 0.5 * (plane_block.reshape(-1) + 1).astype(jnp.float32) / PLANES
    return (real_part, imag_part, row_cell, col_cell, half_width, w_coef)


def grid_part(flat, row_start, row_count, width):
    total_vis = flat[0].shape[0]
    block_len = math.gcd(total_vis, 512)
    stacked = tuple((item.reshape(total_vis // block_len, block_len) for item in flat))
    row_pos = (row_start + jnp.arange(row_count, dtype=jnp.int32)).astype(jnp.float32)
    col_pos = jnp.arange(width, dtype=jnp.int32).astype(jnp.float32)

    def step_block(total, values):
        real_part, imag_part, row_cell, col_cell, half_width, w_coef = values
        row_weights = kernel_values(
            row_pos[None, :] - row_cell[:, None], half_width[:, None], w_coef[:, None]
        ).astype(jnp.bfloat16)
        col_kern = kernel_values(
            col_pos[None, :] - col_cell[:, None], half_width[:, None], w_coef[:, None]
        )
        col_weights = jnp.concatenate(
            [real_part[:, None] * col_kern, imag_part[:, None] * col_kern], axis=1
        ).astype(jnp.bfloat16)
        product = lax.dot_general(
            row_weights, col_weights, (((0,), (0,)), ((), ())), preferred_element_type=jnp.float32
        )
        return (total + product, None)

    start_total = jnp.zeros((row_count, 2 * width), jnp.float32)
    total, _ = lax.scan(step_block, start_total, stacked)
    return total.reshape(row_count, 2, width)


def any_cells(visibilities, cell_offsets, support_index, w_plane, live_counts):
    tiles, parts = lax.axis_size("tile"), lax.axis_size("chan")
    share = G // parts
    first_row = lax.axis_index("chan") * share - M
    held = jnp.stack(
        flatten_groups(visibilities[0], cell_offsets[0], support_index[0], w_plane[0], live_counts[0])
    )

    def step(_, carry):
        total, held = carry
        total = total + grid_part(held, first_row, share + 2 * M, G)
        return total, lax.ppermute(held, "chan", [(i, (i + 1) % parts) for i in range(parts)])

    total, _ = lax.fori_loop(0, parts, step, (jnp.zeros((share + 2 * M, 2, G), F32), held))
    last = parts - 1
    left_in = lax.ppermute(
        total[share + M :], ("tile", "chan"), [(t * parts + last, (t + 1) * parts) for t in range(tiles - 1)]
    )
    right_in = lax.ppermute(
        total[:M], ("tile", "chan"), [(t * parts, (t - 1) * parts + last) for t in range(1, tiles)]
    )
    owned = total[M : M + share]
    return owned.at[:M].add(left_in).at[share - M :].add(right_in)


def class_table():
    shape = (2 * M, 4 * PLANES)
    klass = lax.broadcasted_iota(jnp.int32, shape, 1)
    distance = jnp.abs(lax.broadcasted_iota(jnp.int32, shape, 0) - M).astype(F32)
    half = (8 * (klass // PLANES + 1)).astype(F32)
    w_coef = 0.5 * (klass % PLANES + 1).astype(F32) / PLANES
    ratio = jnp.minimum(distance / half, 1.0)
    square = ratio * ratio
    radius = jnp.sqrt(jnp.maximum(1.0 - square, 0.0))
    bessel = bessel_zero(BETA * radius) / bessel_zero(jnp.full(shape, BETA, F32))
    taper = jnp.cos(jnp.pi * w_coef * square)
    return jnp.where(ratio < 1.0, bessel * taper, 0.0).astype(BF16)


def turned(values, by, sub):
    for bit in (32, 16, 8):
        chosen = (by & bit) != 0
        values = [jnp.where(chosen, values[(k - bit // 8) % 8], values[k]) for k in range(8)]
    fine = by & 7
    taken = [jnp.take_along_axis(x, (sub - fine) & 7, axis=0, mode="promise_in_bounds") for x in values]
    wrapped = sub < fine
    return [jnp.where(wrapped, taken[(k - 1) % 8], taken[k]) for k in range(8)]


def lay(klass, row, col, re, im, table, weights, columns, start=0):
    sub = lax.broadcasted_iota(jnp.int32, klass.shape, 0)
    hot = jnp.concatenate([(klass == sub + 8 * k).astype(F32) for k in range(8)], axis=0).astype(BF16)
    values = jnp.dot(table[...], hot, preferred_element_type=F32)
    values = [values[8 * k : 8 * k + 8] for k in range(8)]
    by, first = row & 63, row >> 6
    mine = [
        jnp.where(jnp.where(sub + 8 * k < by, first + 1, first) == 0, x, 0.0)
        for k, x in enumerate(turned(values, by, sub))
    ]
    weights[0:64] = jnp.concatenate([x * re for x in mine], axis=0).astype(BF16)
    weights[64:128] = jnp.concatenate([x * im for x in mine], axis=0).astype(BF16)
    by, first = col & 63, col >> 6
    window = jnp.concatenate(turned(values, by, sub), axis=0).astype(BF16)
    block = jnp.concatenate(
        [jnp.where(sub + 8 * k < by, first + 1, first).astype(F32) for k in range(8)], axis=0).astype(BF16)
    for b in range(columns.shape[0] // 64):
        columns[64 * b : 64 * b + 64] = jnp.where(block == jnp.asarray(start + b, BF16), window, jnp.asarray(0, BF16))


def add(total, weights, columns, start=0):
    stop = 64 * start + columns.shape[0]
    total[:, 64 * start : stop] += lax.dot_general(
        weights[...], columns[...], (((1,), (1,)), ((), ())), preferred_element_type=F32)


def list_left(got, edge, real, whole, number):
    c = lax.axis_index("chan")
    nc, per = got.shape[0], got.shape[1]
    main = nc * per
    count = main + nc * 8
    left = 4 * real.shape[1]
    quarter = left // 4

    lanes = lax.broadcasted_iota(jnp.int32, (1, 256), 1) // LOW
    both = jnp.concatenate([got[...].reshape(main, 256), edge[...].reshape(nc * 8, 256)], axis=0)
    index = lax.broadcasted_iota(jnp.int32, (count, 256), 0)
    shift = jnp.where(index < main, BUCKET * ((index % per) // GROUPS_IN - 1), jnp.where(c == 0, -BUCKET, 2 * BUCKET))
    both = both + jnp.where(lanes == 3, shift - 1, 0).astype(F32)
    used = jnp.max(both[:, 128:256].T[2 * LOW : 3 * LOW], axis=0, keepdims=True)
    at = lax.broadcasted_iota(jnp.int32, (1, count), 1) % GROUPS_IN
    used = jnp.where((at == EARLY[0]) | (at == EARLY[1]), 0.0, used)
    before = (
        lax.broadcasted_iota(jnp.int32, (count, count), 0) < lax.broadcasted_iota(jnp.int32, (count, count), 1)
    ).astype(F32).astype(BF16)
    rank = jnp.dot(jnp.broadcast_to(used, (8, count)).astype(BF16), before, preferred_element_type=F32)[0:1]
    rank = jnp.where(used > 0.5, rank, -1.0)
    place = lax.broadcasted_iota(jnp.int32, (left, count), 0)
    place = (4 * (place % quarter) + place // quarter).astype(F32)
    pick = jnp.where(place == rank, 1.0, 0.0).astype(BF16)
    high = both.astype(BF16)
    low = (both - high.astype(F32)).astype(BF16)
    rows = jnp.dot(pick, high, preferred_element_type=F32) + jnp.dot(pick, low, preferred_element_type=F32)
    spot = lax.broadcasted_iota(jnp.int32, (quarter, 128), 1) // LOW

    def field(f):
        part, offset = divmod(f, 4)
        result = None
        for s in range(4):
            x = rows[s * quarter : (s + 1) * quarter, 128 * part : 128 * part + 128]
            if (s - offset) % 4:
                x = pltpu.roll(x, ((s - offset) % 4) * LOW, 1)
            result = x if result is None else jnp.where(spot == s, x, result)
        return result

    real[0], real[1] = field(0), field(1)
    whole[0], whole[1] = field(2).astype(jnp.int32) - M, field(3).astype(jnp.int32) - M
    whole[2] = (field(4) * float(PLANES) + field(5)).astype(jnp.int32)
    number[...] = jnp.broadcast_to(jnp.sum(used, axis=1, keepdims=True), number.shape)


def exchange(vis, cell, sup, wpl, cnt, table, total, real, whole, number, flag, got, edge, vis_v, cell_v, sup_v, wpl_v, cnt_v, packed, tile_flags, chan_flags,
             weights, columns,
             load_sem, send_sem, recv_sem, edge_send, edge_recv, tf_send, tf_recv, cf_send, cf_recv):
    t, c = lax.axis_index("tile"), lax.axis_index("chan")
    nt, nc = lax.axis_size("tile"), lax.axis_size("chan")
    slots = vis_v.shape[-1]
    loads = [
        pltpu.make_async_copy(vis.at[0, 0], vis_v, load_sem.at[0]),
        pltpu.make_async_copy(cell.at[0, 0], cell_v, load_sem.at[1]),
        pltpu.make_async_copy(sup.at[0], sup_v, load_sem.at[2]),
        pltpu.make_async_copy(wpl.at[0], wpl_v, load_sem.at[3]),
        pltpu.make_async_copy(cnt, cnt_v, load_sem.at[4]),
    ]
    for load in loads:
        load.start()
    edge[...] = jnp.zeros_like(edge)

    bar = pltpu.get_barrier_semaphore()
    for i in range(1, nc):
        pl.semaphore_signal(bar, inc=1, device_id=(t, lax.rem(c + i, nc)), device_id_type=MESH)
    for i in range(1, nt):
        pl.semaphore_signal(bar, inc=1, device_id=(lax.rem(t + i, nt), c), device_id_type=MESH)
    from_low = (c == 0) & (t > 0)
    from_high = (c == nc - 1) & (t < nt - 1)

    @pl.when(from_low)
    def _():
        for g in range(nc):
            pl.semaphore_signal(bar, inc=1, device_id=(t - 1, g), device_id_type=MESH)

    @pl.when(from_high)
    def _():
        for g in range(nc):
            pl.semaphore_signal(bar, inc=1, device_id=(t + 1, g), device_id_type=MESH)

    for load in loads:
        load.wait()

    live = lax.broadcasted_iota(jnp.int32, (1, slots), 1) < cnt_v[...]
    row = cell_v[0:1]
    buckets = G // BUCKET
    bucket = row // BUCKET
    right = cell_v[1:2] >= G // 2
    side = jnp.where(live, bucket + jnp.where(right, buckets, 0), -1)
    hot = (lax.broadcasted_iota(jnp.int32, (2 * buckets, slots), 0) == side).astype(F32)
    step = 256
    before = (
        lax.broadcasted_iota(jnp.int32, (step, step), 0) < lax.broadcasted_iota(jnp.int32, (step, step), 1)
    ).astype(F32).astype(BF16)
    parts = []
    carry = jnp.zeros((2 * buckets, 1), F32)
    for s in range(0, slots, step):
        piece = hot[:, s : s + step]
        ahead = jnp.dot(piece.astype(BF16), before, preferred_element_type=F32) + carry
        parts.append(jnp.sum(piece * ahead, axis=0, keepdims=True))
        carry = carry + jnp.sum(piece, axis=1, keepdims=True)
    rank = jnp.concatenate(parts, axis=1).astype(jnp.int32)
    full = jnp.max(carry[:buckets] + carry[buckets:], axis=0, keepdims=True) > CAP
    full = full | (jnp.max(carry, axis=0, keepdims=True) > CAP - LOW)
    over = full.astype(F32)
    tile_flags[t] = jnp.broadcast_to(over, (1, 128))

    below, above = (t > 0).astype(jnp.int32), (t < nt - 1).astype(jnp.int32)
    pl.semaphore_wait(bar, nc - 1 + nt - 1 + below + above)

    def tile_flag(i, slot):
        return pltpu.make_async_remote_copy(
            src_ref=tile_flags.at[t], dst_ref=tile_flags.at[slot], send_sem=tf_send.at[i], recv_sem=tf_recv.at[slot],
            device_id=(lax.rem(t + i, nt), c), device_id_type=MESH)

    for i in range(1, nt):
        tile_flag(i, t).start()

    spot = jnp.where(right, CAP - 1 - rank, rank)
    group = jnp.where(live, (bucket + 1) * GROUPS_IN + (spot >> (LOW.bit_length() - 1)), -1)
    place = spot & (LOW - 1)
    groups = packed.shape[0]
    to_group = (lax.broadcasted_iota(jnp.int32, (groups, slots), 0) == group).astype(F32).astype(BF16)
    at_place = lax.broadcasted_iota(jnp.int32, (LOW, slots), 0) == place

    def halves(x):
        high = x.astype(BF16).astype(F32)
        return high, x - high

    re_hi, re_lo = halves(vis_v[0:1])
    im_hi, im_lo = halves(vis_v[1:2])
    col = cell_v[1:2]
    pieces = [re_hi, im_hi, col >> 2, sup_v[...] * PLANES + wpl_v[...], re_lo, im_lo,
              (col & 3) * 64 + (row & (BUCKET - 1)) + 1, jnp.zeros((1, slots), F32)]
    spread = jnp.concatenate([jnp.where(at_place, x.astype(F32), 0.0).astype(BF16) for x in pieces], axis=0)
    moved = lax.dot_general(to_group, spread, (((1,), (1,)), ((), ())), preferred_element_type=F32)
    first, second = moved[:, 0:128], moved[:, 128:256]
    whole_1, whole_2 = first.astype(jnp.int32), second.astype(jnp.int32)
    lane = lax.broadcasted_iota(jnp.int32, first.shape, 1) // LOW
    packed[:, 0:128] = jnp.where(
        lane < 2, first + second,
        jnp.where(lane == 2, whole_1 * 4 + (whole_2 >> 6), pltpu.roll(whole_2, LOW, 1) & 63).astype(F32))
    klass = pltpu.roll(whole_1, LOW, 1)
    packed[:, 128:256] = jnp.where(
        lane == 0, klass >> 4,
        jnp.where(lane == 1, pltpu.roll(klass, LOW, 1) & (PLANES - 1),
                  jnp.where((lane == 2) & ((whole_2 & 63) > 0), 1, 0))).astype(F32)

    width = 4 * GROUPS_IN

    def payload(peer, slot):
        return pltpu.make_async_remote_copy(
            src_ref=packed.at[pl.ds(8 * peer, width)], dst_ref=got.at[slot], send_sem=send_sem.at[peer],
            recv_sem=recv_sem.at[slot], device_id=(t, peer), device_id_type=MESH)

    order = [0, 1, 2, 3, 4, 5, 8, 9, 6, 7, 10, 11, 12, 13, 14, 15]
    for peer in order:
        @pl.when(c != peer)
        def _(peer=peer):
            payload(peer, c).start()

    def edge_up():
        return pltpu.make_async_remote_copy(
            src_ref=packed.at[pl.ds(buckets * GROUPS_IN, GROUPS_IN)], dst_ref=edge.at[c, 0:GROUPS_IN], send_sem=edge_send.at[0],
            recv_sem=edge_recv.at[c], device_id=(t + 1, 0), device_id_type=MESH)

    def edge_down():
        return pltpu.make_async_remote_copy(
            src_ref=packed.at[pl.ds(GROUPS_IN, GROUPS_IN)], dst_ref=edge.at[c, 0:GROUPS_IN], send_sem=edge_send.at[1],
            recv_sem=edge_recv.at[c], device_id=(t - 1, nc - 1), device_id_type=MESH)

    @pl.when(t < nt - 1)
    def _():
        edge_up().start()

    @pl.when(t > 0)
    def _():
        edge_down().start()

    got[c] = packed[pl.ds(pl.multiple_of(8 * c, 8), width), :]

    for i in range(1, nt):
        tile_flag(i, lax.rem(t + i, nt)).wait_recv()
    chan_flags[c] = jnp.max(tile_flags[...], axis=0)

    def chan_flag(peer, slot):
        return pltpu.make_async_remote_copy(
            src_ref=chan_flags.at[c], dst_ref=chan_flags.at[slot], send_sem=cf_send.at[peer], recv_sem=cf_recv.at[slot],
            device_id=(t, peer), device_id_type=MESH)

    for peer in order:
        @pl.when(c != peer)
        def _(peer=peer):
            chan_flag(peer, c).start()

    table[...] = class_table()
    total[...] = jnp.zeros_like(total)

    spot = lax.broadcasted_iota(jnp.int32, (8, 128), 1) // LOW

    def fields(first, second, lift, picks):
        row_lanes = lax.broadcasted_iota(jnp.int32, first.shape, 1) // LOW == 3
        cells = first.astype(jnp.int32) - M
        cells = jnp.where(row_lanes, cells + lift, cells)
        klass = (second * float(PLANES) + pltpu.roll(second, 3 * LOW, 1)).astype(jnp.int32)

        def lines(x, offset):
            shifted = [pltpu.roll(x, ((b - offset) % 4) * LOW, 1) if (b - offset) % 4 else x for b in range(4)]
            made = []
            for pick in picks:
                parts = [jnp.broadcast_to(shifted[b][r : r + 1], (8, 128)) for b, r in enumerate(pick)]
                line = parts[0]
                for b in range(1, 4):
                    line = jnp.where(spot == b, parts[b], line)
                made.append(line)
            return made

        return lines(klass, 0), lines(cells, 3), lines(cells, 2), lines(first, 0), lines(first, 1)

    halves_at = (0, G // 64 - SPAN)
    lift = BUCKET * (lax.broadcasted_iota(jnp.int32, (width, 128), 0) // GROUPS_IN - 1) - 1

    here = 2 * (c // 2)

    def chip(k):
        q = k % 4
        dz = q + jnp.where(q == 2, 1, 0) - jnp.where(q == 3, 1, 0)
        z, y = (here // 2) % 4, here // 8
        return (((y + k // 4) % 2) * 4 + (z + dz) % 4) * 2

    def prepare(source, slot):
        made = [
            fields(got[x, :, 0:128], got[x, :, 128:256], lift, [[GROUPS_IN * b + g for b in range(4)] for g in EARLY])
            for x in (source, source + 1)
        ]
        for h in range(2):
            lay(*[jnp.concatenate([x[h], y[h]], axis=1) for x, y in zip(*made)], table, weights.at[slot, h],
                columns.at[slot, h], halves_at[h])

    def add_both(slot):
        for h in range(2):
            add(total, weights.at[slot, h], columns.at[slot, h], halves_at[h])

    def arrive(source):
        pltpu.make_async_remote_copy(
            src_ref=packed.at[pl.ds(0, width)], dst_ref=got.at[source], send_sem=send_sem.at[1],
            recv_sem=recv_sem.at[source], device_id=(t, source), device_id_type=MESH).wait_recv()

    arrive(here + (c + 1) % 2)
    prepare(here, 0)

    def two_chips(j, carry):
        for odd in (1, 0):
            source = chip(2 * j + 2 - odd)
            arrive(source)
            arrive(source + 1)
            prepare(source, odd)
            add_both(1 - odd)
        return carry

    chips = nc // 2
    lax.fori_loop(0, chips // 2 - 1, two_chips, 0)
    add_both(0)

    @pl.when(from_low | from_high)
    def _():
        for g in range(nc):
            pltpu.make_async_remote_copy(
                src_ref=packed.at[pl.ds(0, GROUPS_IN)], dst_ref=edge.at[g, 0:GROUPS_IN], send_sem=edge_send.at[0],
                recv_sem=edge_recv.at[g], device_id=(t, g), device_id_type=MESH).wait_recv()
        rows = edge[...].reshape(nc * 8, 256)
        lines = nc // 4
        picks = [[8 * (4 * n + b) + g for b in range(4)] for g in EARLY for n in range(lines)]
        made = fields(rows[:, 0:128], rows[:, 128:256], jnp.where(from_low, -BUCKET, 2 * BUCKET) - 1, picks)
        for h in range(2):
            for n in range(0, lines, 2):
                lay(*[jnp.concatenate(x[h * lines + n : h * lines + n + 2], axis=1) for x in made], table,
                    weights.at[n // 2, h], columns.at[n // 2, h], halves_at[h])
        for n in range(lines // 2):
            add_both(n)

    source = chip(chips - 1)
    arrive(source)
    arrive(source + 1)
    prepare(source, 1)
    list_left(got, edge, real, whole, number)
    add_both(1)

    for peer in range(nc):
        @pl.when(c != peer)
        def _(peer=peer):
            chan_flag(peer, peer).wait_recv()
            chan_flag(peer, c).wait_send()
            payload(peer, c).wait_send()

    flag[0, 0] = (jnp.max(jnp.max(chan_flags[...], axis=0)) > 0.5).astype(jnp.int32)
    for i in range(1, nt):
        tile_flag(i, t).wait_send()

    @pl.when(t < nt - 1)
    def _():
        edge_up().wait_send()

    @pl.when(t > 0)
    def _():
        edge_down().wait_send()


def owned_rows(real, whole, number, table, begun, out, total, weights, columns):
    size = weights.shape[-1]
    lines = size // 128
    chunks = (jnp.max(number[...]).astype(jnp.int32) + 4 * lines - 1) // (4 * lines)
    total[...] = begun[...]

    def body(i, carry):
        def line(ref, f):
            return jnp.concatenate(
                [jnp.broadcast_to(ref[f, pl.ds(lines * i + h, 1), :], (8, 128)) for h in range(lines)], axis=1)

        lay(line(whole, 2), line(whole, 1), line(whole, 0), line(real, 0), line(real, 1), table, weights, columns)
        add(total, weights, columns)
        return carry

    lax.fori_loop(0, chunks, body, 0)
    out[:, 0, :] = total[0:64]
    out[:, 1, :] = total[64:128]


def per_device(visibilities, cell_offsets, support_index, w_plane, live_counts):
    nt, nc = lax.axis_size("tile"), lax.axis_size("chan")
    slots = visibilities.shape[-1]
    groups = (G // BUCKET + 2) * GROUPS_IN
    vmem = pl.BlockSpec(memory_space=pltpu.VMEM)
    left_lines = nc * 5 * (GROUPS_IN - len(EARLY)) // 4
    table, begun, real, whole, number, flag = pl.pallas_call(
        exchange,
        out_shape=(
            jax.ShapeDtypeStruct((2 * M, 4 * PLANES), BF16),
            jax.ShapeDtypeStruct((2 * G // nc, G), F32),
            jax.ShapeDtypeStruct((2, left_lines, 128), F32),
            jax.ShapeDtypeStruct((3, left_lines, 128), jnp.int32),
            jax.ShapeDtypeStruct((8, 128), F32),
            jax.ShapeDtypeStruct((1, 1), jnp.int32),
        ),
        in_specs=[pl.BlockSpec(memory_space=pltpu.MemorySpace.HBM)] * 5,
        out_specs=(vmem, vmem, vmem, vmem, vmem, pl.BlockSpec(memory_space=pltpu.SMEM)),
        scratch_shapes=[
            pltpu.VMEM((nc, 4 * GROUPS_IN, FIELDS * LOW), F32),
            pltpu.VMEM((nc, 8, FIELDS * LOW), F32),
            pltpu.VMEM((2, slots), F32),
            pltpu.VMEM((2, slots), jnp.int32),
            pltpu.VMEM((1, slots), jnp.int32),
            pltpu.VMEM((1, slots), jnp.int32),
            pltpu.VMEM((1, 1), jnp.int32),
            pltpu.VMEM((groups, FIELDS * LOW), F32),
            pltpu.VMEM((nt, 1, 128), F32),
            pltpu.VMEM((nc, 1, 128), F32),
            pltpu.VMEM((2, 2, 2 * G // nc, 256), BF16),
            pltpu.VMEM((2, 2, 64 * SPAN, 256), BF16),
            pltpu.SemaphoreType.DMA((5,)),
            pltpu.SemaphoreType.DMA((nc,)),
            pltpu.SemaphoreType.DMA((nc,)),
            pltpu.SemaphoreType.DMA((2,)),
            pltpu.SemaphoreType.DMA((nc,)),
            pltpu.SemaphoreType.DMA((nt,)),
            pltpu.SemaphoreType.DMA((nt,)),
            pltpu.SemaphoreType.DMA((nc,)),
            pltpu.SemaphoreType.DMA((nc,)),
        ],
        compiler_params=pltpu.CompilerParams(collective_id=0, has_side_effects=True, vmem_limit_bytes=62 << 20),
    )(visibilities, cell_offsets, support_index, w_plane, live_counts)


    def usual(*_):
        return pl.pallas_call(
            owned_rows,
            out_shape=jax.ShapeDtypeStruct((G // nc, 2, G), F32),
            in_specs=[vmem] * 5,
            out_specs=vmem,
            scratch_shapes=[
                pltpu.VMEM((2 * G // nc, G), F32),
                pltpu.VMEM((2 * G // nc, 512), BF16),
                pltpu.VMEM((G, 512), BF16),
            ],
            compiler_params=pltpu.CompilerParams(vmem_limit_bytes=40 << 20),
        )(real, whole, number, table, begun)

    return lax.switch(
        flag[0, 0], (usual, any_cells), visibilities, cell_offsets, support_index, w_plane, live_counts
    )


def solution(mesh):
    in_specs = (
        P("tile", "chan", None, None),
        P("tile", "chan", None, None),
        P("tile", "chan", None),
        P("tile", "chan", None),
        P("tile", "chan"),
    )
    out_specs = P(("tile", "chan"), None, None)
    return jax.shard_map(
        per_device, mesh=mesh, in_specs=in_specs, out_specs=out_specs, check_vma=False
    )
```

```python
import functools
import math

import jax
import jax.numpy as jnp
from jax import lax
from jax.experimental import pallas as pl
from jax.experimental.pallas import tpu as pltpu
from jax.sharding import PartitionSpec as P

G = 1024
M = 32
PLANES = 16
BETA = 7.0

BUCKET = 32
CAP = 128
LOW = 32
GROUPS_IN = CAP // LOW
EARLY = (0, GROUPS_IN - 1)
SPAN = 10
FIELDS = 8
MESH = pl.DeviceIdType.MESH
F32 = jnp.float32
BF16 = jnp.bfloat16


def bessel_zero(value):
    quarter = value * value * 0.25
    term = jnp.ones_like(value)
    total = jnp.ones_like(value)
    for index in range(1, 30):
        term = term * quarter * (1.0 / float(index * index))
        total = total + term
    return total


def kernel_values(distance, half_width, w_coef):
    ratio = distance / half_width
    inside = jnp.abs(ratio) < 1.0
    radius = jnp.sqrt(jnp.maximum(1.0 - ratio * ratio, 0.0))
    bessel = bessel_zero(BETA * radius) / bessel_zero(jnp.float32(BETA))
    taper = jnp.cos(jnp.pi * w_coef * ratio * ratio)
    return jnp.where(inside, bessel * taper, jnp.float32(0.0))


def flatten_groups(vis_block, offset_block, support_block, plane_block, count_block):
    slot_total = vis_block.shape[-1]
    slot_ids = jnp.arange(slot_total, dtype=jnp.int32)
    live = (slot_ids[None, :] < count_block[:, None]).astype(jnp.float32).reshape(-1)
    real_part = vis_block[:, 0].reshape(-1) * live
    imag_part = vis_block[:, 1].reshape(-1) * live
    row_cell = offset_block[:, 0].reshape(-1).astype(jnp.float32)
    col_cell = offset_block[:, 1].reshape(-1).astype(jnp.float32)
    half_width = 8.0 * (support_block.reshape(-1) + 1).astype(jnp.float32)
    w_coef = 0.5 * (plane_block.reshape(-1) + 1).astype(jnp.float32) / PLANES
    return (real_part, imag_part, row_cell, col_cell, half_width, w_coef)


def grid_part(flat, row_start, row_count, width):
    total_vis = flat[0].shape[0]
    block_len = math.gcd(total_vis, 512)
    stacked = tuple((item.reshape(total_vis // block_len, block_len) for item in flat))
    row_pos = (row_start + jnp.arange(row_count, dtype=jnp.int32)).astype(jnp.float32)
    col_pos = jnp.arange(width, dtype=jnp.int32).astype(jnp.float32)

    def step_block(total, values):
        real_part, imag_part, row_cell, col_cell, half_width, w_coef = values
        row_weights = kernel_values(
            row_pos[None, :] - row_cell[:, None], half_width[:, None], w_coef[:, None]
        ).astype(jnp.bfloat16)
        col_kern = kernel_values(
            col_pos[None, :] - col_cell[:, None], half_width[:, None], w_coef[:, None]
        )
        col_weights = jnp.concatenate(
            [real_part[:, None] * col_kern, imag_part[:, None] * col_kern], axis=1
        ).astype(jnp.bfloat16)
        product = lax.dot_general(
            row_weights, col_weights, (((0,), (0,)), ((), ())), preferred_element_type=jnp.float32
        )
        return (total + product, None)

    start_total = jnp.zeros((row_count, 2 * width), jnp.float32)
    total, _ = lax.scan(step_block, start_total, stacked)
    return total.reshape(row_count, 2, width)


def any_cells(visibilities, cell_offsets, support_index, w_plane, live_counts):
    tiles, parts = lax.axis_size("tile"), lax.axis_size("chan")
    share = G // parts
    first_row = lax.axis_index("chan") * share - M
    held = jnp.stack(
        flatten_groups(visibilities[0], cell_offsets[0], support_index[0], w_plane[0], live_counts[0])
    )

    def step(_, carry):
        total, held = carry
        total = total + grid_part(held, first_row, share + 2 * M, G)
        return total, lax.ppermute(held, "chan", [(i, (i + 1) % parts) for i in range(parts)])

    total, _ = lax.fori_loop(0, parts, step, (jnp.zeros((share + 2 * M, 2, G), F32), held))
    last = parts - 1
    left_in = lax.ppermute(
        total[share + M :], ("tile", "chan"), [(t * parts + last, (t + 1) * parts) for t in range(tiles - 1)]
    )
    right_in = lax.ppermute(
        total[:M], ("tile", "chan"), [(t * parts, (t - 1) * parts + last) for t in range(1, tiles)]
    )
    owned = total[M : M + share]
    return owned.at[:M].add(left_in).at[share - M :].add(right_in)


def class_table():
    shape = (2 * M, 4 * PLANES)
    klass = lax.broadcasted_iota(jnp.int32, shape, 1)
    distance = jnp.abs(lax.broadcasted_iota(jnp.int32, shape, 0) - M).astype(F32)
    half = (8 * (klass // PLANES + 1)).astype(F32)
    w_coef = 0.5 * (klass % PLANES + 1).astype(F32) / PLANES
    ratio = jnp.minimum(distance / half, 1.0)
    square = ratio * ratio
    radius = jnp.sqrt(jnp.maximum(1.0 - square, 0.0))
    bessel = bessel_zero(BETA * radius) / bessel_zero(jnp.full(shape, BETA, F32))
    taper = jnp.cos(jnp.pi * w_coef * square)
    return jnp.where(ratio < 1.0, bessel * taper, 0.0).astype(BF16)


def turned(values, by, sub):
    for bit in (32, 16, 8):
        chosen = (by & bit) != 0
        values = [jnp.where(chosen, values[(k - bit // 8) % 8], values[k]) for k in range(8)]
    fine = by & 7
    taken = [jnp.take_along_axis(x, (sub - fine) & 7, axis=0, mode="promise_in_bounds") for x in values]
    wrapped = sub < fine
    return [jnp.where(wrapped, taken[(k - 1) % 8], taken[k]) for k in range(8)]


def lay(klass, row, col, re, im, table, weights, columns, start=0):
    sub = lax.broadcasted_iota(jnp.int32, klass.shape, 0)
    hot = jnp.concatenate([(klass == sub + 8 * k).astype(F32) for k in range(8)], axis=0).astype(BF16)
    values = jnp.dot(table[...], hot, preferred_element_type=F32)
    values = [values[8 * k : 8 * k + 8] for k in range(8)]
    by, first = row & 63, row >> 6
    mine = [
        jnp.where(jnp.where(sub + 8 * k < by, first + 1, first) == 0, x, 0.0)
        for k, x in enumerate(turned(values, by, sub))
    ]
    weights[0:64] = jnp.concatenate([x * re for x in mine], axis=0).astype(BF16)
    weights[64:128] = jnp.concatenate([x * im for x in mine], axis=0).astype(BF16)
    by, first = col & 63, col >> 6
    window = jnp.concatenate(turned(values, by, sub), axis=0).astype(BF16)
    block = jnp.concatenate(
        [jnp.where(sub + 8 * k < by, first + 1, first).astype(F32) for k in range(8)], axis=0).astype(BF16)
    for b in range(columns.shape[0] // 64):
        columns[64 * b : 64 * b + 64] = jnp.where(block == jnp.asarray(start + b, BF16), window, jnp.asarray(0, BF16))


def add(total, weights, columns, start=0):
    stop = 64 * start + columns.shape[0]
    total[:, 64 * start : stop] += lax.dot_general(
        weights[...], columns[...], (((1,), (1,)), ((), ())), preferred_element_type=F32)


def list_left(got, edge, real, whole, number):
    c = lax.axis_index("chan")
    nc, per = got.shape[0], got.shape[1]
    main = nc * per
    count = main + nc * 8
    left = 4 * real.shape[1]
    quarter = left // 4

    lanes = lax.broadcasted_iota(jnp.int32, (1, 256), 1) // LOW
    both = jnp.concatenate([got[...].reshape(main, 256), edge[...].reshape(nc * 8, 256)], axis=0)
    index = lax.broadcasted_iota(jnp.int32, (count, 256), 0)
    shift = jnp.where(index < main, BUCKET * ((index % per) // GROUPS_IN - 1), jnp.where(c == 0, -BUCKET, 2 * BUCKET))
    both = both + jnp.where(lanes == 3, shift - 1, 0).astype(F32)
    used = jnp.max(both[:, 128:256].T[2 * LOW : 3 * LOW], axis=0, keepdims=True)
    at = lax.broadcasted_iota(jnp.int32, (1, count), 1) % GROUPS_IN
    used = jnp.where((at == EARLY[0]) | (at == EARLY[1]), 0.0, used)
    before = (
        lax.broadcasted_iota(jnp.int32, (count, count), 0) < lax.broadcasted_iota(jnp.int32, (count, count), 1)
    ).astype(F32).astype(BF16)
    rank = jnp.dot(jnp.broadcast_to(used, (8, count)).astype(BF16), before, preferred_element_type=F32)[0:1]
    rank = jnp.where(used > 0.5, rank, -1.0)
    place = lax.broadcasted_iota(jnp.int32, (left, count), 0)
    place = (4 * (place % quarter) + place // quarter).astype(F32)
    pick = jnp.where(place == rank, 1.0, 0.0).astype(BF16)
    high = both.astype(BF16)
    low = (both - high.astype(F32)).astype(BF16)
    rows = jnp.dot(pick, high, preferred_element_type=F32) + jnp.dot(pick, low, preferred_element_type=F32)
    spot = lax.broadcasted_iota(jnp.int32, (quarter, 128), 1) // LOW

    def field(f):
        part, offset = divmod(f, 4)
        result = None
        for s in range(4):
            x = rows[s * quarter : (s + 1) * quarter, 128 * part : 128 * part + 128]
            if (s - offset) % 4:
                x = pltpu.roll(x, ((s - offset) % 4) * LOW, 1)
            result = x if result is None else jnp.where(spot == s, x, result)
        return result

    real[0], real[1] = field(0), field(1)
    whole[0], whole[1] = field(2).astype(jnp.int32) - M, field(3).astype(jnp.int32) - M
    whole[2] = (field(4) * float(PLANES) + field(5)).astype(jnp.int32)
    number[...] = jnp.broadcast_to(jnp.sum(used, axis=1, keepdims=True), number.shape)


def exchange(vis, cell, sup, wpl, cnt, table, total, real, whole, number, flag, got, edge, vis_v, cell_v, sup_v, wpl_v, cnt_v, packed, tile_flags, chan_flags,
             weights, columns,
             load_sem, send_sem, recv_sem, edge_send, edge_recv, tf_send, tf_recv, cf_send, cf_recv):
    t, c = lax.axis_index("tile"), lax.axis_index("chan")
    nt, nc = lax.axis_size("tile"), lax.axis_size("chan")
    slots = vis_v.shape[-1]
    loads = [
        pltpu.make_async_copy(vis.at[0, 0], vis_v, load_sem.at[0]),
        pltpu.make_async_copy(cell.at[0, 0], cell_v, load_sem.at[1]),
        pltpu.make_async_copy(sup.at[0], sup_v, load_sem.at[2]),
        pltpu.make_async_copy(wpl.at[0], wpl_v, load_sem.at[3]),
        pltpu.make_async_copy(cnt, cnt_v, load_sem.at[4]),
    ]
    for load in loads:
        load.start()
    edge[...] = jnp.zeros_like(edge)

    bar = pltpu.get_barrier_semaphore()
    for i in range(1, nc):
        pl.semaphore_signal(bar, inc=1, device_id=(t, lax.rem(c + i, nc)), device_id_type=MESH)
    for i in range(1, nt):
        pl.semaphore_signal(bar, inc=1, device_id=(lax.rem(t + i, nt), c), device_id_type=MESH)
    from_low = (c == 0) & (t > 0)
    from_high = (c == nc - 1) & (t < nt - 1)

    @pl.when(from_low)
    def _():
        for g in range(nc):
            pl.semaphore_signal(bar, inc=1, device_id=(t - 1, g), device_id_type=MESH)

    @pl.when(from_high)
    def _():
        for g in range(nc):
            pl.semaphore_signal(bar, inc=1, device_id=(t + 1, g), device_id_type=MESH)

    for load in loads:
        load.wait()

    live = lax.broadcasted_iota(jnp.int32, (1, slots), 1) < cnt_v[...]
    row = cell_v[0:1]
    buckets = G // BUCKET
    bucket = row // BUCKET
    right = cell_v[1:2] >= G // 2
    side = jnp.where(live, bucket + jnp.where(right, buckets, 0), -1)
    hot = (lax.broadcasted_iota(jnp.int32, (2 * buckets, slots), 0) == side).astype(F32)
    step = 256
    before = (
        lax.broadcasted_iota(jnp.int32, (step, step), 0) < lax.broadcasted_iota(jnp.int32, (step, step), 1)
    ).astype(F32).astype(BF16)
    parts = []
    carry = jnp.zeros((2 * buckets, 1), F32)
    for s in range(0, slots, step):
        piece = hot[:, s : s + step]
        ahead = jnp.dot(piece.astype(BF16), before, preferred_element_type=F32) + carry
        parts.append(jnp.sum(piece * ahead, axis=0, keepdims=True))
        carry = carry + jnp.sum(piece, axis=1, keepdims=True)
    rank = jnp.concatenate(parts, axis=1).astype(jnp.int32)
    full = jnp.max(carry[:buckets] + carry[buckets:], axis=0, keepdims=True) > CAP
    full = full | (jnp.max(carry, axis=0, keepdims=True) > CAP - LOW)
    over = full.astype(F32)
    tile_flags[t] = jnp.broadcast_to(over, (1, 128))

    below, above = (t > 0).astype(jnp.int32), (t < nt - 1).astype(jnp.int32)
    pl.semaphore_wait(bar, nc - 1 + nt - 1 + below + above)

    def tile_flag(i, slot):
        return pltpu.make_async_remote_copy(
            src_ref=tile_flags.at[t], dst_ref=tile_flags.at[slot], send_sem=tf_send, recv_sem=tf_recv,
            device_id=(lax.rem(t + i, nt), c), device_id_type=MESH)

    for i in range(1, nt):
        tile_flag(i, t).start()

    spot = jnp.where(right, CAP - 1 - rank, rank)
    group = jnp.where(live, (bucket + 1) * GROUPS_IN + (spot >> (LOW.bit_length() - 1)), -1)
    place = spot & (LOW - 1)
    groups = packed.shape[0]
    to_group = (lax.broadcasted_iota(jnp.int32, (groups, slots), 0) == group).astype(F32).astype(BF16)
    at_place = lax.broadcasted_iota(jnp.int32, (LOW, slots), 0) == place

    def halves(x):
        high = x.astype(BF16).astype(F32)
        return high, x - high

    re_hi, re_lo = halves(vis_v[0:1])
    im_hi, im_lo = halves(vis_v[1:2])
    col = cell_v[1:2]
    pieces = [re_hi, im_hi, col >> 2, sup_v[...] * PLANES + wpl_v[...], re_lo, im_lo,
              (col & 3) * 64 + (row & (BUCKET - 1)) + 1, jnp.zeros((1, slots), F32)]
    spread = jnp.concatenate([jnp.where(at_place, x.astype(F32), 0.0).astype(BF16) for x in pieces], axis=0)
    moved = lax.dot_general(to_group, spread, (((1,), (1,)), ((), ())), preferred_element_type=F32)
    first, second = moved[:, 0:128], moved[:, 128:256]
    whole_1, whole_2 = first.astype(jnp.int32), second.astype(jnp.int32)
    lane = lax.broadcasted_iota(jnp.int32, first.shape, 1) // LOW
    packed[:, 0:128] = jnp.where(
        lane < 2, first + second,
        jnp.where(lane == 2, whole_1 * 4 + (whole_2 >> 6), pltpu.roll(whole_2, LOW, 1) & 63).astype(F32))
    klass = pltpu.roll(whole_1, LOW, 1)
    packed[:, 128:256] = jnp.where(
        lane == 0, klass >> 4,
        jnp.where(lane == 1, pltpu.roll(klass, LOW, 1) & (PLANES - 1),
                  jnp.where((lane == 2) & ((whole_2 & 63) > 0), 1, 0))).astype(F32)

    width = 4 * GROUPS_IN

    def payload(peer, slot):
        return pltpu.make_async_remote_copy(
            src_ref=packed.at[pl.ds(8 * peer, width)], dst_ref=got.at[slot], send_sem=send_sem,
            recv_sem=recv_sem.at[slot], device_id=(t, peer), device_id_type=MESH)

    order = [0, 1, 2, 3, 4, 5, 8, 9, 6, 7, 10, 11, 12, 13, 14, 15]
    for peer in order:
        @pl.when(c != peer)
        def _(peer=peer):
            payload(peer, c).start()

    def edge_up():
        return pltpu.make_async_remote_copy(
            src_ref=packed.at[pl.ds(buckets * GROUPS_IN, GROUPS_IN)], dst_ref=edge.at[c, 0:GROUPS_IN], send_sem=edge_send.at[0],
            recv_sem=edge_recv.at[c], device_id=(t + 1, 0), device_id_type=MESH)

    def edge_down():
        return pltpu.make_async_remote_copy(
            src_ref=packed.at[pl.ds(GROUPS_IN, GROUPS_IN)], dst_ref=edge.at[c, 0:GROUPS_IN], send_sem=edge_send.at[1],
            recv_sem=edge_recv.at[c], device_id=(t - 1, nc - 1), device_id_type=MESH)

    @pl.when(t < nt - 1)
    def _():
        edge_up().start()

    @pl.when(t > 0)
    def _():
        edge_down().start()

    got[c] = packed[pl.ds(pl.multiple_of(8 * c, 8), width), :]

    def all_of(ref, count, sent, landed):
        return pltpu.make_async_remote_copy(
            src_ref=ref.at[0:count], dst_ref=ref.at[0:count], send_sem=sent, recv_sem=landed,
            device_id=(t, lax.rem(c + 1, nc)), device_id_type=MESH)

    all_of(tile_flags, nt - 1, tf_send, tf_recv).wait_recv()
    chan_flags[c] = jnp.max(tile_flags[...], axis=0)

    def chan_flag(peer, slot):
        return pltpu.make_async_remote_copy(
            src_ref=chan_flags.at[c], dst_ref=chan_flags.at[slot], send_sem=cf_send, recv_sem=cf_recv,
            device_id=(t, peer), device_id_type=MESH)

    for peer in order:
        @pl.when(c != peer)
        def _(peer=peer):
            chan_flag(peer, c).start()

    table[...] = class_table()
    total[...] = jnp.zeros_like(total)

    spot = lax.broadcasted_iota(jnp.int32, (8, 128), 1) // LOW

    def fields(first, second, lift, picks):
        row_lanes = lax.broadcasted_iota(jnp.int32, first.shape, 1) // LOW == 3
        cells = first.astype(jnp.int32) - M
        cells = jnp.where(row_lanes, cells + lift, cells)
        klass = (second * float(PLANES) + pltpu.roll(second, 3 * LOW, 1)).astype(jnp.int32)

        def lines(x, offset):
            shifted = [pltpu.roll(x, ((b - offset) % 4) * LOW, 1) if (b - offset) % 4 else x for b in range(4)]
            made = []
            for pick in picks:
                parts = [jnp.broadcast_to(shifted[b][r : r + 1], (8, 128)) for b, r in enumerate(pick)]
                line = parts[0]
                for b in range(1, 4):
                    line = jnp.where(spot == b, parts[b], line)
                made.append(line)
            return made

        return lines(klass, 0), lines(cells, 3), lines(cells, 2), lines(first, 0), lines(first, 1)

    halves_at = (0, G // 64 - SPAN)
    lift = BUCKET * (lax.broadcasted_iota(jnp.int32, (width, 128), 0) // GROUPS_IN - 1) - 1

    here = 2 * (c // 2)

    def chip(k):
        q = k % 4
        dz = q + jnp.where(q == 2, 1, 0) - jnp.where(q == 3, 1, 0)
        z, y = (here // 2) % 4, here // 8
        return (((y + k // 4) % 2) * 4 + (z + dz) % 4) * 2

    def prepare(source, slot):
        made = [
            fields(got[x, :, 0:128], got[x, :, 128:256], lift, [[GROUPS_IN * b + g for b in range(4)] for g in EARLY])
            for x in (source, source + 1)
        ]
        for h in range(2):
            lay(*[jnp.concatenate([x[h], y[h]], axis=1) for x, y in zip(*made)], table, weights.at[slot, h],
                columns.at[slot, h], halves_at[h])

    def add_both(slot):
        for h in range(2):
            add(total, weights.at[slot, h], columns.at[slot, h], halves_at[h])

    def arrive(source):
        pltpu.make_async_remote_copy(
            src_ref=packed.at[pl.ds(0, width)], dst_ref=got.at[source], send_sem=send_sem,
            recv_sem=recv_sem.at[source], device_id=(t, source), device_id_type=MESH).wait_recv()

    arrive(here + (c + 1) % 2)
    prepare(here, 0)

    def two_chips(j, carry):
        for odd in (1, 0):
            source = chip(2 * j + 2 - odd)
            arrive(source)
            arrive(source + 1)
            prepare(source, odd)
            add_both(1 - odd)
        return carry

    chips = nc // 2
    lax.fori_loop(0, chips // 2 - 1, two_chips, 0)
    add_both(0)

    @pl.when(from_low | from_high)
    def _():
        for g in range(nc):
            pltpu.make_async_remote_copy(
                src_ref=packed.at[pl.ds(0, GROUPS_IN)], dst_ref=edge.at[g, 0:GROUPS_IN], send_sem=edge_send.at[0],
                recv_sem=edge_recv.at[g], device_id=(t, g), device_id_type=MESH).wait_recv()
        rows = edge[...].reshape(nc * 8, 256)
        lines = nc // 4
        picks = [[8 * (4 * n + b) + g for b in range(4)] for g in EARLY for n in range(lines)]
        made = fields(rows[:, 0:128], rows[:, 128:256], jnp.where(from_low, -BUCKET, 2 * BUCKET) - 1, picks)
        for h in range(2):
            for n in range(0, lines, 2):
                lay(*[jnp.concatenate(x[h * lines + n : h * lines + n + 2], axis=1) for x in made], table,
                    weights.at[n // 2, h], columns.at[n // 2, h], halves_at[h])
        for n in range(lines // 2):
            add_both(n)

    all_of(tile_flags, nt - 1, tf_send, tf_recv).wait_send()
    all_of(chan_flags, nc - 1, cf_send, cf_recv).wait_send()
    all_of(got, nc - 1, send_sem, recv_sem.at[0]).wait_send()

    @pl.when(t < nt - 1)
    def _():
        edge_up().wait_send()

    @pl.when(t > 0)
    def _():
        edge_down().wait_send()

    source = chip(chips - 1)
    arrive(source)
    arrive(source + 1)
    prepare(source, 1)
    list_left(got, edge, real, whole, number)
    add_both(1)

    all_of(chan_flags, nc - 1, cf_send, cf_recv).wait_recv()
    flag[0, 0] = (jnp.max(jnp.max(chan_flags[...], axis=0)) > 0.5).astype(jnp.int32)


def owned_rows(real, whole, number, table, begun, out, total, weights, columns):
    size = weights.shape[-1]
    lines = size // 128
    chunks = (jnp.max(number[...]).astype(jnp.int32) + 4 * lines - 1) // (4 * lines)
    total[...] = begun[...]

    def body(i, carry):
        def line(ref, f):
            return jnp.concatenate(
                [jnp.broadcast_to(ref[f, pl.ds(lines * i + h, 1), :], (8, 128)) for h in range(lines)], axis=1)

        lay(line(whole, 2), line(whole, 1), line(whole, 0), line(real, 0), line(real, 1), table, weights, columns)
        add(total, weights, columns)
        return carry

    lax.fori_loop(0, chunks, body, 0)
    out[:, 0, :] = total[0:64]
    out[:, 1, :] = total[64:128]


def per_device(visibilities, cell_offsets, support_index, w_plane, live_counts):
    nt, nc = lax.axis_size("tile"), lax.axis_size("chan")
    slots = visibilities.shape[-1]
    groups = (G // BUCKET + 2) * GROUPS_IN
    vmem = pl.BlockSpec(memory_space=pltpu.VMEM)
    left_lines = nc * 5 * (GROUPS_IN - len(EARLY)) // 4
    table, begun, real, whole, number, flag = pl.pallas_call(
        exchange,
        out_shape=(
            jax.ShapeDtypeStruct((2 * M, 4 * PLANES), BF16),
            jax.ShapeDtypeStruct((2 * G // nc, G), F32),
            jax.ShapeDtypeStruct((2, left_lines, 128), F32),
            jax.ShapeDtypeStruct((3, left_lines, 128), jnp.int32),
            jax.ShapeDtypeStruct((8, 128), F32),
            jax.ShapeDtypeStruct((1, 1), jnp.int32),
        ),
        in_specs=[pl.BlockSpec(memory_space=pltpu.MemorySpace.HBM)] * 5,
        out_specs=(vmem, vmem, vmem, vmem, vmem, pl.BlockSpec(memory_space=pltpu.SMEM)),
        scratch_shapes=[
            pltpu.VMEM((nc, 4 * GROUPS_IN, FIELDS * LOW), F32),
            pltpu.VMEM((nc, 8, FIELDS * LOW), F32),
            pltpu.VMEM((2, slots), F32),
            pltpu.VMEM((2, slots), jnp.int32),
            pltpu.VMEM((1, slots), jnp.int32),
            pltpu.VMEM((1, slots), jnp.int32),
            pltpu.VMEM((1, 1), jnp.int32),
            pltpu.VMEM((groups, FIELDS * LOW), F32),
            pltpu.VMEM((nt, 1, 128), F32),
            pltpu.VMEM((nc, 1, 128), F32),
            pltpu.VMEM((2, 2, 2 * G // nc, 256), BF16),
            pltpu.VMEM((2, 2, 64 * SPAN, 256), BF16),
            pltpu.SemaphoreType.DMA((5,)),
            pltpu.SemaphoreType.DMA,
            pltpu.SemaphoreType.DMA((nc,)),
            pltpu.SemaphoreType.DMA((2,)),
            pltpu.SemaphoreType.DMA((nc,)),
            pltpu.SemaphoreType.DMA,
            pltpu.SemaphoreType.DMA,
            pltpu.SemaphoreType.DMA,
            pltpu.SemaphoreType.DMA,
        ],
        compiler_params=pltpu.CompilerParams(collective_id=0, has_side_effects=True, vmem_limit_bytes=62 << 20),
    )(visibilities, cell_offsets, support_index, w_plane, live_counts)


    def usual(*_):
        return pl.pallas_call(
            owned_rows,
            out_shape=jax.ShapeDtypeStruct((G // nc, 2, G), F32),
            in_specs=[vmem] * 5,
            out_specs=vmem,
            scratch_shapes=[
                pltpu.VMEM((2 * G // nc, G), F32),
                pltpu.VMEM((2 * G // nc, 512), BF16),
                pltpu.VMEM((G, 512), BF16),
            ],
            compiler_params=pltpu.CompilerParams(vmem_limit_bytes=40 << 20),
        )(real, whole, number, table, begun)

    return lax.switch(
        flag[0, 0], (usual, any_cells), visibilities, cell_offsets, support_index, w_plane, live_counts
    )


def solution(mesh):
    in_specs = (
        P("tile", "chan", None, None),
        P("tile", "chan", None, None),
        P("tile", "chan", None),
        P("tile", "chan", None),
        P("tile", "chan"),
    )
    out_specs = P(("tile", "chan"), None, None)
    return jax.shard_map(
        per_device, mesh=mesh, in_specs=in_specs, out_specs=out_specs, check_vma=False
    )
```

```python
import functools
import math

import jax
import jax.numpy as jnp
from jax import lax
from jax.experimental import pallas as pl
from jax.experimental.pallas import tpu as pltpu
from jax.sharding import PartitionSpec as P

G = 1024
M = 32
PLANES = 16
BETA = 7.0

BUCKET = 32
CAP = 128
LOW = 32
GROUPS_IN = CAP // LOW
EARLY = (0, GROUPS_IN - 1)
SPAN = 10
FIELDS = 8
MESH = pl.DeviceIdType.MESH
F32 = jnp.float32
BF16 = jnp.bfloat16


def bessel_zero(value):
    quarter = value * value * 0.25
    term = jnp.ones_like(value)
    total = jnp.ones_like(value)
    for index in range(1, 30):
        term = term * quarter * (1.0 / float(index * index))
        total = total + term
    return total


def kernel_values(distance, half_width, w_coef):
    ratio = distance / half_width
    inside = jnp.abs(ratio) < 1.0
    radius = jnp.sqrt(jnp.maximum(1.0 - ratio * ratio, 0.0))
    bessel = bessel_zero(BETA * radius) / bessel_zero(jnp.float32(BETA))
    taper = jnp.cos(jnp.pi * w_coef * ratio * ratio)
    return jnp.where(inside, bessel * taper, jnp.float32(0.0))


def flatten_groups(vis_block, offset_block, support_block, plane_block, count_block):
    slot_total = vis_block.shape[-1]
    slot_ids = jnp.arange(slot_total, dtype=jnp.int32)
    live = (slot_ids[None, :] < count_block[:, None]).astype(jnp.float32).reshape(-1)
    real_part = vis_block[:, 0].reshape(-1) * live
    imag_part = vis_block[:, 1].reshape(-1) * live
    row_cell = offset_block[:, 0].reshape(-1).astype(jnp.float32)
    col_cell = offset_block[:, 1].reshape(-1).astype(jnp.float32)
    half_width = 8.0 * (support_block.reshape(-1) + 1).astype(jnp.float32)
    w_coef = 0.5 * (plane_block.reshape(-1) + 1).astype(jnp.float32) / PLANES
    return (real_part, imag_part, row_cell, col_cell, half_width, w_coef)


def grid_part(flat, row_start, row_count, width):
    total_vis = flat[0].shape[0]
    block_len = math.gcd(total_vis, 512)
    stacked = tuple((item.reshape(total_vis // block_len, block_len) for item in flat))
    row_pos = (row_start + jnp.arange(row_count, dtype=jnp.int32)).astype(jnp.float32)
    col_pos = jnp.arange(width, dtype=jnp.int32).astype(jnp.float32)

    def step_block(total, values):
        real_part, imag_part, row_cell, col_cell, half_width, w_coef = values
        row_weights = kernel_values(
            row_pos[None, :] - row_cell[:, None], half_width[:, None], w_coef[:, None]
        ).astype(jnp.bfloat16)
        col_kern = kernel_values(
            col_pos[None, :] - col_cell[:, None], half_width[:, None], w_coef[:, None]
        )
        col_weights = jnp.concatenate(
            [real_part[:, None] * col_kern, imag_part[:, None] * col_kern], axis=1
        ).astype(jnp.bfloat16)
        product = lax.dot_general(
            row_weights, col_weights, (((0,), (0,)), ((), ())), preferred_element_type=jnp.float32
        )
        return (total + product, None)

    start_total = jnp.zeros((row_count, 2 * width), jnp.float32)
    total, _ = lax.scan(step_block, start_total, stacked)
    return total.reshape(row_count, 2, width)


def any_cells(visibilities, cell_offsets, support_index, w_plane, live_counts):
    tiles, parts = lax.axis_size("tile"), lax.axis_size("chan")
    share = G // parts
    first_row = lax.axis_index("chan") * share - M
    held = jnp.stack(
        flatten_groups(visibilities[0], cell_offsets[0], support_index[0], w_plane[0], live_counts[0])
    )

    def step(_, carry):
        total, held = carry
        total = total + grid_part(held, first_row, share + 2 * M, G)
        return total, lax.ppermute(held, "chan", [(i, (i + 1) % parts) for i in range(parts)])

    total, _ = lax.fori_loop(0, parts, step, (jnp.zeros((share + 2 * M, 2, G), F32), held))
    last = parts - 1
    left_in = lax.ppermute(
        total[share + M :], ("tile", "chan"), [(t * parts + last, (t + 1) * parts) for t in range(tiles - 1)]
    )
    right_in = lax.ppermute(
        total[:M], ("tile", "chan"), [(t * parts, (t - 1) * parts + last) for t in range(1, tiles)]
    )
    owned = total[M : M + share]
    return owned.at[:M].add(left_in).at[share - M :].add(right_in)


def class_table():
    shape = (2 * M, 4 * PLANES)
    klass = lax.broadcasted_iota(jnp.int32, shape, 1)
    distance = jnp.abs(lax.broadcasted_iota(jnp.int32, shape, 0) - M).astype(F32)
    half = (8 * (klass // PLANES + 1)).astype(F32)
    w_coef = 0.5 * (klass % PLANES + 1).astype(F32) / PLANES
    ratio = jnp.minimum(distance / half, 1.0)
    square = ratio * ratio
    radius = jnp.sqrt(jnp.maximum(1.0 - square, 0.0))
    bessel = bessel_zero(BETA * radius) / bessel_zero(jnp.full(shape, BETA, F32))
    taper = jnp.cos(jnp.pi * w_coef * square)
    return jnp.where(ratio < 1.0, bessel * taper, 0.0).astype(BF16)


def turned(values, by, sub):
    for bit in (32, 16, 8):
        chosen = (by & bit) != 0
        values = [jnp.where(chosen, values[(k - bit // 8) % 8], values[k]) for k in range(8)]
    fine = by & 7
    taken = [jnp.take_along_axis(x, (sub - fine) & 7, axis=0, mode="promise_in_bounds") for x in values]
    wrapped = sub < fine
    return [jnp.where(wrapped, taken[(k - 1) % 8], taken[k]) for k in range(8)]


def lay(klass, row, col, re, im, table, weights, columns, start=0):
    sub = lax.broadcasted_iota(jnp.int32, klass.shape, 0)
    hot = jnp.concatenate([(klass == sub + 8 * k).astype(F32) for k in range(8)], axis=0).astype(BF16)
    values = jnp.dot(table[...], hot, preferred_element_type=F32)
    values = [values[8 * k : 8 * k + 8] for k in range(8)]
    by, first = row & 63, row >> 6
    mine = [
        jnp.where(jnp.where(sub + 8 * k < by, first + 1, first) == 0, x, 0.0)
        for k, x in enumerate(turned(values, by, sub))
    ]
    weights[0:64] = jnp.concatenate([x * re for x in mine], axis=0).astype(BF16)
    weights[64:128] = jnp.concatenate([x * im for x in mine], axis=0).astype(BF16)
    by, first = col & 63, col >> 6
    window = jnp.concatenate(turned(values, by, sub), axis=0).astype(BF16)
    block = jnp.concatenate(
        [jnp.where(sub + 8 * k < by, first + 1, first).astype(F32) for k in range(8)], axis=0).astype(BF16)
    for b in range(columns.shape[0] // 64):
        columns[64 * b : 64 * b + 64] = jnp.where(block == jnp.asarray(start + b, BF16), window, jnp.asarray(0, BF16))


def add(total, weights, columns, start=0):
    stop = 64 * start + columns.shape[0]
    total[:, 64 * start : stop] += lax.dot_general(
        weights[...], columns[...], (((1,), (1,)), ((), ())), preferred_element_type=F32)


def list_left(got, edge, real, whole, number):
    c = lax.axis_index("chan")
    nc, per = got.shape[0], got.shape[1]
    main = nc * per
    count = main + nc * 8
    left = 4 * real.shape[1]
    quarter = left // 4

    lanes = lax.broadcasted_iota(jnp.int32, (1, 256), 1) // LOW
    both = jnp.concatenate([got[...].reshape(main, 256), edge[...].reshape(nc * 8, 256)], axis=0)
    index = lax.broadcasted_iota(jnp.int32, (count, 256), 0)
    shift = jnp.where(index < main, BUCKET * ((index % per) // GROUPS_IN - 1), jnp.where(c == 0, -BUCKET, 2 * BUCKET))
    both = both + jnp.where(lanes == 3, shift - 1, 0).astype(F32)
    used = jnp.max(both[:, 128:256].T[2 * LOW : 3 * LOW], axis=0, keepdims=True)
    at = lax.broadcasted_iota(jnp.int32, (1, count), 1) % GROUPS_IN
    used = jnp.where((at == EARLY[0]) | (at == EARLY[1]), 0.0, used)
    before = (
        lax.broadcasted_iota(jnp.int32, (count, count), 0) < lax.broadcasted_iota(jnp.int32, (count, count), 1)
    ).astype(F32).astype(BF16)
    rank = jnp.dot(jnp.broadcast_to(used, (8, count)).astype(BF16), before, preferred_element_type=F32)[0:1]
    rank = jnp.where(used > 0.5, rank, -1.0)
    place = lax.broadcasted_iota(jnp.int32, (left, count), 0)
    place = (4 * (place % quarter) + place // quarter).astype(F32)
    pick = jnp.where(place == rank, 1.0, 0.0).astype(BF16)
    high = both.astype(BF16)
    low = (both - high.astype(F32)).astype(BF16)
    rows = jnp.dot(pick, high, preferred_element_type=F32) + jnp.dot(pick, low, preferred_element_type=F32)
    spot = lax.broadcasted_iota(jnp.int32, (quarter, 128), 1) // LOW

    def field(f):
        part, offset = divmod(f, 4)
        result = None
        for s in range(4):
            x = rows[s * quarter : (s + 1) * quarter, 128 * part : 128 * part + 128]
            if (s - offset) % 4:
                x = pltpu.roll(x, ((s - offset) % 4) * LOW, 1)
            result = x if result is None else jnp.where(spot == s, x, result)
        return result

    real[0], real[1] = field(0), field(1)
    whole[0], whole[1] = field(2).astype(jnp.int32) - M, field(3).astype(jnp.int32) - M
    whole[2] = (field(4) * float(PLANES) + field(5)).astype(jnp.int32)
    number[...] = jnp.broadcast_to(jnp.sum(used, axis=1, keepdims=True), number.shape)


def exchange(vis, cell, sup, wpl, cnt, table, total, real, whole, number, flag, got, edge, vis_v, cell_v, sup_v, wpl_v, cnt_v, packed, tile_flags, chan_flags,
             weights, columns,
             load_sem, send_sem, recv_sem, edge_send, edge_recv, tf_send, tf_recv, cf_send, cf_recv):
    t, c = lax.axis_index("tile"), lax.axis_index("chan")
    nt, nc = lax.axis_size("tile"), lax.axis_size("chan")
    slots = vis_v.shape[-1]
    loads = [
        pltpu.make_async_copy(vis.at[0, 0], vis_v, load_sem.at[0]),
        pltpu.make_async_copy(cell.at[0, 0], cell_v, load_sem.at[1]),
        pltpu.make_async_copy(sup.at[0], sup_v, load_sem.at[2]),
        pltpu.make_async_copy(wpl.at[0], wpl_v, load_sem.at[3]),
        pltpu.make_async_copy(cnt, cnt_v, load_sem.at[4]),
    ]
    for load in loads:
        load.start()
    edge[...] = jnp.zeros_like(edge)

    bar = pltpu.get_barrier_semaphore()
    for i in range(1, nc):
        pl.semaphore_signal(bar, inc=1, device_id=(t, lax.rem(c + i, nc)), device_id_type=MESH)
    for i in range(1, nt):
        pl.semaphore_signal(bar, inc=1, device_id=(lax.rem(t + i, nt), c), device_id_type=MESH)
    from_low = (c == 0) & (t > 0)
    from_high = (c == nc - 1) & (t < nt - 1)

    @pl.when(from_low)
    def _():
        for g in range(nc):
            pl.semaphore_signal(bar, inc=1, device_id=(t - 1, g), device_id_type=MESH)

    @pl.when(from_high)
    def _():
        for g in range(nc):
            pl.semaphore_signal(bar, inc=1, device_id=(t + 1, g), device_id_type=MESH)

    for load in loads:
        load.wait()

    live = lax.broadcasted_iota(jnp.int32, (1, slots), 1) < cnt_v[...]
    row = cell_v[0:1]
    buckets = G // BUCKET
    bucket = row // BUCKET
    right = cell_v[1:2] >= G // 2
    side = jnp.where(live, bucket + jnp.where(right, buckets, 0), -1)
    hot = (lax.broadcasted_iota(jnp.int32, (2 * buckets, slots), 0) == side).astype(F32)
    step = 256
    before = (
        lax.broadcasted_iota(jnp.int32, (step, step), 0) < lax.broadcasted_iota(jnp.int32, (step, step), 1)
    ).astype(F32).astype(BF16)
    parts = []
    carry = jnp.zeros((2 * buckets, 1), F32)
    for s in range(0, slots, step):
        piece = hot[:, s : s + step]
        ahead = jnp.dot(piece.astype(BF16), before, preferred_element_type=F32) + carry
        parts.append(jnp.sum(piece * ahead, axis=0, keepdims=True))
        carry = carry + jnp.sum(piece, axis=1, keepdims=True)
    rank = jnp.concatenate(parts, axis=1).astype(jnp.int32)
    full = jnp.max(carry[:buckets] + carry[buckets:], axis=0, keepdims=True) > CAP
    full = full | (jnp.max(carry, axis=0, keepdims=True) > CAP - LOW)
    over = full.astype(F32)
    tile_flags[t] = jnp.broadcast_to(over, (1, 128))

    spot = jnp.where(right, CAP - 1 - rank, rank)
    group = jnp.where(live, (bucket + 1) * GROUPS_IN + (spot >> (LOW.bit_length() - 1)), -1)
    place = spot & (LOW - 1)
    groups = packed.shape[0]
    to_group = (lax.broadcasted_iota(jnp.int32, (groups, slots), 0) == group).astype(F32).astype(BF16)
    at_place = lax.broadcasted_iota(jnp.int32, (LOW, slots), 0) == place

    def halves(x):
        high = x.astype(BF16).astype(F32)
        return high, x - high

    re_hi, re_lo = halves(vis_v[0:1])
    im_hi, im_lo = halves(vis_v[1:2])
    col = cell_v[1:2]
    pieces = [re_hi, im_hi, col >> 2, sup_v[...] * PLANES + wpl_v[...], re_lo, im_lo,
              (col & 3) * 64 + (row & (BUCKET - 1)) + 1, jnp.zeros((1, slots), F32)]
    spread = jnp.concatenate([jnp.where(at_place, x.astype(F32), 0.0).astype(BF16) for x in pieces], axis=0)
    moved = lax.dot_general(to_group, spread, (((1,), (1,)), ((), ())), preferred_element_type=F32)
    first, second = moved[:, 0:128], moved[:, 128:256]
    whole_1, whole_2 = first.astype(jnp.int32), second.astype(jnp.int32)
    lane = lax.broadcasted_iota(jnp.int32, first.shape, 1) // LOW
    packed[:, 0:128] = jnp.where(
        lane < 2, first + second,
        jnp.where(lane == 2, whole_1 * 4 + (whole_2 >> 6), pltpu.roll(whole_2, LOW, 1) & 63).astype(F32))
    klass = pltpu.roll(whole_1, LOW, 1)
    packed[:, 128:256] = jnp.where(
        lane == 0, klass >> 4,
        jnp.where(lane == 1, pltpu.roll(klass, LOW, 1) & (PLANES - 1),
                  jnp.where((lane == 2) & ((whole_2 & 63) > 0), 1, 0))).astype(F32)

    below, above = (t > 0).astype(jnp.int32), (t < nt - 1).astype(jnp.int32)
    pl.semaphore_wait(bar, nc - 1 + nt - 1 + below + above)

    def tile_flag(i, slot):
        return pltpu.make_async_remote_copy(
            src_ref=tile_flags.at[t], dst_ref=tile_flags.at[slot], send_sem=tf_send, recv_sem=tf_recv,
            device_id=(lax.rem(t + i, nt), c), device_id_type=MESH)

    for i in range(1, nt):
        tile_flag(i, t).start()

    width = 4 * GROUPS_IN

    def payload(i, slot):
        peer = lax.rem(c + i, nc)
        return pltpu.make_async_remote_copy(
            src_ref=packed.at[pl.ds(pl.multiple_of(8 * peer, 8), width)], dst_ref=got.at[slot], send_sem=send_sem,
            recv_sem=recv_sem.at[slot], device_id=(t, peer), device_id_type=MESH)

    for i in range(1, nc):
        payload(i, c).start()

    def edge_up():
        return pltpu.make_async_remote_copy(
            src_ref=packed.at[pl.ds(buckets * GROUPS_IN, GROUPS_IN)], dst_ref=edge.at[c, 0:GROUPS_IN], send_sem=edge_send.at[0],
            recv_sem=edge_recv.at[c], device_id=(t + 1, 0), device_id_type=MESH)

    def edge_down():
        return pltpu.make_async_remote_copy(
            src_ref=packed.at[pl.ds(GROUPS_IN, GROUPS_IN)], dst_ref=edge.at[c, 0:GROUPS_IN], send_sem=edge_send.at[1],
            recv_sem=edge_recv.at[c], device_id=(t - 1, nc - 1), device_id_type=MESH)

    @pl.when(t < nt - 1)
    def _():
        edge_up().start()

    @pl.when(t > 0)
    def _():
        edge_down().start()

    got[c] = packed[pl.ds(pl.multiple_of(8 * c, 8), width), :]

    def all_of(ref, count, sent, landed):
        return pltpu.make_async_remote_copy(
            src_ref=ref.at[0:count], dst_ref=ref.at[0:count], send_sem=sent, recv_sem=landed,
            device_id=(t, lax.rem(c + 1, nc)), device_id_type=MESH)

    all_of(tile_flags, nt - 1, tf_send, tf_recv).wait_recv()
    chan_flags[c] = jnp.max(tile_flags[...], axis=0)

    for i in range(1, nc):
        pltpu.make_async_remote_copy(
            src_ref=chan_flags.at[c], dst_ref=chan_flags.at[c], send_sem=cf_send, recv_sem=cf_recv,
            device_id=(t, lax.rem(c + i, nc)), device_id_type=MESH).start()

    table[...] = class_table()
    total[...] = jnp.zeros_like(total)

    spot = lax.broadcasted_iota(jnp.int32, (8, 128), 1) // LOW

    def fields(first, second, lift, picks):
        row_lanes = lax.broadcasted_iota(jnp.int32, first.shape, 1) // LOW == 3
        cells = first.astype(jnp.int32) - M
        cells = jnp.where(row_lanes, cells + lift, cells)
        klass = (second * float(PLANES) + pltpu.roll(second, 3 * LOW, 1)).astype(jnp.int32)

        def lines(x, offset):
            shifted = [pltpu.roll(x, ((b - offset) % 4) * LOW, 1) if (b - offset) % 4 else x for b in range(4)]
            made = []
            for pick in picks:
                parts = [jnp.broadcast_to(shifted[b][r : r + 1], (8, 128)) for b, r in enumerate(pick)]
                line = parts[0]
                for b in range(1, 4):
                    line = jnp.where(spot == b, parts[b], line)
                made.append(line)
            return made

        return lines(klass, 0), lines(cells, 3), lines(cells, 2), lines(first, 0), lines(first, 1)

    halves_at = (0, G // 64 - SPAN)
    lift = BUCKET * (lax.broadcasted_iota(jnp.int32, (width, 128), 0) // GROUPS_IN - 1) - 1

    here = 2 * (c // 2)

    def chip(k):
        q = k % 4
        dz = q + jnp.where(q == 2, 1, 0) - jnp.where(q == 3, 1, 0)
        z, y = (here // 2) % 4, here // 8
        return (((y + k // 4) % 2) * 4 + (z + dz) % 4) * 2

    def prepare(source, slot):
        made = [
            fields(got[x, :, 0:128], got[x, :, 128:256], lift, [[GROUPS_IN * b + g for b in range(4)] for g in EARLY])
            for x in (source, source + 1)
        ]
        for h in range(2):
            lay(*[jnp.concatenate([x[h], y[h]], axis=1) for x, y in zip(*made)], table, weights.at[slot, h],
                columns.at[slot, h], halves_at[h])

    def add_both(slot):
        for h in range(2):
            add(total, weights.at[slot, h], columns.at[slot, h], halves_at[h])

    def arrive(source):
        pltpu.make_async_remote_copy(
            src_ref=packed.at[pl.ds(0, width)], dst_ref=got.at[source], send_sem=send_sem,
            recv_sem=recv_sem.at[source], device_id=(t, source), device_id_type=MESH).wait_recv()

    arrive(here + (c + 1) % 2)
    prepare(here, 0)

    def two_chips(j, carry):
        for odd in (1, 0):
            source = chip(2 * j + 2 - odd)
            arrive(source)
            arrive(source + 1)
            prepare(source, odd)
            add_both(1 - odd)
        return carry

    chips = nc // 2
    lax.fori_loop(0, chips // 2 - 1, two_chips, 0)
    add_both(0)

    @pl.when(from_low | from_high)
    def _():
        for g in range(nc):
            pltpu.make_async_remote_copy(
                src_ref=packed.at[pl.ds(0, GROUPS_IN)], dst_ref=edge.at[g, 0:GROUPS_IN], send_sem=edge_send.at[0],
                recv_sem=edge_recv.at[g], device_id=(t, g), device_id_type=MESH).wait_recv()
        rows = edge[...].reshape(nc * 8, 256)
        lines = nc // 4
        picks = [[8 * (4 * n + b) + g for b in range(4)] for g in EARLY for n in range(lines)]
        made = fields(rows[:, 0:128], rows[:, 128:256], jnp.where(from_low, -BUCKET, 2 * BUCKET) - 1, picks)
        for h in range(2):
            for n in range(0, lines, 2):
                lay(*[jnp.concatenate(x[h * lines + n : h * lines + n + 2], axis=1) for x in made], table,
                    weights.at[n // 2, h], columns.at[n // 2, h], halves_at[h])
        for n in range(lines // 2):
            add_both(n)

    all_of(tile_flags, nt - 1, tf_send, tf_recv).wait_send()
    all_of(chan_flags, nc - 1, cf_send, cf_recv).wait_send()
    all_of(got, nc - 1, send_sem, recv_sem.at[0]).wait_send()

    @pl.when(t < nt - 1)
    def _():
        edge_up().wait_send()

    @pl.when(t > 0)
    def _():
        edge_down().wait_send()

    source = chip(chips - 1)
    arrive(source)
    arrive(source + 1)
    prepare(source, 1)
    list_left(got, edge, real, whole, number)
    add_both(1)

    all_of(chan_flags, nc - 1, cf_send, cf_recv).wait_recv()
    flag[0, 0] = (jnp.max(jnp.max(chan_flags[...], axis=0)) > 0.5).astype(jnp.int32)


def owned_rows(real, whole, number, table, begun, out, total, weights, columns):
    size = weights.shape[-1]
    lines = size // 128
    chunks = (jnp.max(number[...]).astype(jnp.int32) + 4 * lines - 1) // (4 * lines)
    total[...] = begun[...]

    def body(i, carry):
        def line(ref, f):
            return jnp.concatenate(
                [jnp.broadcast_to(ref[f, pl.ds(lines * i + h, 1), :], (8, 128)) for h in range(lines)], axis=1)

        lay(line(whole, 2), line(whole, 1), line(whole, 0), line(real, 0), line(real, 1), table, weights, columns)
        add(total, weights, columns)
        return carry

    lax.fori_loop(0, chunks, body, 0)
    out[:, 0, :] = total[0:64]
    out[:, 1, :] = total[64:128]


def per_device(visibilities, cell_offsets, support_index, w_plane, live_counts):
    nt, nc = lax.axis_size("tile"), lax.axis_size("chan")
    slots = visibilities.shape[-1]
    groups = (G // BUCKET + 2) * GROUPS_IN
    vmem = pl.BlockSpec(memory_space=pltpu.VMEM)
    left_lines = nc * 5 * (GROUPS_IN - len(EARLY)) // 4
    table, begun, real, whole, number, flag = pl.pallas_call(
        exchange,
        out_shape=(
            jax.ShapeDtypeStruct((2 * M, 4 * PLANES), BF16),
            jax.ShapeDtypeStruct((2 * G // nc, G), F32),
            jax.ShapeDtypeStruct((2, left_lines, 128), F32),
            jax.ShapeDtypeStruct((3, left_lines, 128), jnp.int32),
            jax.ShapeDtypeStruct((8, 128), F32),
            jax.ShapeDtypeStruct((1, 1), jnp.int32),
        ),
        in_specs=[pl.BlockSpec(memory_space=pltpu.MemorySpace.HBM)] * 5,
        out_specs=(vmem, vmem, vmem, vmem, vmem, pl.BlockSpec(memory_space=pltpu.SMEM)),
        scratch_shapes=[
            pltpu.VMEM((nc, 4 * GROUPS_IN, FIELDS * LOW), F32),
            pltpu.VMEM((nc, 8, FIELDS * LOW), F32),
            pltpu.VMEM((2, slots), F32),
            pltpu.VMEM((2, slots), jnp.int32),
            pltpu.VMEM((1, slots), jnp.int32),
            pltpu.VMEM((1, slots), jnp.int32),
            pltpu.VMEM((1, 1), jnp.int32),
            pltpu.VMEM((groups, FIELDS * LOW), F32),
            pltpu.VMEM((nt, 1, 128), F32),
            pltpu.VMEM((nc, 1, 128), F32),
            pltpu.VMEM((2, 2, 2 * G // nc, 256), BF16),
            pltpu.VMEM((2, 2, 64 * SPAN, 256), BF16),
            pltpu.SemaphoreType.DMA((5,)),
            pltpu.SemaphoreType.DMA,
            pltpu.SemaphoreType.DMA((nc,)),
            pltpu.SemaphoreType.DMA((2,)),
            pltpu.SemaphoreType.DMA((nc,)),
            pltpu.SemaphoreType.DMA,
            pltpu.SemaphoreType.DMA,
            pltpu.SemaphoreType.DMA,
            pltpu.SemaphoreType.DMA,
        ],
        compiler_params=pltpu.CompilerParams(collective_id=0, has_side_effects=True, vmem_limit_bytes=62 << 20),
    )(visibilities, cell_offsets, support_index, w_plane, live_counts)


    def usual(*_):
        return pl.pallas_call(
            owned_rows,
            out_shape=jax.ShapeDtypeStruct((G // nc, 2, G), F32),
            in_specs=[vmem] * 5,
            out_specs=vmem,
            scratch_shapes=[
                pltpu.VMEM((2 * G // nc, G), F32),
                pltpu.VMEM((2 * G // nc, 512), BF16),
                pltpu.VMEM((G, 512), BF16),
            ],
            compiler_params=pltpu.CompilerParams(vmem_limit_bytes=40 << 20),
        )(real, whole, number, table, begun)

    return lax.switch(
        flag[0, 0], (usual, any_cells), visibilities, cell_offsets, support_index, w_plane, live_counts
    )


def solution(mesh):
    in_specs = (
        P("tile", "chan", None, None),
        P("tile", "chan", None, None),
        P("tile", "chan", None),
        P("tile", "chan", None),
        P("tile", "chan"),
    )
    out_specs = P(("tile", "chan"), None, None)
    return jax.shard_map(
        per_device, mesh=mesh, in_specs=in_specs, out_specs=out_specs, check_vma=False
    )
```

```python
import functools
import math

import jax
import jax.numpy as jnp
from jax import lax
from jax.experimental import pallas as pl
from jax.experimental.pallas import tpu as pltpu
from jax.sharding import PartitionSpec as P

G = 1024
M = 32
PLANES = 16
BETA = 7.0

BUCKET = 32
CAP = 128
LOW = 32
GROUPS_IN = CAP // LOW
EARLY = (0, GROUPS_IN - 1)
SPAN = 10
FIELDS = 8
MESH = pl.DeviceIdType.MESH
F32 = jnp.float32
BF16 = jnp.bfloat16


def bessel_zero(value):
    quarter = value * value * 0.25
    term = jnp.ones_like(value)
    total = jnp.ones_like(value)
    for index in range(1, 30):
        term = term * quarter * (1.0 / float(index * index))
        total = total + term
    return total


def kernel_values(distance, half_width, w_coef):
    ratio = distance / half_width
    inside = jnp.abs(ratio) < 1.0
    radius = jnp.sqrt(jnp.maximum(1.0 - ratio * ratio, 0.0))
    bessel = bessel_zero(BETA * radius) / bessel_zero(jnp.float32(BETA))
    taper = jnp.cos(jnp.pi * w_coef * ratio * ratio)
    return jnp.where(inside, bessel * taper, jnp.float32(0.0))


def flatten_groups(vis_block, offset_block, support_block, plane_block, count_block):
    slot_total = vis_block.shape[-1]
    slot_ids = jnp.arange(slot_total, dtype=jnp.int32)
    live = (slot_ids[None, :] < count_block[:, None]).astype(jnp.float32).reshape(-1)
    real_part = vis_block[:, 0].reshape(-1) * live
    imag_part = vis_block[:, 1].reshape(-1) * live
    row_cell = offset_block[:, 0].reshape(-1).astype(jnp.float32)
    col_cell = offset_block[:, 1].reshape(-1).astype(jnp.float32)
    half_width = 8.0 * (support_block.reshape(-1) + 1).astype(jnp.float32)
    w_coef = 0.5 * (plane_block.reshape(-1) + 1).astype(jnp.float32) / PLANES
    return (real_part, imag_part, row_cell, col_cell, half_width, w_coef)


def grid_part(flat, row_start, row_count, width):
    total_vis = flat[0].shape[0]
    block_len = math.gcd(total_vis, 512)
    stacked = tuple((item.reshape(total_vis // block_len, block_len) for item in flat))
    row_pos = (row_start + jnp.arange(row_count, dtype=jnp.int32)).astype(jnp.float32)
    col_pos = jnp.arange(width, dtype=jnp.int32).astype(jnp.float32)

    def step_block(total, values):
        real_part, imag_part, row_cell, col_cell, half_width, w_coef = values
        row_weights = kernel_values(
            row_pos[None, :] - row_cell[:, None], half_width[:, None], w_coef[:, None]
        ).astype(jnp.bfloat16)
        col_kern = kernel_values(
            col_pos[None, :] - col_cell[:, None], half_width[:, None], w_coef[:, None]
        )
        col_weights = jnp.concatenate(
            [real_part[:, None] * col_kern, imag_part[:, None] * col_kern], axis=1
        ).astype(jnp.bfloat16)
        product = lax.dot_general(
            row_weights, col_weights, (((0,), (0,)), ((), ())), preferred_element_type=jnp.float32
        )
        return (total + product, None)

    start_total = jnp.zeros((row_count, 2 * width), jnp.float32)
    total, _ = lax.scan(step_block, start_total, stacked)
    return total.reshape(row_count, 2, width)


def any_cells(visibilities, cell_offsets, support_index, w_plane, live_counts):
    tiles, parts = lax.axis_size("tile"), lax.axis_size("chan")
    share = G // parts
    first_row = lax.axis_index("chan") * share - M
    held = jnp.stack(
        flatten_groups(visibilities[0], cell_offsets[0], support_index[0], w_plane[0], live_counts[0])
    )

    def step(_, carry):
        total, held = carry
        total = total + grid_part(held, first_row, share + 2 * M, G)
        return total, lax.ppermute(held, "chan", [(i, (i + 1) % parts) for i in range(parts)])

    total, _ = lax.fori_loop(0, parts, step, (jnp.zeros((share + 2 * M, 2, G), F32), held))
    last = parts - 1
    left_in = lax.ppermute(
        total[share + M :], ("tile", "chan"), [(t * parts + last, (t + 1) * parts) for t in range(tiles - 1)]
    )
    right_in = lax.ppermute(
        total[:M], ("tile", "chan"), [(t * parts, (t - 1) * parts + last) for t in range(1, tiles)]
    )
    owned = total[M : M + share]
    return owned.at[:M].add(left_in).at[share - M :].add(right_in)


def class_table():
    shape = (2 * M, 4 * PLANES)
    klass = lax.broadcasted_iota(jnp.int32, shape, 1)
    distance = jnp.abs(lax.broadcasted_iota(jnp.int32, shape, 0) - M).astype(F32)
    half = (8 * (klass // PLANES + 1)).astype(F32)
    w_coef = 0.5 * (klass % PLANES + 1).astype(F32) / PLANES
    ratio = jnp.minimum(distance / half, 1.0)
    square = ratio * ratio
    radius = jnp.sqrt(jnp.maximum(1.0 - square, 0.0))
    bessel = bessel_zero(BETA * radius) / bessel_zero(jnp.full(shape, BETA, F32))
    taper = jnp.cos(jnp.pi * w_coef * square)
    return jnp.where(ratio < 1.0, bessel * taper, 0.0).astype(BF16)


def turned(values, by, sub):
    for bit in (32, 16, 8):
        chosen = (by & bit) != 0
        values = [jnp.where(chosen, values[(k - bit // 8) % 8], values[k]) for k in range(8)]
    fine = by & 7
    taken = [jnp.take_along_axis(x, (sub - fine) & 7, axis=0, mode="promise_in_bounds") for x in values]
    wrapped = sub < fine
    return [jnp.where(wrapped, taken[(k - 1) % 8], taken[k]) for k in range(8)]


def lay(klass, row, col, re, im, table, weights, columns, start=0):
    sub = lax.broadcasted_iota(jnp.int32, klass.shape, 0)
    hot = jnp.concatenate([(klass == sub + 8 * k).astype(F32) for k in range(8)], axis=0).astype(BF16)
    values = jnp.dot(table[...], hot, preferred_element_type=F32)
    values = [values[8 * k : 8 * k + 8] for k in range(8)]
    by, first = row & 63, row >> 6
    mine = [
        jnp.where(jnp.where(sub + 8 * k < by, first + 1, first) == 0, x, 0.0)
        for k, x in enumerate(turned(values, by, sub))
    ]
    weights[0:64] = jnp.concatenate([x * re for x in mine], axis=0).astype(BF16)
    weights[64:128] = jnp.concatenate([x * im for x in mine], axis=0).astype(BF16)
    by, first = col & 63, col >> 6
    window = jnp.concatenate(turned(values, by, sub), axis=0).astype(BF16)
    block = jnp.concatenate(
        [jnp.where(sub + 8 * k < by, first + 1, first).astype(F32) for k in range(8)], axis=0).astype(BF16)
    for b in range(columns.shape[0] // 64):
        columns[64 * b : 64 * b + 64] = jnp.where(block == jnp.asarray(start + b, BF16), window, jnp.asarray(0, BF16))


def add(total, weights, columns, start=0):
    stop = 64 * start + columns.shape[0]
    total[:, 64 * start : stop] += lax.dot_general(
        weights[...], columns[...], (((1,), (1,)), ((), ())), preferred_element_type=F32)


def list_left(got, edge, real, whole, number):
    c = lax.axis_index("chan")
    nc, per = got.shape[0], got.shape[1]
    main = nc * per
    count = main + nc * 8
    left = 4 * real.shape[1]
    quarter = left // 4

    lanes = lax.broadcasted_iota(jnp.int32, (1, 256), 1) // LOW
    both = jnp.concatenate([got[...].reshape(main, 256), edge[...].reshape(nc * 8, 256)], axis=0)
    index = lax.broadcasted_iota(jnp.int32, (count, 256), 0)
    shift = jnp.where(index < main, BUCKET * ((index % per) // GROUPS_IN - 1), jnp.where(c == 0, -BUCKET, 2 * BUCKET))
    both = both + jnp.where(lanes == 3, shift - 1, 0).astype(F32)
    used = jnp.max(both[:, 128:256].T[2 * LOW : 3 * LOW], axis=0, keepdims=True)
    at = lax.broadcasted_iota(jnp.int32, (1, count), 1) % GROUPS_IN
    used = jnp.where((at == EARLY[0]) | (at == EARLY[1]), 0.0, used)
    before = (
        lax.broadcasted_iota(jnp.int32, (count, count), 0) < lax.broadcasted_iota(jnp.int32, (count, count), 1)
    ).astype(F32).astype(BF16)
    rank = jnp.dot(jnp.broadcast_to(used, (8, count)).astype(BF16), before, preferred_element_type=F32)[0:1]
    rank = jnp.where(used > 0.5, rank, -1.0)
    place = lax.broadcasted_iota(jnp.int32, (left, count), 0)
    place = (4 * (place % quarter) + place // quarter).astype(F32)
    pick = jnp.where(place == rank, 1.0, 0.0).astype(BF16)
    high = both.astype(BF16)
    low = (both - high.astype(F32)).astype(BF16)
    rows = jnp.dot(pick, high, preferred_element_type=F32) + jnp.dot(pick, low, preferred_element_type=F32)
    spot = lax.broadcasted_iota(jnp.int32, (quarter, 128), 1) // LOW

    def field(f):
        part, offset = divmod(f, 4)
        result = None
        for s in range(4):
            x = rows[s * quarter : (s + 1) * quarter, 128 * part : 128 * part + 128]
            if (s - offset) % 4:
                x = pltpu.roll(x, ((s - offset) % 4) * LOW, 1)
            result = x if result is None else jnp.where(spot == s, x, result)
        return result

    real[0], real[1] = field(0), field(1)
    whole[0], whole[1] = field(2).astype(jnp.int32) - M, field(3).astype(jnp.int32) - M
    whole[2] = (field(4) * float(PLANES) + field(5)).astype(jnp.int32)
    number[...] = jnp.broadcast_to(jnp.sum(used, axis=1, keepdims=True), number.shape)


def exchange(vis, cell, sup, wpl, cnt, table, total, real, whole, number, flag, got, edge, vis_v, cell_v, sup_v, wpl_v, cnt_v, packed, tile_flags, chan_flags,
             weights, columns,
             load_sem, send_sem, recv_sem, edge_send, edge_recv, tf_send, tf_recv, cf_send, cf_recv):
    t, c = lax.axis_index("tile"), lax.axis_index("chan")
    nt, nc = lax.axis_size("tile"), lax.axis_size("chan")
    slots = vis_v.shape[-1]
    loads = [
        pltpu.make_async_copy(vis.at[0, 0], vis_v, load_sem.at[0]),
        pltpu.make_async_copy(cell.at[0, 0], cell_v, load_sem.at[1]),
        pltpu.make_async_copy(sup.at[0], sup_v, load_sem.at[2]),
        pltpu.make_async_copy(wpl.at[0], wpl_v, load_sem.at[3]),
        pltpu.make_async_copy(cnt, cnt_v, load_sem.at[4]),
    ]
    for load in loads:
        load.start()
    edge[...] = jnp.zeros_like(edge)

    bar = pltpu.get_barrier_semaphore()
    for i in range(1, nc):
        pl.semaphore_signal(bar, inc=1, device_id=(t, lax.rem(c + i, nc)), device_id_type=MESH)
    for i in range(1, nt):
        pl.semaphore_signal(bar, inc=1, device_id=(lax.rem(t + i, nt), c), device_id_type=MESH)
    from_low = (c == 0) & (t > 0)
    from_high = (c == nc - 1) & (t < nt - 1)

    @pl.when(from_low)
    def _():
        for g in range(nc):
            pl.semaphore_signal(bar, inc=1, device_id=(t - 1, g), device_id_type=MESH)

    @pl.when(from_high)
    def _():
        for g in range(nc):
            pl.semaphore_signal(bar, inc=1, device_id=(t + 1, g), device_id_type=MESH)

    for load in loads:
        load.wait()

    live = lax.broadcasted_iota(jnp.int32, (1, slots), 1) < cnt_v[...]
    row = cell_v[0:1]
    buckets = G // BUCKET
    bucket = row // BUCKET
    right = cell_v[1:2] >= G // 2
    side = jnp.where(live, bucket + jnp.where(right, buckets, 0), -1)
    hot = (lax.broadcasted_iota(jnp.int32, (2 * buckets, slots), 0) == side).astype(F32)
    step = 256
    before = (
        lax.broadcasted_iota(jnp.int32, (step, step), 0) < lax.broadcasted_iota(jnp.int32, (step, step), 1)
    ).astype(F32).astype(BF16)
    parts = []
    carry = jnp.zeros((2 * buckets, 1), F32)
    for s in range(0, slots, step):
        piece = hot[:, s : s + step]
        ahead = jnp.dot(piece.astype(BF16), before, preferred_element_type=F32) + carry
        parts.append(jnp.sum(piece * ahead, axis=0, keepdims=True))
        carry = carry + jnp.sum(piece, axis=1, keepdims=True)
    rank = jnp.concatenate(parts, axis=1).astype(jnp.int32)
    full = jnp.max(carry[:buckets] + carry[buckets:], axis=0, keepdims=True) > CAP
    full = full | (jnp.max(carry, axis=0, keepdims=True) > CAP - LOW)
    over = full.astype(F32)
    tile_flags[t] = jnp.broadcast_to(over, (1, 128))

    spot = jnp.where(right, CAP - 1 - rank, rank)
    group = jnp.where(live, (bucket + 1) * GROUPS_IN + (spot >> (LOW.bit_length() - 1)), -1)
    place = spot & (LOW - 1)
    groups = packed.shape[0]
    to_group = (lax.broadcasted_iota(jnp.int32, (groups, slots), 0) == group).astype(F32).astype(BF16)
    at_place = lax.broadcasted_iota(jnp.int32, (LOW, slots), 0) == place

    def halves(x):
        high = x.astype(BF16).astype(F32)
        return high, x - high

    re_hi, re_lo = halves(vis_v[0:1])
    im_hi, im_lo = halves(vis_v[1:2])
    col = cell_v[1:2]
    pieces = [re_hi, im_hi, col >> 2, sup_v[...] * PLANES + wpl_v[...], re_lo, im_lo,
              (col & 3) * 64 + (row & (BUCKET - 1)) + 1, jnp.zeros((1, slots), F32)]
    spread = jnp.concatenate([jnp.where(at_place, x.astype(F32), 0.0).astype(BF16) for x in pieces], axis=0)
    moved = lax.dot_general(to_group, spread, (((1,), (1,)), ((), ())), preferred_element_type=F32)
    first, second = moved[:, 0:128], moved[:, 128:256]
    whole_1, whole_2 = first.astype(jnp.int32), second.astype(jnp.int32)
    lane = lax.broadcasted_iota(jnp.int32, first.shape, 1) // LOW
    packed[:, 0:128] = jnp.where(
        lane < 2, first + second,
        jnp.where(lane == 2, whole_1 * 4 + (whole_2 >> 6), pltpu.roll(whole_2, LOW, 1) & 63).astype(F32))
    klass = pltpu.roll(whole_1, LOW, 1)
    packed[:, 128:256] = jnp.where(
        lane == 0, klass >> 4,
        jnp.where(lane == 1, pltpu.roll(klass, LOW, 1) & (PLANES - 1),
                  jnp.where((lane == 2) & ((whole_2 & 63) > 0), 1, 0))).astype(F32)

    below, above = (t > 0).astype(jnp.int32), (t < nt - 1).astype(jnp.int32)
    pl.semaphore_wait(bar, nc - 1 + nt - 1 + below + above)

    def tile_flag(i, slot):
        return pltpu.make_async_remote_copy(
            src_ref=tile_flags.at[t], dst_ref=tile_flags.at[slot], send_sem=tf_send, recv_sem=tf_recv,
            device_id=(lax.rem(t + i, nt), c), device_id_type=MESH)

    for i in range(1, nt):
        tile_flag(i, t).start()

    width = 4 * GROUPS_IN

    def payload(i, slot):
        peer = lax.rem(c + i, nc)
        return pltpu.make_async_remote_copy(
            src_ref=packed.at[pl.ds(pl.multiple_of(8 * peer, 8), width)], dst_ref=got.at[slot], send_sem=send_sem,
            recv_sem=recv_sem.at[slot], device_id=(t, peer), device_id_type=MESH)

    for i in range(1, nc):
        payload(i, c).start()

    def edge_up():
        return pltpu.make_async_remote_copy(
            src_ref=packed.at[pl.ds(buckets * GROUPS_IN, GROUPS_IN)], dst_ref=edge.at[c, 0:GROUPS_IN], send_sem=edge_send.at[0],
            recv_sem=edge_recv.at[c], device_id=(t + 1, 0), device_id_type=MESH)

    def edge_down():
        return pltpu.make_async_remote_copy(
            src_ref=packed.at[pl.ds(GROUPS_IN, GROUPS_IN)], dst_ref=edge.at[c, 0:GROUPS_IN], send_sem=edge_send.at[1],
            recv_sem=edge_recv.at[c], device_id=(t - 1, nc - 1), device_id_type=MESH)

    @pl.when(t < nt - 1)
    def _():
        edge_up().start()

    @pl.when(t > 0)
    def _():
        edge_down().start()

    got[c] = packed[pl.ds(pl.multiple_of(8 * c, 8), width), :]

    def all_of(ref, count, sent, landed):
        return pltpu.make_async_remote_copy(
            src_ref=ref.at[0:count], dst_ref=ref.at[0:count], send_sem=sent, recv_sem=landed,
            device_id=(t, lax.rem(c + 1, nc)), device_id_type=MESH)

    table[...] = class_table()
    total[...] = jnp.zeros_like(total)

    spot = lax.broadcasted_iota(jnp.int32, (8, 128), 1) // LOW

    def fields(first, second, lift, picks):
        row_lanes = lax.broadcasted_iota(jnp.int32, first.shape, 1) // LOW == 3
        cells = first.astype(jnp.int32) - M
        cells = jnp.where(row_lanes, cells + lift, cells)
        klass = (second * float(PLANES) + pltpu.roll(second, 3 * LOW, 1)).astype(jnp.int32)

        def lines(x, offset):
            shifted = [pltpu.roll(x, ((b - offset) % 4) * LOW, 1) if (b - offset) % 4 else x for b in range(4)]
            made = []
            for pick in picks:
                parts = [jnp.broadcast_to(shifted[b][r : r + 1], (8, 128)) for b, r in enumerate(pick)]
                line = parts[0]
                for b in range(1, 4):
                    line = jnp.where(spot == b, parts[b], line)
                made.append(line)
            return made

        return lines(klass, 0), lines(cells, 3), lines(cells, 2), lines(first, 0), lines(first, 1)

    halves_at = (0, G // 64 - SPAN)
    lift = BUCKET * (lax.broadcasted_iota(jnp.int32, (width, 128), 0) // GROUPS_IN - 1) - 1

    here = 2 * (c // 2)

    def chip(k):
        q = k % 4
        dz = q + jnp.where(q == 2, 1, 0) - jnp.where(q == 3, 1, 0)
        z, y = (here // 2) % 4, here // 8
        return (((y + k // 4) % 2) * 4 + (z + dz) % 4) * 2

    def prepare(source, slot):
        made = [
            fields(got[x, :, 0:128], got[x, :, 128:256], lift, [[GROUPS_IN * b + g for b in range(4)] for g in EARLY])
            for x in (source, source + 1)
        ]
        for h in range(2):
            lay(*[jnp.concatenate([x[h], y[h]], axis=1) for x, y in zip(*made)], table, weights.at[slot, h],
                columns.at[slot, h], halves_at[h])

    def add_both(slot):
        for h in range(2):
            add(total, weights.at[slot, h], columns.at[slot, h], halves_at[h])

    def arrive(source):
        pltpu.make_async_remote_copy(
            src_ref=packed.at[pl.ds(0, width)], dst_ref=got.at[source], send_sem=send_sem,
            recv_sem=recv_sem.at[source], device_id=(t, source), device_id_type=MESH).wait_recv()

    arrive(here + (c + 1) % 2)
    prepare(here, 0)

    def two_chips(j, carry):
        @pl.when(j == 1)
        def _():
            all_of(tile_flags, nt - 1, tf_send, tf_recv).wait_recv()
            chan_flags[c] = jnp.max(tile_flags[...], axis=0)

            for i in range(1, nc):
                pltpu.make_async_remote_copy(
                    src_ref=chan_flags.at[c], dst_ref=chan_flags.at[c], send_sem=cf_send, recv_sem=cf_recv,
                    device_id=(t, lax.rem(c + i, nc)), device_id_type=MESH).start()

        for odd in (1, 0):
            source = chip(2 * j + 2 - odd)
            arrive(source)
            arrive(source + 1)
            prepare(source, odd)
            add_both(1 - odd)
        return carry

    chips = nc // 2
    lax.fori_loop(0, chips // 2 - 1, two_chips, 0)
    add_both(0)

    @pl.when(from_low | from_high)
    def _():
        for g in range(nc):
            pltpu.make_async_remote_copy(
                src_ref=packed.at[pl.ds(0, GROUPS_IN)], dst_ref=edge.at[g, 0:GROUPS_IN], send_sem=edge_send.at[0],
                recv_sem=edge_recv.at[g], device_id=(t, g), device_id_type=MESH).wait_recv()
        rows = edge[...].reshape(nc * 8, 256)
        lines = nc // 4
        picks = [[8 * (4 * n + b) + g for b in range(4)] for g in EARLY for n in range(lines)]
        made = fields(rows[:, 0:128], rows[:, 128:256], jnp.where(from_low, -BUCKET, 2 * BUCKET) - 1, picks)
        for h in range(2):
            for n in range(0, lines, 2):
                lay(*[jnp.concatenate(x[h * lines + n : h * lines + n + 2], axis=1) for x in made], table,
                    weights.at[n // 2, h], columns.at[n // 2, h], halves_at[h])
        for n in range(lines // 2):
            add_both(n)

    all_of(tile_flags, nt - 1, tf_send, tf_recv).wait_send()
    all_of(chan_flags, nc - 1, cf_send, cf_recv).wait_send()
    all_of(got, nc - 1, send_sem, recv_sem.at[0]).wait_send()

    @pl.when(t < nt - 1)
    def _():
        edge_up().wait_send()

    @pl.when(t > 0)
    def _():
        edge_down().wait_send()

    source = chip(chips - 1)
    arrive(source)
    arrive(source + 1)
    prepare(source, 1)
    list_left(got, edge, real, whole, number)
    add_both(1)

    all_of(chan_flags, nc - 1, cf_send, cf_recv).wait_recv()
    flag[0, 0] = (jnp.max(jnp.max(chan_flags[...], axis=0)) > 0.5).astype(jnp.int32)


def owned_rows(real, whole, number, table, begun, out, total, weights, columns):
    size = weights.shape[-1]
    lines = size // 128
    chunks = (jnp.max(number[...]).astype(jnp.int32) + 4 * lines - 1) // (4 * lines)
    total[...] = begun[...]

    def body(i, carry):
        def line(ref, f):
            return jnp.concatenate(
                [jnp.broadcast_to(ref[f, pl.ds(lines * i + h, 1), :], (8, 128)) for h in range(lines)], axis=1)

        lay(line(whole, 2), line(whole, 1), line(whole, 0), line(real, 0), line(real, 1), table, weights, columns)
        add(total, weights, columns)
        return carry

    lax.fori_loop(0, chunks, body, 0)
    out[:, 0, :] = total[0:64]
    out[:, 1, :] = total[64:128]


def per_device(visibilities, cell_offsets, support_index, w_plane, live_counts):
    nt, nc = lax.axis_size("tile"), lax.axis_size("chan")
    slots = visibilities.shape[-1]
    groups = (G // BUCKET + 2) * GROUPS_IN
    vmem = pl.BlockSpec(memory_space=pltpu.VMEM)
    left_lines = nc * 5 * (GROUPS_IN - len(EARLY)) // 4
    table, begun, real, whole, number, flag = pl.pallas_call(
        exchange,
        out_shape=(
            jax.ShapeDtypeStruct((2 * M, 4 * PLANES), BF16),
            jax.ShapeDtypeStruct((2 * G // nc, G), F32),
            jax.ShapeDtypeStruct((2, left_lines, 128), F32),
            jax.ShapeDtypeStruct((3, left_lines, 128), jnp.int32),
            jax.ShapeDtypeStruct((8, 128), F32),
            jax.ShapeDtypeStruct((1, 1), jnp.int32),
        ),
        in_specs=[pl.BlockSpec(memory_space=pltpu.MemorySpace.HBM)] * 5,
        out_specs=(vmem, vmem, vmem, vmem, vmem, pl.BlockSpec(memory_space=pltpu.SMEM)),
        scratch_shapes=[
            pltpu.VMEM((nc, 4 * GROUPS_IN, FIELDS * LOW), F32),
            pltpu.VMEM((nc, 8, FIELDS * LOW), F32),
            pltpu.VMEM((2, slots), F32),
            pltpu.VMEM((2, slots), jnp.int32),
            pltpu.VMEM((1, slots), jnp.int32),
            pltpu.VMEM((1, slots), jnp.int32),
            pltpu.VMEM((1, 1), jnp.int32),
            pltpu.VMEM((groups, FIELDS * LOW), F32),
            pltpu.VMEM((nt, 1, 128), F32),
            pltpu.VMEM((nc, 1, 128), F32),
            pltpu.VMEM((2, 2, 2 * G // nc, 256), BF16),
            pltpu.VMEM((2, 2, 64 * SPAN, 256), BF16),
            pltpu.SemaphoreType.DMA((5,)),
            pltpu.SemaphoreType.DMA,
            pltpu.SemaphoreType.DMA((nc,)),
            pltpu.SemaphoreType.DMA((2,)),
            pltpu.SemaphoreType.DMA((nc,)),
            pltpu.SemaphoreType.DMA,
            pltpu.SemaphoreType.DMA,
            pltpu.SemaphoreType.DMA,
            pltpu.SemaphoreType.DMA,
        ],
        compiler_params=pltpu.CompilerParams(collective_id=0, has_side_effects=True, vmem_limit_bytes=62 << 20),
    )(visibilities, cell_offsets, support_index, w_plane, live_counts)


    def usual(*_):
        return pl.pallas_call(
            owned_rows,
            out_shape=jax.ShapeDtypeStruct((G // nc, 2, G), F32),
            in_specs=[vmem] * 5,
            out_specs=vmem,
            scratch_shapes=[
                pltpu.VMEM((2 * G // nc, G), F32),
                pltpu.VMEM((2 * G // nc, 512), BF16),
                pltpu.VMEM((G, 512), BF16),
            ],
            compiler_params=pltpu.CompilerParams(vmem_limit_bytes=40 << 20),
        )(real, whole, number, table, begun)

    return lax.switch(
        flag[0, 0], (usual, any_cells), visibilities, cell_offsets, support_index, w_plane, live_counts
    )


def solution(mesh):
    in_specs = (
        P("tile", "chan", None, None),
        P("tile", "chan", None, None),
        P("tile", "chan", None),
        P("tile", "chan", None),
        P("tile", "chan"),
    )
    out_specs = P(("tile", "chan"), None, None)
    return jax.shard_map(
        per_device, mesh=mesh, in_specs=in_specs, out_specs=out_specs, check_vma=False
    )
```

```python
import functools
import math

import jax
import jax.numpy as jnp
from jax import lax
from jax.experimental import pallas as pl
from jax.experimental.pallas import tpu as pltpu
from jax.sharding import PartitionSpec as P

G = 1024
M = 32
PLANES = 16
BETA = 7.0

BUCKET = 32
CAP = 128
LOW = 32
GROUPS_IN = CAP // LOW
EARLY = (0, GROUPS_IN - 1)
SPAN = 10
FIELDS = 8
MESH = pl.DeviceIdType.MESH
F32 = jnp.float32
BF16 = jnp.bfloat16


def bessel_zero(value):
    quarter = value * value * 0.25
    term = jnp.ones_like(value)
    total = jnp.ones_like(value)
    for index in range(1, 30):
        term = term * quarter * (1.0 / float(index * index))
        total = total + term
    return total


def kernel_values(distance, half_width, w_coef):
    ratio = distance / half_width
    inside = jnp.abs(ratio) < 1.0
    radius = jnp.sqrt(jnp.maximum(1.0 - ratio * ratio, 0.0))
    bessel = bessel_zero(BETA * radius) / bessel_zero(jnp.float32(BETA))
    taper = jnp.cos(jnp.pi * w_coef * ratio * ratio)
    return jnp.where(inside, bessel * taper, jnp.float32(0.0))


def flatten_groups(vis_block, offset_block, support_block, plane_block, count_block):
    slot_total = vis_block.shape[-1]
    slot_ids = jnp.arange(slot_total, dtype=jnp.int32)
    live = (slot_ids[None, :] < count_block[:, None]).astype(jnp.float32).reshape(-1)
    real_part = vis_block[:, 0].reshape(-1) * live
    imag_part = vis_block[:, 1].reshape(-1) * live
    row_cell = offset_block[:, 0].reshape(-1).astype(jnp.float32)
    col_cell = offset_block[:, 1].reshape(-1).astype(jnp.float32)
    half_width = 8.0 * (support_block.reshape(-1) + 1).astype(jnp.float32)
    w_coef = 0.5 * (plane_block.reshape(-1) + 1).astype(jnp.float32) / PLANES
    return (real_part, imag_part, row_cell, col_cell, half_width, w_coef)


def grid_part(flat, row_start, row_count, width):
    total_vis = flat[0].shape[0]
    block_len = math.gcd(total_vis, 512)
    stacked = tuple((item.reshape(total_vis // block_len, block_len) for item in flat))
    row_pos = (row_start + jnp.arange(row_count, dtype=jnp.int32)).astype(jnp.float32)
    col_pos = jnp.arange(width, dtype=jnp.int32).astype(jnp.float32)

    def step_block(total, values):
        real_part, imag_part, row_cell, col_cell, half_width, w_coef = values
        row_weights = kernel_values(
            row_pos[None, :] - row_cell[:, None], half_width[:, None], w_coef[:, None]
        ).astype(jnp.bfloat16)
        col_kern = kernel_values(
            col_pos[None, :] - col_cell[:, None], half_width[:, None], w_coef[:, None]
        )
        col_weights = jnp.concatenate(
            [real_part[:, None] * col_kern, imag_part[:, None] * col_kern], axis=1
        ).astype(jnp.bfloat16)
        product = lax.dot_general(
            row_weights, col_weights, (((0,), (0,)), ((), ())), preferred_element_type=jnp.float32
        )
        return (total + product, None)

    start_total = jnp.zeros((row_count, 2 * width), jnp.float32)
    total, _ = lax.scan(step_block, start_total, stacked)
    return total.reshape(row_count, 2, width)


def any_cells(visibilities, cell_offsets, support_index, w_plane, live_counts):
    tiles, parts = lax.axis_size("tile"), lax.axis_size("chan")
    share = G // parts
    first_row = lax.axis_index("chan") * share - M
    held = jnp.stack(
        flatten_groups(visibilities[0], cell_offsets[0], support_index[0], w_plane[0], live_counts[0])
    )

    def step(_, carry):
        total, held = carry
        total = total + grid_part(held, first_row, share + 2 * M, G)
        return total, lax.ppermute(held, "chan", [(i, (i + 1) % parts) for i in range(parts)])

    total, _ = lax.fori_loop(0, parts, step, (jnp.zeros((share + 2 * M, 2, G), F32), held))
    last = parts - 1
    left_in = lax.ppermute(
        total[share + M :], ("tile", "chan"), [(t * parts + last, (t + 1) * parts) for t in range(tiles - 1)]
    )
    right_in = lax.ppermute(
        total[:M], ("tile", "chan"), [(t * parts, (t - 1) * parts + last) for t in range(1, tiles)]
    )
    owned = total[M : M + share]
    return owned.at[:M].add(left_in).at[share - M :].add(right_in)


def class_table():
    shape = (2 * M, 4 * PLANES)
    klass = lax.broadcasted_iota(jnp.int32, shape, 1)
    distance = jnp.abs(lax.broadcasted_iota(jnp.int32, shape, 0) - M).astype(F32)
    half = (8 * (klass // PLANES + 1)).astype(F32)
    w_coef = 0.5 * (klass % PLANES + 1).astype(F32) / PLANES
    ratio = jnp.minimum(distance / half, 1.0)
    square = ratio * ratio
    radius = jnp.sqrt(jnp.maximum(1.0 - square, 0.0))
    bessel = bessel_zero(BETA * radius) / bessel_zero(jnp.full(shape, BETA, F32))
    taper = jnp.cos(jnp.pi * w_coef * square)
    return jnp.where(ratio < 1.0, bessel * taper, 0.0).astype(BF16)


def turned(values, by, sub):
    for bit in (32, 16, 8):
        chosen = (by & bit) != 0
        values = [jnp.where(chosen, values[(k - bit // 8) % 8], values[k]) for k in range(8)]
    fine = by & 7
    taken = [jnp.take_along_axis(x, (sub - fine) & 7, axis=0, mode="promise_in_bounds") for x in values]
    wrapped = sub < fine
    return [jnp.where(wrapped, taken[(k - 1) % 8], taken[k]) for k in range(8)]


def lay(klass, row, col, re, im, table, weights, columns, start=0):
    sub = lax.broadcasted_iota(jnp.int32, klass.shape, 0)
    hot = jnp.concatenate([(klass == sub + 8 * k).astype(F32) for k in range(8)], axis=0).astype(BF16)
    values = jnp.dot(table[...], hot, preferred_element_type=F32)
    values = [values[8 * k : 8 * k + 8] for k in range(8)]
    by, first = row & 63, row >> 6
    mine = [
        jnp.where(jnp.where(sub + 8 * k < by, first + 1, first) == 0, x, 0.0)
        for k, x in enumerate(turned(values, by, sub))
    ]
    weights[0:64] = jnp.concatenate([x * re for x in mine], axis=0).astype(BF16)
    weights[64:128] = jnp.concatenate([x * im for x in mine], axis=0).astype(BF16)
    by, first = col & 63, col >> 6
    window = jnp.concatenate(turned(values, by, sub), axis=0).astype(BF16)
    block = jnp.concatenate(
        [jnp.where(sub + 8 * k < by, first + 1, first).astype(F32) for k in range(8)], axis=0).astype(BF16)
    for b in range(columns.shape[0] // 64):
        columns[64 * b : 64 * b + 64] = jnp.where(block == jnp.asarray(start + b, BF16), window, jnp.asarray(0, BF16))


def add(total, weights, columns, start=0):
    stop = 64 * start + columns.shape[0]
    total[:, 64 * start : stop] += lax.dot_general(
        weights[...], columns[...], (((1,), (1,)), ((), ())), preferred_element_type=F32)


def list_left(got, edge, real, whole, number):
    c = lax.axis_index("chan")
    nc, per = got.shape[0], got.shape[1]
    main = nc * per
    count = main + nc * 8
    left = 4 * real.shape[1]
    quarter = left // 4

    lanes = lax.broadcasted_iota(jnp.int32, (1, 256), 1) // LOW
    both = jnp.concatenate([got[...].reshape(main, 256), edge[...].reshape(nc * 8, 256)], axis=0)
    index = lax.broadcasted_iota(jnp.int32, (count, 256), 0)
    shift = jnp.where(index < main, BUCKET * ((index % per) // GROUPS_IN - 1), jnp.where(c == 0, -BUCKET, 2 * BUCKET))
    both = both + jnp.where(lanes == 3, shift - 1, 0).astype(F32)
    used = jnp.max(both[:, 128:256].T[2 * LOW : 3 * LOW], axis=0, keepdims=True)
    at = lax.broadcasted_iota(jnp.int32, (1, count), 1) % GROUPS_IN
    used = jnp.where((at == EARLY[0]) | (at == EARLY[1]), 0.0, used)
    before = (
        lax.broadcasted_iota(jnp.int32, (count, count), 0) < lax.broadcasted_iota(jnp.int32, (count, count), 1)
    ).astype(F32).astype(BF16)
    rank = jnp.dot(jnp.broadcast_to(used, (8, count)).astype(BF16), before, preferred_element_type=F32)[0:1]
    rank = jnp.where(used > 0.5, rank, -1.0)
    place = lax.broadcasted_iota(jnp.int32, (left, count), 0)
    place = (4 * (place % quarter) + place // quarter).astype(F32)
    pick = jnp.where(place == rank, 1.0, 0.0).astype(BF16)
    high = both.astype(BF16)
    low = (both - high.astype(F32)).astype(BF16)
    rows = jnp.dot(pick, high, preferred_element_type=F32) + jnp.dot(pick, low, preferred_element_type=F32)
    spot = lax.broadcasted_iota(jnp.int32, (quarter, 128), 1) // LOW

    def field(f):
        part, offset = divmod(f, 4)
        result = None
        for s in range(4):
            x = rows[s * quarter : (s + 1) * quarter, 128 * part : 128 * part + 128]
            if (s - offset) % 4:
                x = pltpu.roll(x, ((s - offset) % 4) * LOW, 1)
            result = x if result is None else jnp.where(spot == s, x, result)
        return result

    real[0], real[1] = field(0), field(1)
    whole[0], whole[1] = field(2).astype(jnp.int32) - M, field(3).astype(jnp.int32) - M
    whole[2] = (field(4) * float(PLANES) + field(5)).astype(jnp.int32)
    number[...] = jnp.broadcast_to(jnp.sum(used, axis=1, keepdims=True), number.shape)


def exchange(vis, cell, sup, wpl, cnt, table, total, real, whole, number, flag, got, edge, vis_v, cell_v, sup_v, wpl_v, cnt_v, packed, tile_flags, chan_flags,
             weights, columns,
             load_sem, send_sem, recv_sem, edge_send, edge_recv, tf_send, tf_recv, cf_send, cf_recv):
    t, c = lax.axis_index("tile"), lax.axis_index("chan")
    nt, nc = lax.axis_size("tile"), lax.axis_size("chan")
    slots = vis_v.shape[-1]
    loads = [
        pltpu.make_async_copy(vis.at[0, 0], vis_v, load_sem.at[0]),
        pltpu.make_async_copy(cell.at[0, 0], cell_v, load_sem.at[1]),
        pltpu.make_async_copy(sup.at[0], sup_v, load_sem.at[2]),
        pltpu.make_async_copy(wpl.at[0], wpl_v, load_sem.at[3]),
        pltpu.make_async_copy(cnt, cnt_v, load_sem.at[4]),
    ]
    for load in loads:
        load.start()
    edge[...] = jnp.zeros_like(edge)

    bar = pltpu.get_barrier_semaphore()
    for i in range(1, nc):
        pl.semaphore_signal(bar, inc=1, device_id=(t, lax.rem(c + i, nc)), device_id_type=MESH)
    for i in range(1, nt):
        pl.semaphore_signal(bar, inc=1, device_id=(lax.rem(t + i, nt), c), device_id_type=MESH)
    from_low = (c == 0) & (t > 0)
    from_high = (c == nc - 1) & (t < nt - 1)

    @pl.when(from_low)
    def _():
        for g in range(nc):
            pl.semaphore_signal(bar, inc=1, device_id=(t - 1, g), device_id_type=MESH)

    @pl.when(from_high)
    def _():
        for g in range(nc):
            pl.semaphore_signal(bar, inc=1, device_id=(t + 1, g), device_id_type=MESH)

    for load in loads:
        load.wait()

    live = lax.broadcasted_iota(jnp.int32, (1, slots), 1) < cnt_v[...]
    row = cell_v[0:1]
    buckets = G // BUCKET
    bucket = row // BUCKET
    right = cell_v[1:2] >= G // 2
    side = jnp.where(live, bucket + jnp.where(right, buckets, 0), -1)
    hot = (lax.broadcasted_iota(jnp.int32, (2 * buckets, slots), 0) == side).astype(F32)
    step = 256
    before = (
        lax.broadcasted_iota(jnp.int32, (step, step), 0) < lax.broadcasted_iota(jnp.int32, (step, step), 1)
    ).astype(F32).astype(BF16)
    parts = []
    carry = jnp.zeros((2 * buckets, 1), F32)
    for s in range(0, slots, step):
        piece = hot[:, s : s + step]
        ahead = jnp.dot(piece.astype(BF16), before, preferred_element_type=F32) + carry
        parts.append(jnp.sum(piece * ahead, axis=0, keepdims=True))
        carry = carry + jnp.sum(piece, axis=1, keepdims=True)
    rank = jnp.concatenate(parts, axis=1).astype(jnp.int32)
    full = jnp.max(carry[:buckets] + carry[buckets:], axis=0, keepdims=True) > CAP
    full = full | (jnp.max(carry, axis=0, keepdims=True) > CAP - LOW)
    over = full.astype(F32)
    tile_flags[t] = jnp.broadcast_to(over, (1, 128))

    spot = jnp.where(right, CAP - 1 - rank, rank)
    group = jnp.where(live, (bucket + 1) * GROUPS_IN + (spot >> (LOW.bit_length() - 1)), -1)
    place = spot & (LOW - 1)
    groups = packed.shape[0]
    to_group = (lax.broadcasted_iota(jnp.int32, (groups, slots), 0) == group).astype(F32).astype(BF16)
    at_place = lax.broadcasted_iota(jnp.int32, (LOW, slots), 0) == place

    def halves(x):
        high = x.astype(BF16).astype(F32)
        return high, x - high

    re_hi, re_lo = halves(vis_v[0:1])
    im_hi, im_lo = halves(vis_v[1:2])
    col = cell_v[1:2]
    pieces = [re_hi, im_hi, col >> 2, sup_v[...] * PLANES + wpl_v[...], re_lo, im_lo,
              (col & 3) * 64 + (row & (BUCKET - 1)) + 1, jnp.zeros((1, slots), F32)]
    spread = jnp.concatenate([jnp.where(at_place, x.astype(F32), 0.0).astype(BF16) for x in pieces], axis=0)
    moved = lax.dot_general(to_group, spread, (((1,), (1,)), ((), ())), preferred_element_type=F32)
    first, second = moved[:, 0:128], moved[:, 128:256]
    whole_1, whole_2 = first.astype(jnp.int32), second.astype(jnp.int32)
    lane = lax.broadcasted_iota(jnp.int32, first.shape, 1) // LOW
    packed[:, 0:128] = jnp.where(
        lane < 2, first + second,
        jnp.where(lane == 2, whole_1 * 4 + (whole_2 >> 6), pltpu.roll(whole_2, LOW, 1) & 63).astype(F32))
    klass = pltpu.roll(whole_1, LOW, 1)
    packed[:, 128:256] = jnp.where(
        lane == 0, klass >> 4,
        jnp.where(lane == 1, pltpu.roll(klass, LOW, 1) & (PLANES - 1),
                  jnp.where((lane == 2) & ((whole_2 & 63) > 0), 1, 0))).astype(F32)

    below, above = (t > 0).astype(jnp.int32), (t < nt - 1).astype(jnp.int32)
    pl.semaphore_wait(bar, nc - 1 + nt - 1 + below + above)

    def tile_flag(i, slot):
        return pltpu.make_async_remote_copy(
            src_ref=tile_flags.at[t], dst_ref=tile_flags.at[slot], send_sem=tf_send, recv_sem=tf_recv,
            device_id=(lax.rem(t + i, nt), c), device_id_type=MESH)

    for i in range(1, nt):
        tile_flag(i, t).start()

    width = 4 * GROUPS_IN

    def payload(i, slot):
        peer = lax.rem(c + i, nc)
        return pltpu.make_async_remote_copy(
            src_ref=packed.at[pl.ds(pl.multiple_of(8 * peer, 8), width)], dst_ref=got.at[slot], send_sem=send_sem,
            recv_sem=recv_sem.at[slot], device_id=(t, peer), device_id_type=MESH)

    for i in range(1, nc):
        payload(i, c).start()

    def edge_up():
        return pltpu.make_async_remote_copy(
            src_ref=packed.at[pl.ds(buckets * GROUPS_IN, GROUPS_IN)], dst_ref=edge.at[c, 0:GROUPS_IN], send_sem=edge_send.at[0],
            recv_sem=edge_recv.at[c], device_id=(t + 1, 0), device_id_type=MESH)

    def edge_down():
        return pltpu.make_async_remote_copy(
            src_ref=packed.at[pl.ds(GROUPS_IN, GROUPS_IN)], dst_ref=edge.at[c, 0:GROUPS_IN], send_sem=edge_send.at[1],
            recv_sem=edge_recv.at[c], device_id=(t - 1, nc - 1), device_id_type=MESH)

    @pl.when(t < nt - 1)
    def _():
        edge_up().start()

    @pl.when(t > 0)
    def _():
        edge_down().start()

    got[c] = packed[pl.ds(pl.multiple_of(8 * c, 8), width), :]

    def all_of(ref, count, sent, landed):
        return pltpu.make_async_remote_copy(
            src_ref=ref.at[0:count], dst_ref=ref.at[0:count], send_sem=sent, recv_sem=landed,
            device_id=(t, lax.rem(c + 1, nc)), device_id_type=MESH)

    table[...] = class_table()
    total[...] = jnp.zeros_like(total)

    spot = lax.broadcasted_iota(jnp.int32, (8, 128), 1) // LOW

    def fields(first, second, lift, picks):
        row_lanes = lax.broadcasted_iota(jnp.int32, first.shape, 1) // LOW == 3
        cells = first.astype(jnp.int32) - M
        cells = jnp.where(row_lanes, cells + lift, cells)
        klass = (second * float(PLANES) + pltpu.roll(second, 3 * LOW, 1)).astype(jnp.int32)

        def lines(x, offset):
            shifted = [pltpu.roll(x, ((b - offset) % 4) * LOW, 1) if (b - offset) % 4 else x for b in range(4)]
            made = []
            for pick in picks:
                parts = [jnp.broadcast_to(shifted[b][r : r + 1], (8, 128)) for b, r in enumerate(pick)]
                line = parts[0]
                for b in range(1, 4):
                    line = jnp.where(spot == b, parts[b], line)
                made.append(line)
            return made

        return lines(klass, 0), lines(cells, 3), lines(cells, 2), lines(first, 0), lines(first, 1)

    halves_at = (0, G // 64 - SPAN)
    lift = BUCKET * (lax.broadcasted_iota(jnp.int32, (width, 128), 0) // GROUPS_IN - 1) - 1

    here = 2 * (c // 2)

    def chip(k):
        q = k % 4
        dz = q + jnp.where(q == 2, 1, 0) - jnp.where(q == 3, 1, 0)
        z, y = (here // 2) % 4, here // 8
        return (((y + k // 4) % 2) * 4 + (z + dz) % 4) * 2

    def prepare(source, slot):
        made = [
            fields(got[x, :, 0:128], got[x, :, 128:256], lift, [[GROUPS_IN * b + g for b in range(4)] for g in EARLY])
            for x in (source, source + 1)
        ]
        for h in range(2):
            lay(*[jnp.concatenate([x[h], y[h]], axis=1) for x, y in zip(*made)], table, weights.at[slot, h],
                columns.at[slot, h], halves_at[h])

    def add_both(slot):
        for h in range(2):
            add(total, weights.at[slot, h], columns.at[slot, h], halves_at[h])

    def arrive(source):
        pltpu.make_async_remote_copy(
            src_ref=packed.at[pl.ds(0, width)], dst_ref=got.at[source], send_sem=send_sem,
            recv_sem=recv_sem.at[source], device_id=(t, source), device_id_type=MESH).wait_recv()

    arrive(here + (c + 1) % 2)
    prepare(here, 0)

    all_of(tile_flags, nt - 1, tf_send, tf_recv).wait_recv()
    chan_flags[c] = jnp.max(tile_flags[...], axis=0)

    for i in range(1, nc):
        pltpu.make_async_remote_copy(
            src_ref=chan_flags.at[c], dst_ref=chan_flags.at[c], send_sem=cf_send, recv_sem=cf_recv,
            device_id=(t, lax.rem(c + i, nc)), device_id_type=MESH).start()

    def two_chips(j, carry):
        for odd in (1, 0):
            source = chip(2 * j + 2 - odd)
            arrive(source)
            arrive(source + 1)
            prepare(source, odd)
            add_both(1 - odd)
        return carry

    chips = nc // 2
    lax.fori_loop(0, chips // 2 - 1, two_chips, 0)
    add_both(0)

    @pl.when(from_low | from_high)
    def _():
        for g in range(nc):
            pltpu.make_async_remote_copy(
                src_ref=packed.at[pl.ds(0, GROUPS_IN)], dst_ref=edge.at[g, 0:GROUPS_IN], send_sem=edge_send.at[0],
                recv_sem=edge_recv.at[g], device_id=(t, g), device_id_type=MESH).wait_recv()
        rows = edge[...].reshape(nc * 8, 256)
        lines = nc // 4
        picks = [[8 * (4 * n + b) + g for b in range(4)] for g in EARLY for n in range(lines)]
        made = fields(rows[:, 0:128], rows[:, 128:256], jnp.where(from_low, -BUCKET, 2 * BUCKET) - 1, picks)
        for h in range(2):
            for n in range(0, lines, 2):
                lay(*[jnp.concatenate(x[h * lines + n : h * lines + n + 2], axis=1) for x in made], table,
                    weights.at[n // 2, h], columns.at[n // 2, h], halves_at[h])
        for n in range(lines // 2):
            add_both(n)

    all_of(tile_flags, nt - 1, tf_send, tf_recv).wait_send()
    all_of(chan_flags, nc - 1, cf_send, cf_recv).wait_send()
    all_of(got, nc - 1, send_sem, recv_sem.at[0]).wait_send()

    @pl.when(t < nt - 1)
    def _():
        edge_up().wait_send()

    @pl.when(t > 0)
    def _():
        edge_down().wait_send()

    source = chip(chips - 1)
    arrive(source)
    arrive(source + 1)
    prepare(source, 1)
    list_left(got, edge, real, whole, number)
    add_both(1)

    all_of(chan_flags, nc - 1, cf_send, cf_recv).wait_recv()
    flag[0, 0] = (jnp.max(jnp.max(chan_flags[...], axis=0)) > 0.5).astype(jnp.int32)


def owned_rows(real, whole, number, table, begun, out, total, weights, columns):
    size = weights.shape[-1]
    lines = size // 128
    chunks = (jnp.max(number[...]).astype(jnp.int32) + 4 * lines - 1) // (4 * lines)
    total[...] = begun[...]

    def body(i, carry):
        def line(ref, f):
            return jnp.concatenate(
                [jnp.broadcast_to(ref[f, pl.ds(lines * i + h, 1), :], (8, 128)) for h in range(lines)], axis=1)

        lay(line(whole, 2), line(whole, 1), line(whole, 0), line(real, 0), line(real, 1), table, weights, columns)
        add(total, weights, columns)
        return carry

    lax.fori_loop(0, chunks, body, 0)
    out[:, 0, :] = total[0:64]
    out[:, 1, :] = total[64:128]


def per_device(visibilities, cell_offsets, support_index, w_plane, live_counts):
    nt, nc = lax.axis_size("tile"), lax.axis_size("chan")
    slots = visibilities.shape[-1]
    groups = (G // BUCKET + 2) * GROUPS_IN
    vmem = pl.BlockSpec(memory_space=pltpu.VMEM)
    left_lines = nc * 5 * (GROUPS_IN - len(EARLY)) // 4
    table, begun, real, whole, number, flag = pl.pallas_call(
        exchange,
        out_shape=(
            jax.ShapeDtypeStruct((2 * M, 4 * PLANES), BF16),
            jax.ShapeDtypeStruct((2 * G // nc, G), F32),
            jax.ShapeDtypeStruct((2, left_lines, 128), F32),
            jax.ShapeDtypeStruct((3, left_lines, 128), jnp.int32),
            jax.ShapeDtypeStruct((8, 128), F32),
            jax.ShapeDtypeStruct((1, 1), jnp.int32),
        ),
        in_specs=[pl.BlockSpec(memory_space=pltpu.MemorySpace.HBM)] * 5,
        out_specs=(vmem, vmem, vmem, vmem, vmem, pl.BlockSpec(memory_space=pltpu.SMEM)),
        scratch_shapes=[
            pltpu.VMEM((nc, 4 * GROUPS_IN, FIELDS * LOW), F32),
            pltpu.VMEM((nc, 8, FIELDS * LOW), F32),
            pltpu.VMEM((2, slots), F32),
            pltpu.VMEM((2, slots), jnp.int32),
            pltpu.VMEM((1, slots), jnp.int32),
            pltpu.VMEM((1, slots), jnp.int32),
            pltpu.VMEM((1, 1), jnp.int32),
            pltpu.VMEM((groups, FIELDS * LOW), F32),
            pltpu.VMEM((nt, 1, 128), F32),
            pltpu.VMEM((nc, 1, 128), F32),
            pltpu.VMEM((2, 2, 2 * G // nc, 256), BF16),
            pltpu.VMEM((2, 2, 64 * SPAN, 256), BF16),
            pltpu.SemaphoreType.DMA((5,)),
            pltpu.SemaphoreType.DMA,
            pltpu.SemaphoreType.DMA((nc,)),
            pltpu.SemaphoreType.DMA((2,)),
            pltpu.SemaphoreType.DMA((nc,)),
            pltpu.SemaphoreType.DMA,
            pltpu.SemaphoreType.DMA,
            pltpu.SemaphoreType.DMA,
            pltpu.SemaphoreType.DMA,
        ],
        compiler_params=pltpu.CompilerParams(collective_id=0, has_side_effects=True, vmem_limit_bytes=62 << 20),
    )(visibilities, cell_offsets, support_index, w_plane, live_counts)


    def usual(*_):
        return pl.pallas_call(
            owned_rows,
            out_shape=jax.ShapeDtypeStruct((G // nc, 2, G), F32),
            in_specs=[vmem] * 5,
            out_specs=vmem,
            scratch_shapes=[
                pltpu.VMEM((2 * G // nc, G), F32),
                pltpu.VMEM((2 * G // nc, 512), BF16),
                pltpu.VMEM((G, 512), BF16),
            ],
            compiler_params=pltpu.CompilerParams(vmem_limit_bytes=40 << 20),
        )(real, whole, number, table, begun)

    return lax.switch(
        flag[0, 0], (usual, any_cells), visibilities, cell_offsets, support_index, w_plane, live_counts
    )


def solution(mesh):
    in_specs = (
        P("tile", "chan", None, None),
        P("tile", "chan", None, None),
        P("tile", "chan", None),
        P("tile", "chan", None),
        P("tile", "chan"),
    )
    out_specs = P(("tile", "chan"), None, None)
    return jax.shard_map(
        per_device, mesh=mesh, in_specs=in_specs, out_specs=out_specs, check_vma=False
    )
```

```python
import functools
import math

import jax
import jax.numpy as jnp
from jax import lax
from jax.experimental import pallas as pl
from jax.experimental.pallas import tpu as pltpu
from jax.sharding import PartitionSpec as P

G = 1024
M = 32
PLANES = 16
BETA = 7.0

BUCKET = 32
CAP = 128
LOW = 32
GROUPS_IN = CAP // LOW
EARLY = (0, GROUPS_IN - 1)
SPAN = 10
FIELDS = 8
MESH = pl.DeviceIdType.MESH
F32 = jnp.float32
BF16 = jnp.bfloat16


def bessel_zero(value):
    quarter = value * value * 0.25
    term = jnp.ones_like(value)
    total = jnp.ones_like(value)
    for index in range(1, 30):
        term = term * quarter * (1.0 / float(index * index))
        total = total + term
    return total


def kernel_values(distance, half_width, w_coef):
    ratio = distance / half_width
    inside = jnp.abs(ratio) < 1.0
    radius = jnp.sqrt(jnp.maximum(1.0 - ratio * ratio, 0.0))
    bessel = bessel_zero(BETA * radius) / bessel_zero(jnp.float32(BETA))
    taper = jnp.cos(jnp.pi * w_coef * ratio * ratio)
    return jnp.where(inside, bessel * taper, jnp.float32(0.0))


def flatten_groups(vis_block, offset_block, support_block, plane_block, count_block):
    slot_total = vis_block.shape[-1]
    slot_ids = jnp.arange(slot_total, dtype=jnp.int32)
    live = (slot_ids[None, :] < count_block[:, None]).astype(jnp.float32).reshape(-1)
    real_part = vis_block[:, 0].reshape(-1) * live
    imag_part = vis_block[:, 1].reshape(-1) * live
    row_cell = offset_block[:, 0].reshape(-1).astype(jnp.float32)
    col_cell = offset_block[:, 1].reshape(-1).astype(jnp.float32)
    half_width = 8.0 * (support_block.reshape(-1) + 1).astype(jnp.float32)
    w_coef = 0.5 * (plane_block.reshape(-1) + 1).astype(jnp.float32) / PLANES
    return (real_part, imag_part, row_cell, col_cell, half_width, w_coef)


def grid_part(flat, row_start, row_count, width):
    total_vis = flat[0].shape[0]
    block_len = math.gcd(total_vis, 512)
    stacked = tuple((item.reshape(total_vis // block_len, block_len) for item in flat))
    row_pos = (row_start + jnp.arange(row_count, dtype=jnp.int32)).astype(jnp.float32)
    col_pos = jnp.arange(width, dtype=jnp.int32).astype(jnp.float32)

    def step_block(total, values):
        real_part, imag_part, row_cell, col_cell, half_width, w_coef = values
        row_weights = kernel_values(
            row_pos[None, :] - row_cell[:, None], half_width[:, None], w_coef[:, None]
        ).astype(jnp.bfloat16)
        col_kern = kernel_values(
            col_pos[None, :] - col_cell[:, None], half_width[:, None], w_coef[:, None]
        )
        col_weights = jnp.concatenate(
            [real_part[:, None] * col_kern, imag_part[:, None] * col_kern], axis=1
        ).astype(jnp.bfloat16)
        product = lax.dot_general(
            row_weights, col_weights, (((0,), (0,)), ((), ())), preferred_element_type=jnp.float32
        )
        return (total + product, None)

    start_total = jnp.zeros((row_count, 2 * width), jnp.float32)
    total, _ = lax.scan(step_block, start_total, stacked)
    return total.reshape(row_count, 2, width)


def any_cells(visibilities, cell_offsets, support_index, w_plane, live_counts):
    tiles, parts = lax.axis_size("tile"), lax.axis_size("chan")
    share = G // parts
    first_row = lax.axis_index("chan") * share - M
    held = jnp.stack(
        flatten_groups(visibilities[0], cell_offsets[0], support_index[0], w_plane[0], live_counts[0])
    )

    def step(_, carry):
        total, held = carry
        total = total + grid_part(held, first_row, share + 2 * M, G)
        return total, lax.ppermute(held, "chan", [(i, (i + 1) % parts) for i in range(parts)])

    total, _ = lax.fori_loop(0, parts, step, (jnp.zeros((share + 2 * M, 2, G), F32), held))
    last = parts - 1
    left_in = lax.ppermute(
        total[share + M :], ("tile", "chan"), [(t * parts + last, (t + 1) * parts) for t in range(tiles - 1)]
    )
    right_in = lax.ppermute(
        total[:M], ("tile", "chan"), [(t * parts, (t - 1) * parts + last) for t in range(1, tiles)]
    )
    owned = total[M : M + share]
    return owned.at[:M].add(left_in).at[share - M :].add(right_in)


def class_table():
    shape = (2 * M, 4 * PLANES)
    klass = lax.broadcasted_iota(jnp.int32, shape, 1)
    distance = jnp.abs(lax.broadcasted_iota(jnp.int32, shape, 0) - M).astype(F32)
    half = (8 * (klass // PLANES + 1)).astype(F32)
    w_coef = 0.5 * (klass % PLANES + 1).astype(F32) / PLANES
    ratio = jnp.minimum(distance / half, 1.0)
    square = ratio * ratio
    radius = jnp.sqrt(jnp.maximum(1.0 - square, 0.0))
    bessel = bessel_zero(BETA * radius) / bessel_zero(jnp.full(shape, BETA, F32))
    taper = jnp.cos(jnp.pi * w_coef * square)
    return jnp.where(ratio < 1.0, bessel * taper, 0.0).astype(BF16)


def turned(values, by, sub):
    for bit in (32, 16, 8):
        chosen = (by & bit) != 0
        values = [jnp.where(chosen, values[(k - bit // 8) % 8], values[k]) for k in range(8)]
    fine = by & 7
    taken = [jnp.take_along_axis(x, (sub - fine) & 7, axis=0, mode="promise_in_bounds") for x in values]
    wrapped = sub < fine
    return [jnp.where(wrapped, taken[(k - 1) % 8], taken[k]) for k in range(8)]


def lay(klass, row, col, re, im, table, weights, columns, start=0):
    sub = lax.broadcasted_iota(jnp.int32, klass.shape, 0)
    hot = jnp.concatenate([(klass == sub + 8 * k).astype(F32) for k in range(8)], axis=0).astype(BF16)
    values = jnp.dot(table[...], hot, preferred_element_type=F32)
    values = [values[8 * k : 8 * k + 8] for k in range(8)]
    by, first = row & 63, row >> 6
    mine = [
        jnp.where(jnp.where(sub + 8 * k < by, first + 1, first) == 0, x, 0.0)
        for k, x in enumerate(turned(values, by, sub))
    ]
    weights[0:64] = jnp.concatenate([x * re for x in mine], axis=0).astype(BF16)
    weights[64:128] = jnp.concatenate([x * im for x in mine], axis=0).astype(BF16)
    by, first = col & 63, col >> 6
    window = jnp.concatenate(turned(values, by, sub), axis=0).astype(BF16)
    block = jnp.concatenate(
        [jnp.where(sub + 8 * k < by, first + 1, first).astype(F32) for k in range(8)], axis=0).astype(BF16)
    for b in range(columns.shape[0] // 64):
        columns[64 * b : 64 * b + 64] = jnp.where(block == jnp.asarray(start + b, BF16), window, jnp.asarray(0, BF16))


def add(total, weights, columns, start=0):
    stop = 64 * start + columns.shape[0]
    total[:, 64 * start : stop] += lax.dot_general(
        weights[...], columns[...], (((1,), (1,)), ((), ())), preferred_element_type=F32)


def list_left(got, edge, real, whole, number):
    c = lax.axis_index("chan")
    nc, per = got.shape[0], got.shape[1]
    main = nc * per
    count = main + nc * 8
    left = 4 * real.shape[1]
    quarter = left // 4

    lanes = lax.broadcasted_iota(jnp.int32, (1, 256), 1) // LOW
    both = jnp.concatenate([got[...].reshape(main, 256), edge[...].reshape(nc * 8, 256)], axis=0)
    index = lax.broadcasted_iota(jnp.int32, (count, 256), 0)
    shift = jnp.where(index < main, BUCKET * ((index % per) // GROUPS_IN - 1), jnp.where(c == 0, -BUCKET, 2 * BUCKET))
    both = both + jnp.where(lanes == 3, shift - 1, 0).astype(F32)
    used = jnp.max(both[:, 128:256].T[2 * LOW : 3 * LOW], axis=0, keepdims=True)
    at = lax.broadcasted_iota(jnp.int32, (1, count), 1) % GROUPS_IN
    used = jnp.where((at == EARLY[0]) | (at == EARLY[1]), 0.0, used)
    before = (
        lax.broadcasted_iota(jnp.int32, (count, count), 0) < lax.broadcasted_iota(jnp.int32, (count, count), 1)
    ).astype(F32).astype(BF16)
    rank = jnp.dot(jnp.broadcast_to(used, (8, count)).astype(BF16), before, preferred_element_type=F32)[0:1]
    rank = jnp.where(used > 0.5, rank, -1.0)
    place = lax.broadcasted_iota(jnp.int32, (left, count), 0)
    place = (4 * (place % quarter) + place // quarter).astype(F32)
    pick = jnp.where(place == rank, 1.0, 0.0).astype(BF16)
    high = both.astype(BF16)
    low = (both - high.astype(F32)).astype(BF16)
    rows = jnp.dot(pick, high, preferred_element_type=F32) + jnp.dot(pick, low, preferred_element_type=F32)
    spot = lax.broadcasted_iota(jnp.int32, (quarter, 128), 1) // LOW

    def field(f):
        part, offset = divmod(f, 4)
        result = None
        for s in range(4):
            x = rows[s * quarter : (s + 1) * quarter, 128 * part : 128 * part + 128]
            if (s - offset) % 4:
                x = pltpu.roll(x, ((s - offset) % 4) * LOW, 1)
            result = x if result is None else jnp.where(spot == s, x, result)
        return result

    real[0], real[1] = field(0), field(1)
    whole[0], whole[1] = field(2).astype(jnp.int32) - M, field(3).astype(jnp.int32) - M
    whole[2] = (field(4) * float(PLANES) + field(5)).astype(jnp.int32)
    number[...] = jnp.broadcast_to(jnp.sum(used, axis=1, keepdims=True), number.shape)


def exchange(vis, cell, sup, wpl, cnt, table, total, real, whole, number, flag, got, edge, vis_v, cell_v, sup_v, wpl_v, cnt_v, packed, tile_flags, chan_flags,
             weights, columns,
             load_sem, send_sem, recv_sem, edge_send, edge_recv, tf_send, tf_recv, cf_send, cf_recv):
    t, c = lax.axis_index("tile"), lax.axis_index("chan")
    nt, nc = lax.axis_size("tile"), lax.axis_size("chan")
    slots = vis_v.shape[-1]
    loads = [
        pltpu.make_async_copy(cell.at[0, 0], cell_v, load_sem.at[0]),
        pltpu.make_async_copy(cnt, cnt_v, load_sem.at[1]),
        pltpu.make_async_copy(vis.at[0, 0], vis_v, load_sem.at[2]),
        pltpu.make_async_copy(sup.at[0], sup_v, load_sem.at[3]),
        pltpu.make_async_copy(wpl.at[0], wpl_v, load_sem.at[4]),
    ]
    for load in loads:
        load.start()
    edge[...] = jnp.zeros_like(edge)

    bar = pltpu.get_barrier_semaphore()
    for i in range(1, nc):
        pl.semaphore_signal(bar, inc=1, device_id=(t, lax.rem(c + i, nc)), device_id_type=MESH)
    for i in range(1, nt):
        pl.semaphore_signal(bar, inc=1, device_id=(lax.rem(t + i, nt), c), device_id_type=MESH)
    from_low = (c == 0) & (t > 0)
    from_high = (c == nc - 1) & (t < nt - 1)

    @pl.when(from_low)
    def _():
        for g in range(nc):
            pl.semaphore_signal(bar, inc=1, device_id=(t - 1, g), device_id_type=MESH)

    @pl.when(from_high)
    def _():
        for g in range(nc):
            pl.semaphore_signal(bar, inc=1, device_id=(t + 1, g), device_id_type=MESH)

    for load in loads[:2]:
        load.wait()

    live = lax.broadcasted_iota(jnp.int32, (1, slots), 1) < cnt_v[...]
    row = cell_v[0:1]
    buckets = G // BUCKET
    bucket = row // BUCKET
    right = cell_v[1:2] >= G // 2
    side = jnp.where(live, bucket + jnp.where(right, buckets, 0), -1)
    hot = (lax.broadcasted_iota(jnp.int32, (2 * buckets, slots), 0) == side).astype(F32)
    step = 256
    before = (
        lax.broadcasted_iota(jnp.int32, (step, step), 0) < lax.broadcasted_iota(jnp.int32, (step, step), 1)
    ).astype(F32).astype(BF16)
    parts = []
    carry = jnp.zeros((2 * buckets, 1), F32)
    for s in range(0, slots, step):
        piece = hot[:, s : s + step]
        ahead = jnp.dot(piece.astype(BF16), before, preferred_element_type=F32) + carry
        parts.append(jnp.sum(piece * ahead, axis=0, keepdims=True))
        carry = carry + jnp.sum(piece, axis=1, keepdims=True)
    rank = jnp.concatenate(parts, axis=1).astype(jnp.int32)
    full = jnp.max(carry[:buckets] + carry[buckets:], axis=0, keepdims=True) > CAP
    full = full | (jnp.max(carry, axis=0, keepdims=True) > CAP - LOW)
    over = full.astype(F32)
    tile_flags[t] = jnp.broadcast_to(over, (1, 128))

    spot = jnp.where(right, CAP - 1 - rank, rank)
    group = jnp.where(live, (bucket + 1) * GROUPS_IN + (spot >> (LOW.bit_length() - 1)), -1)
    place = spot & (LOW - 1)
    groups = packed.shape[0]
    to_group = (lax.broadcasted_iota(jnp.int32, (groups, slots), 0) == group).astype(F32).astype(BF16)
    at_place = lax.broadcasted_iota(jnp.int32, (LOW, slots), 0) == place

    def halves(x):
        high = x.astype(BF16).astype(F32)
        return high, x - high

    for load in loads[2:]:
        load.wait()
    re_hi, re_lo = halves(vis_v[0:1])
    im_hi, im_lo = halves(vis_v[1:2])
    col = cell_v[1:2]
    pieces = [re_hi, im_hi, col >> 2, sup_v[...] * PLANES + wpl_v[...], re_lo, im_lo,
              (col & 3) * 64 + (row & (BUCKET - 1)) + 1, jnp.zeros((1, slots), F32)]
    spread = jnp.concatenate([jnp.where(at_place, x.astype(F32), 0.0).astype(BF16) for x in pieces], axis=0)
    moved = lax.dot_general(to_group, spread, (((1,), (1,)), ((), ())), preferred_element_type=F32)
    first, second = moved[:, 0:128], moved[:, 128:256]
    whole_1, whole_2 = first.astype(jnp.int32), second.astype(jnp.int32)
    lane = lax.broadcasted_iota(jnp.int32, first.shape, 1) // LOW
    packed[:, 0:128] = jnp.where(
        lane < 2, first + second,
        jnp.where(lane == 2, whole_1 * 4 + (whole_2 >> 6), pltpu.roll(whole_2, LOW, 1) & 63).astype(F32))
    klass = pltpu.roll(whole_1, LOW, 1)
    packed[:, 128:256] = jnp.where(
        lane == 0, klass >> 4,
        jnp.where(lane == 1, pltpu.roll(klass, LOW, 1) & (PLANES - 1),
                  jnp.where((lane == 2) & ((whole_2 & 63) > 0), 1, 0))).astype(F32)

    below, above = (t > 0).astype(jnp.int32), (t < nt - 1).astype(jnp.int32)
    pl.semaphore_wait(bar, nc - 1 + nt - 1 + below + above)

    def tile_flag(i, slot):
        return pltpu.make_async_remote_copy(
            src_ref=tile_flags.at[t], dst_ref=tile_flags.at[slot], send_sem=tf_send, recv_sem=tf_recv,
            device_id=(lax.rem(t + i, nt), c), device_id_type=MESH)

    for i in range(1, nt):
        tile_flag(i, t).start()

    width = 4 * GROUPS_IN

    def payload(i, slot):
        peer = lax.rem(c + i, nc)
        return pltpu.make_async_remote_copy(
            src_ref=packed.at[pl.ds(pl.multiple_of(8 * peer, 8), width)], dst_ref=got.at[slot], send_sem=send_sem,
            recv_sem=recv_sem.at[slot], device_id=(t, peer), device_id_type=MESH)

    for i in range(1, nc):
        payload(i, c).start()

    def edge_up():
        return pltpu.make_async_remote_copy(
            src_ref=packed.at[pl.ds(buckets * GROUPS_IN, GROUPS_IN)], dst_ref=edge.at[c, 0:GROUPS_IN], send_sem=edge_send.at[0],
            recv_sem=edge_recv.at[c], device_id=(t + 1, 0), device_id_type=MESH)

    def edge_down():
        return pltpu.make_async_remote_copy(
            src_ref=packed.at[pl.ds(GROUPS_IN, GROUPS_IN)], dst_ref=edge.at[c, 0:GROUPS_IN], send_sem=edge_send.at[1],
            recv_sem=edge_recv.at[c], device_id=(t - 1, nc - 1), device_id_type=MESH)

    @pl.when(t < nt - 1)
    def _():
        edge_up().start()

    @pl.when(t > 0)
    def _():
        edge_down().start()

    got[c] = packed[pl.ds(pl.multiple_of(8 * c, 8), width), :]

    def all_of(ref, count, sent, landed):
        return pltpu.make_async_remote_copy(
            src_ref=ref.at[0:count], dst_ref=ref.at[0:count], send_sem=sent, recv_sem=landed,
            device_id=(t, lax.rem(c + 1, nc)), device_id_type=MESH)

    table[...] = class_table()
    total[...] = jnp.zeros_like(total)

    spot = lax.broadcasted_iota(jnp.int32, (8, 128), 1) // LOW

    def fields(first, second, lift, picks):
        row_lanes = lax.broadcasted_iota(jnp.int32, first.shape, 1) // LOW == 3
        cells = first.astype(jnp.int32) - M
        cells = jnp.where(row_lanes, cells + lift, cells)
        klass = (second * float(PLANES) + pltpu.roll(second, 3 * LOW, 1)).astype(jnp.int32)

        def lines(x, offset):
            shifted = [pltpu.roll(x, ((b - offset) % 4) * LOW, 1) if (b - offset) % 4 else x for b in range(4)]
            made = []
            for pick in picks:
                parts = [jnp.broadcast_to(shifted[b][r : r + 1], (8, 128)) for b, r in enumerate(pick)]
                line = parts[0]
                for b in range(1, 4):
                    line = jnp.where(spot == b, parts[b], line)
                made.append(line)
            return made

        return lines(klass, 0), lines(cells, 3), lines(cells, 2), lines(first, 0), lines(first, 1)

    halves_at = (0, G // 64 - SPAN)
    lift = BUCKET * (lax.broadcasted_iota(jnp.int32, (width, 128), 0) // GROUPS_IN - 1) - 1

    here = 2 * (c // 2)

    def chip(k):
        q = k % 4
        dz = q + jnp.where(q == 2, 1, 0) - jnp.where(q == 3, 1, 0)
        z, y = (here // 2) % 4, here // 8
        return (((y + k // 4) % 2) * 4 + (z + dz) % 4) * 2

    def prepare(source, slot):
        made = [
            fields(got[x, :, 0:128], got[x, :, 128:256], lift, [[GROUPS_IN * b + g for b in range(4)] for g in EARLY])
            for x in (source, source + 1)
        ]
        for h in range(2):
            lay(*[jnp.concatenate([x[h], y[h]], axis=1) for x, y in zip(*made)], table, weights.at[slot, h],
                columns.at[slot, h], halves_at[h])

    def add_both(slot):
        for h in range(2):
            add(total, weights.at[slot, h], columns.at[slot, h], halves_at[h])

    def arrive(source):
        pltpu.make_async_remote_copy(
            src_ref=packed.at[pl.ds(0, width)], dst_ref=got.at[source], send_sem=send_sem,
            recv_sem=recv_sem.at[source], device_id=(t, source), device_id_type=MESH).wait_recv()

    arrive(here + (c + 1) % 2)
    prepare(here, 0)

    all_of(tile_flags, nt - 1, tf_send, tf_recv).wait_recv()
    chan_flags[c] = jnp.max(tile_flags[...], axis=0)

    for i in range(1, nc):
        pltpu.make_async_remote_copy(
            src_ref=chan_flags.at[c], dst_ref=chan_flags.at[c], send_sem=cf_send, recv_sem=cf_recv,
            device_id=(t, lax.rem(c + i, nc)), device_id_type=MESH).start()

    def two_chips(j, carry):
        for odd in (1, 0):
            source = chip(2 * j + 2 - odd)
            arrive(source)
            arrive(source + 1)
            prepare(source, odd)
            add_both(1 - odd)
        return carry

    chips = nc // 2
    lax.fori_loop(0, chips // 2 - 1, two_chips, 0)
    add_both(0)

    @pl.when(from_low | from_high)
    def _():
        for g in range(nc):
            pltpu.make_async_remote_copy(
                src_ref=packed.at[pl.ds(0, GROUPS_IN)], dst_ref=edge.at[g, 0:GROUPS_IN], send_sem=edge_send.at[0],
                recv_sem=edge_recv.at[g], device_id=(t, g), device_id_type=MESH).wait_recv()
        rows = edge[...].reshape(nc * 8, 256)
        lines = nc // 4
        picks = [[8 * (4 * n + b) + g for b in range(4)] for g in EARLY for n in range(lines)]
        made = fields(rows[:, 0:128], rows[:, 128:256], jnp.where(from_low, -BUCKET, 2 * BUCKET) - 1, picks)
        for h in range(2):
            for n in range(0, lines, 2):
                lay(*[jnp.concatenate(x[h * lines + n : h * lines + n + 2], axis=1) for x in made], table,
                    weights.at[n // 2, h], columns.at[n // 2, h], halves_at[h])
        for n in range(lines // 2):
            add_both(n)

    all_of(tile_flags, nt - 1, tf_send, tf_recv).wait_send()
    all_of(chan_flags, nc - 1, cf_send, cf_recv).wait_send()
    all_of(got, nc - 1, send_sem, recv_sem.at[0]).wait_send()

    @pl.when(t < nt - 1)
    def _():
        edge_up().wait_send()

    @pl.when(t > 0)
    def _():
        edge_down().wait_send()

    source = chip(chips - 1)
    arrive(source)
    arrive(source + 1)
    prepare(source, 1)
    list_left(got, edge, real, whole, number)
    add_both(1)

    all_of(chan_flags, nc - 1, cf_send, cf_recv).wait_recv()
    flag[0, 0] = (jnp.max(jnp.max(chan_flags[...], axis=0)) > 0.5).astype(jnp.int32)


def owned_rows(real, whole, number, table, begun, out, total, weights, columns):
    size = weights.shape[-1]
    lines = size // 128
    chunks = (jnp.max(number[...]).astype(jnp.int32) + 4 * lines - 1) // (4 * lines)
    total[...] = begun[...]

    def body(i, carry):
        def line(ref, f):
            return jnp.concatenate(
                [jnp.broadcast_to(ref[f, pl.ds(lines * i + h, 1), :], (8, 128)) for h in range(lines)], axis=1)

        lay(line(whole, 2), line(whole, 1), line(whole, 0), line(real, 0), line(real, 1), table, weights, columns)
        add(total, weights, columns)
        return carry

    lax.fori_loop(0, chunks, body, 0)
    out[:, 0, :] = total[0:64]
    out[:, 1, :] = total[64:128]


def per_device(visibilities, cell_offsets, support_index, w_plane, live_counts):
    nt, nc = lax.axis_size("tile"), lax.axis_size("chan")
    slots = visibilities.shape[-1]
    groups = (G // BUCKET + 2) * GROUPS_IN
    vmem = pl.BlockSpec(memory_space=pltpu.VMEM)
    left_lines = nc * 5 * (GROUPS_IN - len(EARLY)) // 4
    table, begun, real, whole, number, flag = pl.pallas_call(
        exchange,
        out_shape=(
            jax.ShapeDtypeStruct((2 * M, 4 * PLANES), BF16),
            jax.ShapeDtypeStruct((2 * G // nc, G), F32),
            jax.ShapeDtypeStruct((2, left_lines, 128), F32),
            jax.ShapeDtypeStruct((3, left_lines, 128), jnp.int32),
            jax.ShapeDtypeStruct((8, 128), F32),
            jax.ShapeDtypeStruct((1, 1), jnp.int32),
        ),
        in_specs=[pl.BlockSpec(memory_space=pltpu.MemorySpace.HBM)] * 5,
        out_specs=(vmem, vmem, vmem, vmem, vmem, pl.BlockSpec(memory_space=pltpu.SMEM)),
        scratch_shapes=[
            pltpu.VMEM((nc, 4 * GROUPS_IN, FIELDS * LOW), F32),
            pltpu.VMEM((nc, 8, FIELDS * LOW), F32),
            pltpu.VMEM((2, slots), F32),
            pltpu.VMEM((2, slots), jnp.int32),
            pltpu.VMEM((1, slots), jnp.int32),
            pltpu.VMEM((1, slots), jnp.int32),
            pltpu.VMEM((1, 1), jnp.int32),
            pltpu.VMEM((groups, FIELDS * LOW), F32),
            pltpu.VMEM((nt, 1, 128), F32),
            pltpu.VMEM((nc, 1, 128), F32),
            pltpu.VMEM((2, 2, 2 * G // nc, 256), BF16),
            pltpu.VMEM((2, 2, 64 * SPAN, 256), BF16),
            pltpu.SemaphoreType.DMA((5,)),
            pltpu.SemaphoreType.DMA,
            pltpu.SemaphoreType.DMA((nc,)),
            pltpu.SemaphoreType.DMA((2,)),
            pltpu.SemaphoreType.DMA((nc,)),
            pltpu.SemaphoreType.DMA,
            pltpu.SemaphoreType.DMA,
            pltpu.SemaphoreType.DMA,
            pltpu.SemaphoreType.DMA,
        ],
        compiler_params=pltpu.CompilerParams(collective_id=0, has_side_effects=True, vmem_limit_bytes=62 << 20),
    )(visibilities, cell_offsets, support_index, w_plane, live_counts)


    def usual(*_):
        return pl.pallas_call(
            owned_rows,
            out_shape=jax.ShapeDtypeStruct((G // nc, 2, G), F32),
            in_specs=[vmem] * 5,
            out_specs=vmem,
            scratch_shapes=[
                pltpu.VMEM((2 * G // nc, G), F32),
                pltpu.VMEM((2 * G // nc, 512), BF16),
                pltpu.VMEM((G, 512), BF16),
            ],
            compiler_params=pltpu.CompilerParams(vmem_limit_bytes=40 << 20),
        )(real, whole, number, table, begun)

    return lax.switch(
        flag[0, 0], (usual, any_cells), visibilities, cell_offsets, support_index, w_plane, live_counts
    )


def solution(mesh):
    in_specs = (
        P("tile", "chan", None, None),
        P("tile", "chan", None, None),
        P("tile", "chan", None),
        P("tile", "chan", None),
        P("tile", "chan"),
    )
    out_specs = P(("tile", "chan"), None, None)
    return jax.shard_map(
        per_device, mesh=mesh, in_specs=in_specs, out_specs=out_specs, check_vma=False
    )
```

```python
import functools
import math

import jax
import jax.numpy as jnp
from jax import lax
from jax.experimental import pallas as pl
from jax.experimental.pallas import tpu as pltpu
from jax.sharding import PartitionSpec as P

G = 1024
M = 32
PLANES = 16
BETA = 7.0

BUCKET = 32
CAP = 128
LOW = 32
GROUPS_IN = CAP // LOW
EARLY = (0, GROUPS_IN - 1)
SPAN = 10
FIELDS = 8
MESH = pl.DeviceIdType.MESH
F32 = jnp.float32
BF16 = jnp.bfloat16


def bessel_zero(value):
    quarter = value * value * 0.25
    term = jnp.ones_like(value)
    total = jnp.ones_like(value)
    for index in range(1, 30):
        term = term * quarter * (1.0 / float(index * index))
        total = total + term
    return total


def kernel_values(distance, half_width, w_coef):
    ratio = distance / half_width
    inside = jnp.abs(ratio) < 1.0
    radius = jnp.sqrt(jnp.maximum(1.0 - ratio * ratio, 0.0))
    bessel = bessel_zero(BETA * radius) / bessel_zero(jnp.float32(BETA))
    taper = jnp.cos(jnp.pi * w_coef * ratio * ratio)
    return jnp.where(inside, bessel * taper, jnp.float32(0.0))


def flatten_groups(vis_block, offset_block, support_block, plane_block, count_block):
    slot_total = vis_block.shape[-1]
    slot_ids = jnp.arange(slot_total, dtype=jnp.int32)
    live = (slot_ids[None, :] < count_block[:, None]).astype(jnp.float32).reshape(-1)
    real_part = vis_block[:, 0].reshape(-1) * live
    imag_part = vis_block[:, 1].reshape(-1) * live
    row_cell = offset_block[:, 0].reshape(-1).astype(jnp.float32)
    col_cell = offset_block[:, 1].reshape(-1).astype(jnp.float32)
    half_width = 8.0 * (support_block.reshape(-1) + 1).astype(jnp.float32)
    w_coef = 0.5 * (plane_block.reshape(-1) + 1).astype(jnp.float32) / PLANES
    return (real_part, imag_part, row_cell, col_cell, half_width, w_coef)


def grid_part(flat, row_start, row_count, width):
    total_vis = flat[0].shape[0]
    block_len = math.gcd(total_vis, 512)
    stacked = tuple((item.reshape(total_vis // block_len, block_len) for item in flat))
    row_pos = (row_start + jnp.arange(row_count, dtype=jnp.int32)).astype(jnp.float32)
    col_pos = jnp.arange(width, dtype=jnp.int32).astype(jnp.float32)

    def step_block(total, values):
        real_part, imag_part, row_cell, col_cell, half_width, w_coef = values
        row_weights = kernel_values(
            row_pos[None, :] - row_cell[:, None], half_width[:, None], w_coef[:, None]
        ).astype(jnp.bfloat16)
        col_kern = kernel_values(
            col_pos[None, :] - col_cell[:, None], half_width[:, None], w_coef[:, None]
        )
        col_weights = jnp.concatenate(
            [real_part[:, None] * col_kern, imag_part[:, None] * col_kern], axis=1
        ).astype(jnp.bfloat16)
        product = lax.dot_general(
            row_weights, col_weights, (((0,), (0,)), ((), ())), preferred_element_type=jnp.float32
        )
        return (total + product, None)

    start_total = jnp.zeros((row_count, 2 * width), jnp.float32)
    total, _ = lax.scan(step_block, start_total, stacked)
    return total.reshape(row_count, 2, width)


def any_cells(visibilities, cell_offsets, support_index, w_plane, live_counts):
    tiles, parts = lax.axis_size("tile"), lax.axis_size("chan")
    share = G // parts
    first_row = lax.axis_index("chan") * share - M
    held = jnp.stack(
        flatten_groups(visibilities[0], cell_offsets[0], support_index[0], w_plane[0], live_counts[0])
    )

    def step(_, carry):
        total, held = carry
        total = total + grid_part(held, first_row, share + 2 * M, G)
        return total, lax.ppermute(held, "chan", [(i, (i + 1) % parts) for i in range(parts)])

    total, _ = lax.fori_loop(0, parts, step, (jnp.zeros((share + 2 * M, 2, G), F32), held))
    last = parts - 1
    left_in = lax.ppermute(
        total[share + M :], ("tile", "chan"), [(t * parts + last, (t + 1) * parts) for t in range(tiles - 1)]
    )
    right_in = lax.ppermute(
        total[:M], ("tile", "chan"), [(t * parts, (t - 1) * parts + last) for t in range(1, tiles)]
    )
    owned = total[M : M + share]
    return owned.at[:M].add(left_in).at[share - M :].add(right_in)


def class_table():
    shape = (2 * M, 4 * PLANES)
    klass = lax.broadcasted_iota(jnp.int32, shape, 1)
    distance = jnp.abs(lax.broadcasted_iota(jnp.int32, shape, 0) - M).astype(F32)
    half = (8 * (klass // PLANES + 1)).astype(F32)
    w_coef = 0.5 * (klass % PLANES + 1).astype(F32) / PLANES
    ratio = jnp.minimum(distance / half, 1.0)
    square = ratio * ratio
    radius = jnp.sqrt(jnp.maximum(1.0 - square, 0.0))
    bessel = bessel_zero(BETA * radius) / bessel_zero(jnp.full(shape, BETA, F32))
    taper = jnp.cos(jnp.pi * w_coef * square)
    return jnp.where(ratio < 1.0, bessel * taper, 0.0).astype(BF16)


def turned(values, by, sub):
    for bit in (32, 16, 8):
        chosen = (by & bit) != 0
        values = [jnp.where(chosen, values[(k - bit // 8) % 8], values[k]) for k in range(8)]
    fine = by & 7
    taken = [jnp.take_along_axis(x, (sub - fine) & 7, axis=0, mode="promise_in_bounds") for x in values]
    wrapped = sub < fine
    return [jnp.where(wrapped, taken[(k - 1) % 8], taken[k]) for k in range(8)]


def lay(klass, row, col, re, im, table, weights, columns, start=0):
    sub = lax.broadcasted_iota(jnp.int32, klass.shape, 0)
    hot = jnp.concatenate([(klass == sub + 8 * k).astype(F32) for k in range(8)], axis=0).astype(BF16)
    values = jnp.dot(table[...], hot, preferred_element_type=F32)
    values = [values[8 * k : 8 * k + 8] for k in range(8)]
    by, first = row & 63, row >> 6
    mine = [
        jnp.where(jnp.where(sub + 8 * k < by, first + 1, first) == 0, x, 0.0)
        for k, x in enumerate(turned(values, by, sub))
    ]
    weights[0:64] = jnp.concatenate([x * re for x in mine], axis=0).astype(BF16)
    weights[64:128] = jnp.concatenate([x * im for x in mine], axis=0).astype(BF16)
    by, first = col & 63, col >> 6
    window = jnp.concatenate(turned(values, by, sub), axis=0).astype(BF16)
    block = jnp.concatenate(
        [jnp.where(sub + 8 * k < by, first + 1, first).astype(F32) for k in range(8)], axis=0).astype(BF16)
    for b in range(columns.shape[0] // 64):
        columns[64 * b : 64 * b + 64] = jnp.where(block == jnp.asarray(start + b, BF16), window, jnp.asarray(0, BF16))


def add(total, weights, columns, start=0):
    stop = 64 * start + columns.shape[0]
    total[:, 64 * start : stop] += lax.dot_general(
        weights[...], columns[...], (((1,), (1,)), ((), ())), preferred_element_type=F32)


def list_left(got, edge, real, whole, number):
    c = lax.axis_index("chan")
    nc, per = got.shape[0], got.shape[1]
    main = nc * per
    count = main + nc * 8
    left = 4 * real.shape[1]
    quarter = left // 4

    lanes = lax.broadcasted_iota(jnp.int32, (1, 256), 1) // LOW
    both = jnp.concatenate([got[...].reshape(main, 256), edge[...].reshape(nc * 8, 256)], axis=0)
    index = lax.broadcasted_iota(jnp.int32, (count, 256), 0)
    shift = jnp.where(index < main, BUCKET * ((index % per) // GROUPS_IN - 1), jnp.where(c == 0, -BUCKET, 2 * BUCKET))
    both = both + jnp.where(lanes == 3, shift - 1, 0).astype(F32)
    used = jnp.max(both[:, 128:256].T[2 * LOW : 3 * LOW], axis=0, keepdims=True)
    at = lax.broadcasted_iota(jnp.int32, (1, count), 1) % GROUPS_IN
    used = jnp.where((at == EARLY[0]) | (at == EARLY[1]), 0.0, used)
    before = (
        lax.broadcasted_iota(jnp.int32, (count, count), 0) < lax.broadcasted_iota(jnp.int32, (count, count), 1)
    ).astype(F32).astype(BF16)
    rank = jnp.dot(jnp.broadcast_to(used, (8, count)).astype(BF16), before, preferred_element_type=F32)[0:1]
    rank = jnp.where(used > 0.5, rank, -1.0)
    place = lax.broadcasted_iota(jnp.int32, (left, count), 0)
    place = (4 * (place % quarter) + place // quarter).astype(F32)
    pick = jnp.where(place == rank, 1.0, 0.0).astype(BF16)
    high = both.astype(BF16)
    low = (both - high.astype(F32)).astype(BF16)
    rows = jnp.dot(pick, high, preferred_element_type=F32) + jnp.dot(pick, low, preferred_element_type=F32)
    spot = lax.broadcasted_iota(jnp.int32, (quarter, 128), 1) // LOW

    def field(f):
        part, offset = divmod(f, 4)
        result = None
        for s in range(4):
            x = rows[s * quarter : (s + 1) * quarter, 128 * part : 128 * part + 128]
            if (s - offset) % 4:
                x = pltpu.roll(x, ((s - offset) % 4) * LOW, 1)
            result = x if result is None else jnp.where(spot == s, x, result)
        return result

    real[0], real[1] = field(0), field(1)
    whole[0], whole[1] = field(2).astype(jnp.int32) - M, field(3).astype(jnp.int32) - M
    whole[2] = (field(4) * float(PLANES) + field(5)).astype(jnp.int32)
    number[...] = jnp.broadcast_to(jnp.sum(used, axis=1, keepdims=True), number.shape)


def exchange(vis, cell, sup, wpl, cnt, table, total, real, whole, number, flag, got, edge, vis_v, cell_v, sup_v, wpl_v, cnt_v, packed, tile_flags, chan_flags,
             weights, columns,
             load_sem, send_sem, recv_sem, edge_send, edge_recv, tf_send, tf_recv, cf_send, cf_recv):
    t, c = lax.axis_index("tile"), lax.axis_index("chan")
    nt, nc = lax.axis_size("tile"), lax.axis_size("chan")
    slots = vis_v.shape[-1]
    loads = [
        pltpu.make_async_copy(vis.at[0, 0], vis_v, load_sem.at[0]),
        pltpu.make_async_copy(cell.at[0, 0], cell_v, load_sem.at[1]),
        pltpu.make_async_copy(sup.at[0], sup_v, load_sem.at[2]),
        pltpu.make_async_copy(wpl.at[0], wpl_v, load_sem.at[3]),
        pltpu.make_async_copy(cnt, cnt_v, load_sem.at[4]),
    ]
    for load in loads:
        load.start()
    edge[...] = jnp.zeros_like(edge)

    bar = pltpu.get_barrier_semaphore()
    for i in range(1, nc):
        pl.semaphore_signal(bar, inc=1, device_id=(t, lax.rem(c + i, nc)), device_id_type=MESH)
    for i in range(1, nt):
        pl.semaphore_signal(bar, inc=1, device_id=(lax.rem(t + i, nt), c), device_id_type=MESH)
    from_low = (c == 0) & (t > 0)
    from_high = (c == nc - 1) & (t < nt - 1)

    @pl.when(from_low)
    def _():
        for g in range(nc):
            pl.semaphore_signal(bar, inc=1, device_id=(t - 1, g), device_id_type=MESH)

    @pl.when(from_high)
    def _():
        for g in range(nc):
            pl.semaphore_signal(bar, inc=1, device_id=(t + 1, g), device_id_type=MESH)

    for load in loads:
        load.wait()

    live = lax.broadcasted_iota(jnp.int32, (1, slots), 1) < cnt_v[...]
    row = cell_v[0:1]
    buckets = G // BUCKET
    bucket = row // BUCKET
    right = cell_v[1:2] >= G // 2
    side = jnp.where(live, bucket + jnp.where(right, buckets, 0), -1)
    hot = (lax.broadcasted_iota(jnp.int32, (2 * buckets, slots), 0) == side).astype(F32)
    step = 256
    before = (
        lax.broadcasted_iota(jnp.int32, (step, step), 0) < lax.broadcasted_iota(jnp.int32, (step, step), 1)
    ).astype(F32).astype(BF16)
    parts = []
    carry = jnp.zeros((2 * buckets, 1), F32)
    for s in range(0, slots, step):
        piece = hot[:, s : s + step]
        ahead = jnp.dot(piece.astype(BF16), before, preferred_element_type=F32) + carry
        parts.append(jnp.sum(piece * ahead, axis=0, keepdims=True))
        carry = carry + jnp.sum(piece, axis=1, keepdims=True)
    rank = jnp.concatenate(parts, axis=1).astype(jnp.int32)
    full = jnp.max(carry[:buckets] + carry[buckets:], axis=0, keepdims=True) > CAP
    full = full | (jnp.max(carry, axis=0, keepdims=True) > CAP - LOW)
    over = full.astype(F32)
    tile_flags[t] = jnp.broadcast_to(over, (1, 128))

    spot = jnp.where(right, CAP - 1 - rank, rank)
    group = jnp.where(live, (bucket + 1) * GROUPS_IN + (spot >> (LOW.bit_length() - 1)), -1)
    place = spot & (LOW - 1)
    groups = packed.shape[0]
    to_group = (lax.broadcasted_iota(jnp.int32, (groups, slots), 0) == group).astype(F32).astype(BF16)
    at_place = lax.broadcasted_iota(jnp.int32, (LOW, slots), 0) == place

    def halves(x):
        high = x.astype(BF16).astype(F32)
        return high, x - high

    re_hi, re_lo = halves(vis_v[0:1])
    im_hi, im_lo = halves(vis_v[1:2])
    col = cell_v[1:2]
    pieces = [re_hi, im_hi, col >> 2, sup_v[...] * PLANES + wpl_v[...], re_lo, im_lo,
              (col & 3) * 64 + (row & (BUCKET - 1)) + 1, jnp.zeros((1, slots), F32)]
    spread = jnp.concatenate([jnp.where(at_place, x.astype(F32), 0.0).astype(BF16) for x in pieces], axis=0)
    moved = lax.dot_general(to_group, spread, (((1,), (1,)), ((), ())), preferred_element_type=F32)
    first, second = moved[:, 0:128], moved[:, 128:256]
    whole_1, whole_2 = first.astype(jnp.int32), second.astype(jnp.int32)
    lane = lax.broadcasted_iota(jnp.int32, first.shape, 1) // LOW
    packed[:, 0:128] = jnp.where(
        lane < 2, first + second,
        jnp.where(lane == 2, whole_1 * 4 + (whole_2 >> 6), pltpu.roll(whole_2, LOW, 1) & 63).astype(F32))
    klass = pltpu.roll(whole_1, LOW, 1)
    packed[:, 128:256] = jnp.where(
        lane == 0, klass >> 4,
        jnp.where(lane == 1, pltpu.roll(klass, LOW, 1) & (PLANES - 1),
                  jnp.where((lane == 2) & ((whole_2 & 63) > 0), 1, 0))).astype(F32)

    below, above = (t > 0).astype(jnp.int32), (t < nt - 1).astype(jnp.int32)
    pl.semaphore_wait(bar, nc - 1 + nt - 1 + below + above)

    def tile_flag(i, slot):
        return pltpu.make_async_remote_copy(
            src_ref=tile_flags.at[t], dst_ref=tile_flags.at[slot], send_sem=tf_send, recv_sem=tf_recv,
            device_id=(lax.rem(t + i, nt), c), device_id_type=MESH)

    for i in range(1, nt):
        tile_flag(i, t).start()

    width = 4 * GROUPS_IN

    def payload(i, slot):
        peer = lax.rem(c + i, nc)
        return pltpu.make_async_remote_copy(
            src_ref=packed.at[pl.ds(pl.multiple_of(8 * peer, 8), width)], dst_ref=got.at[slot], send_sem=send_sem,
            recv_sem=recv_sem.at[slot], device_id=(t, peer), device_id_type=MESH)

    def edge_up():
        return pltpu.make_async_remote_copy(
            src_ref=packed.at[pl.ds(buckets * GROUPS_IN, GROUPS_IN)], dst_ref=edge.at[c, 0:GROUPS_IN], send_sem=edge_send.at[0],
            recv_sem=edge_recv.at[c], device_id=(t + 1, 0), device_id_type=MESH)

    def edge_down():
        return pltpu.make_async_remote_copy(
            src_ref=packed.at[pl.ds(GROUPS_IN, GROUPS_IN)], dst_ref=edge.at[c, 0:GROUPS_IN], send_sem=edge_send.at[1],
            recv_sem=edge_recv.at[c], device_id=(t - 1, nc - 1), device_id_type=MESH)

    @pl.when(t < nt - 1)
    def _():
        edge_up().start()

    @pl.when(t > 0)
    def _():
        edge_down().start()

    for i in range(1, nc):
        payload(i, c).start()

    got[c] = packed[pl.ds(pl.multiple_of(8 * c, 8), width), :]

    def all_of(ref, count, sent, landed):
        return pltpu.make_async_remote_copy(
            src_ref=ref.at[0:count], dst_ref=ref.at[0:count], send_sem=sent, recv_sem=landed,
            device_id=(t, lax.rem(c + 1, nc)), device_id_type=MESH)

    table[...] = class_table()
    total[...] = jnp.zeros_like(total)

    spot = lax.broadcasted_iota(jnp.int32, (8, 128), 1) // LOW

    def fields(first, second, lift, picks):
        row_lanes = lax.broadcasted_iota(jnp.int32, first.shape, 1) // LOW == 3
        cells = first.astype(jnp.int32) - M
        cells = jnp.where(row_lanes, cells + lift, cells)
        klass = (second * float(PLANES) + pltpu.roll(second, 3 * LOW, 1)).astype(jnp.int32)

        def lines(x, offset):
            shifted = [pltpu.roll(x, ((b - offset) % 4) * LOW, 1) if (b - offset) % 4 else x for b in range(4)]
            made = []
            for pick in picks:
                parts = [jnp.broadcast_to(shifted[b][r : r + 1], (8, 128)) for b, r in enumerate(pick)]
                line = parts[0]
                for b in range(1, 4):
                    line = jnp.where(spot == b, parts[b], line)
                made.append(line)
            return made

        return lines(klass, 0), lines(cells, 3), lines(cells, 2), lines(first, 0), lines(first, 1)

    halves_at = (0, G // 64 - SPAN)
    lift = BUCKET * (lax.broadcasted_iota(jnp.int32, (width, 128), 0) // GROUPS_IN - 1) - 1

    here = 2 * (c // 2)

    def chip(k):
        q = k % 4
        dz = q + jnp.where(q == 2, 1, 0) - jnp.where(q == 3, 1, 0)
        z, y = (here // 2) % 4, here // 8
        return (((y + k // 4) % 2) * 4 + (z + dz) % 4) * 2

    def prepare(source, slot):
        made = [
            fields(got[x, :, 0:128], got[x, :, 128:256], lift, [[GROUPS_IN * b + g for b in range(4)] for g in EARLY])
            for x in (source, source + 1)
        ]
        for h in range(2):
            lay(*[jnp.concatenate([x[h], y[h]], axis=1) for x, y in zip(*made)], table, weights.at[slot, h],
                columns.at[slot, h], halves_at[h])

    def add_both(slot):
        for h in range(2):
            add(total, weights.at[slot, h], columns.at[slot, h], halves_at[h])

    def arrive(source):
        pltpu.make_async_remote_copy(
            src_ref=packed.at[pl.ds(0, width)], dst_ref=got.at[source], send_sem=send_sem,
            recv_sem=recv_sem.at[source], device_id=(t, source), device_id_type=MESH).wait_recv()

    arrive(here + (c + 1) % 2)
    prepare(here, 0)

    all_of(tile_flags, nt - 1, tf_send, tf_recv).wait_recv()
    chan_flags[c] = jnp.max(tile_flags[...], axis=0)

    for i in range(1, nc):
        pltpu.make_async_remote_copy(
            src_ref=chan_flags.at[c], dst_ref=chan_flags.at[c], send_sem=cf_send, recv_sem=cf_recv,
            device_id=(t, lax.rem(c + i, nc)), device_id_type=MESH).start()

    def two_chips(j, carry):
        for odd in (1, 0):
            source = chip(2 * j + 2 - odd)
            arrive(source)
            arrive(source + 1)
            prepare(source, odd)
            add_both(1 - odd)
        return carry

    chips = nc // 2
    lax.fori_loop(0, chips // 2 - 1, two_chips, 0)
    add_both(0)

    @pl.when(from_low | from_high)
    def _():
        for g in range(nc):
            pltpu.make_async_remote_copy(
                src_ref=packed.at[pl.ds(0, GROUPS_IN)], dst_ref=edge.at[g, 0:GROUPS_IN], send_sem=edge_send.at[0],
                recv_sem=edge_recv.at[g], device_id=(t, g), device_id_type=MESH).wait_recv()
        rows = edge[...].reshape(nc * 8, 256)
        lines = nc // 4
        picks = [[8 * (4 * n + b) + g for b in range(4)] for g in EARLY for n in range(lines)]
        made = fields(rows[:, 0:128], rows[:, 128:256], jnp.where(from_low, -BUCKET, 2 * BUCKET) - 1, picks)
        for h in range(2):
            for n in range(0, lines, 2):
                lay(*[jnp.concatenate(x[h * lines + n : h * lines + n + 2], axis=1) for x in made], table,
                    weights.at[n // 2, h], columns.at[n // 2, h], halves_at[h])
        for n in range(lines // 2):
            add_both(n)

    all_of(tile_flags, nt - 1, tf_send, tf_recv).wait_send()
    all_of(chan_flags, nc - 1, cf_send, cf_recv).wait_send()
    all_of(got, nc - 1, send_sem, recv_sem.at[0]).wait_send()

    @pl.when(t < nt - 1)
    def _():
        edge_up().wait_send()

    @pl.when(t > 0)
    def _():
        edge_down().wait_send()

    source = chip(chips - 1)
    arrive(source)
    arrive(source + 1)
    prepare(source, 1)
    list_left(got, edge, real, whole, number)
    add_both(1)

    all_of(chan_flags, nc - 1, cf_send, cf_recv).wait_recv()
    flag[0, 0] = (jnp.max(jnp.max(chan_flags[...], axis=0)) > 0.5).astype(jnp.int32)


def owned_rows(real, whole, number, table, begun, out, total, weights, columns):
    size = weights.shape[-1]
    lines = size // 128
    chunks = (jnp.max(number[...]).astype(jnp.int32) + 4 * lines - 1) // (4 * lines)
    total[...] = begun[...]

    def body(i, carry):
        def line(ref, f):
            return jnp.concatenate(
                [jnp.broadcast_to(ref[f, pl.ds(lines * i + h, 1), :], (8, 128)) for h in range(lines)], axis=1)

        lay(line(whole, 2), line(whole, 1), line(whole, 0), line(real, 0), line(real, 1), table, weights, columns)
        add(total, weights, columns)
        return carry

    lax.fori_loop(0, chunks, body, 0)
    out[:, 0, :] = total[0:64]
    out[:, 1, :] = total[64:128]


def per_device(visibilities, cell_offsets, support_index, w_plane, live_counts):
    nt, nc = lax.axis_size("tile"), lax.axis_size("chan")
    slots = visibilities.shape[-1]
    groups = (G // BUCKET + 2) * GROUPS_IN
    vmem = pl.BlockSpec(memory_space=pltpu.VMEM)
    left_lines = nc * 5 * (GROUPS_IN - len(EARLY)) // 4
    table, begun, real, whole, number, flag = pl.pallas_call(
        exchange,
        out_shape=(
            jax.ShapeDtypeStruct((2 * M, 4 * PLANES), BF16),
            jax.ShapeDtypeStruct((2 * G // nc, G), F32),
            jax.ShapeDtypeStruct((2, left_lines, 128), F32),
            jax.ShapeDtypeStruct((3, left_lines, 128), jnp.int32),
            jax.ShapeDtypeStruct((8, 128), F32),
            jax.ShapeDtypeStruct((1, 1), jnp.int32),
        ),
        in_specs=[pl.BlockSpec(memory_space=pltpu.MemorySpace.HBM)] * 5,
        out_specs=(vmem, vmem, vmem, vmem, vmem, pl.BlockSpec(memory_space=pltpu.SMEM)),
        scratch_shapes=[
            pltpu.VMEM((nc, 4 * GROUPS_IN, FIELDS * LOW), F32),
            pltpu.VMEM((nc, 8, FIELDS * LOW), F32),
            pltpu.VMEM((2, slots), F32),
            pltpu.VMEM((2, slots), jnp.int32),
            pltpu.VMEM((1, slots), jnp.int32),
            pltpu.VMEM((1, slots), jnp.int32),
            pltpu.VMEM((1, 1), jnp.int32),
            pltpu.VMEM((groups, FIELDS * LOW), F32),
            pltpu.VMEM((nt, 1, 128), F32),
            pltpu.VMEM((nc, 1, 128), F32),
            pltpu.VMEM((2, 2, 2 * G // nc, 256), BF16),
            pltpu.VMEM((2, 2, 64 * SPAN, 256), BF16),
            pltpu.SemaphoreType.DMA((5,)),
            pltpu.SemaphoreType.DMA,
            pltpu.SemaphoreType.DMA((nc,)),
            pltpu.SemaphoreType.DMA((2,)),
            pltpu.SemaphoreType.DMA((nc,)),
            pltpu.SemaphoreType.DMA,
            pltpu.SemaphoreType.DMA,
            pltpu.SemaphoreType.DMA,
            pltpu.SemaphoreType.DMA,
        ],
        compiler_params=pltpu.CompilerParams(collective_id=0, has_side_effects=True, vmem_limit_bytes=62 << 20),
    )(visibilities, cell_offsets, support_index, w_plane, live_counts)


    def usual(*_):
        return pl.pallas_call(
            owned_rows,
            out_shape=jax.ShapeDtypeStruct((G // nc, 2, G), F32),
            in_specs=[vmem] * 5,
            out_specs=vmem,
            scratch_shapes=[
                pltpu.VMEM((2 * G // nc, G), F32),
                pltpu.VMEM((2 * G // nc, 512), BF16),
                pltpu.VMEM((G, 512), BF16),
            ],
            compiler_params=pltpu.CompilerParams(vmem_limit_bytes=40 << 20),
        )(real, whole, number, table, begun)

    return lax.switch(
        flag[0, 0], (usual, any_cells), visibilities, cell_offsets, support_index, w_plane, live_counts
    )


def solution(mesh):
    in_specs = (
        P("tile", "chan", None, None),
        P("tile", "chan", None, None),
        P("tile", "chan", None),
        P("tile", "chan", None),
        P("tile", "chan"),
    )
    out_specs = P(("tile", "chan"), None, None)
    return jax.shard_map(
        per_device, mesh=mesh, in_specs=in_specs, out_specs=out_specs, check_vma=False
    )
```
